32 devices in a mesh: dp: 8 (over y, x, core), tensor: 4 (over z).
Axes of the slice: x: 2, y: 2, z: 4, core: 2. Of those that a mesh axis runs over, the one named last changes fastest.
Arguments:
- patches: bfloat16 [2304, 1024], P(('dp', 'tensor')), may hold values from -6 to 6
- hires: bfloat16 [192, 48, 1536], P(('dp', 'tensor')), may hold values from -6 to 6
- valid_rows: int32 [4], replicated, may hold values from 12 to 24, as said below
- ln1_gain: float32 [1024], replicated, may hold values from 0.25 to 1.75
- ln1_bias: float32 [1024], replicated, may hold values from -1.75 to 1.75
- w_qkv: bfloat16 [3, 1024, 1024], P(None, None, 'tensor'), may hold values from -0.1875 to 0.1875
- qv_bias: float32 [2, 1024], P(None, 'tensor'), may hold values from -1.75 to 1.75
- w_out: bfloat16 [1024, 1024], P('tensor'), may hold values from -2.5 to 2.5
- out_bias: float32 [1024], replicated, may hold values from -1.75 to 1.75
- ln2_gain: float32 [1024], replicated, may hold values from 0.25 to 1.75
- ln2_bias: float32 [1024], replicated, may hold values from -1.75 to 1.75
- w_fc1: bfloat16 [1024, 4096], P(None, 'tensor'), may hold values from -0.1875 to 0.1875
- fc1_bias: float32 [4096], P('tensor'), may hold values from -3 to 3
- w_fc2: bfloat16 [4096, 1024], P('tensor'), may hold values from -0.125 to 0.125
- fc2_bias: float32 [1024], replicated, may hold values from -1.75 to 1.75
- dw_weight: float32 [49, 1536], replicated, may hold values from -0.875 to 0.875
- dw_bias: float32 [1536], replicated, may hold values from -1.75 to 1.75
- lnc_gain: float32 [1536], replicated, may hold values from 0.25 to 1.75
- lnc_bias: float32 [1536], replicated, may hold values from -1.75 to 1.75
- w_pw1: bfloat16 [1536, 6144], P(None, 'tensor'), may hold values from -0.15625 to 0.15625
- pw1_bias: float32 [6144], P('tensor'), may hold values from -3 to 3
- w_pw2: bfloat16 [6144, 1536], P('tensor'), may hold values from -0.109375 to 0.109375
- pw2_bias: float32 [1536], replicated, may hold values from -1.75 to 1.75
- layer_scale: float32 [1536], replicated, may hold values from 0.3 to 1.5
- w_adapt: bfloat16 [1536, 1024], replicated, may hold values from -0.15625 to 0.15625
- adapt_bias: float32 [1024], replicated, may hold values from -1.75 to 1.75
- adapt_gain: float32 [1024], replicated, may hold values from 0.5 to 1.5
- grad_out: bfloat16 [2304, 1024], P(('dp', 'tensor')), may hold values from -12 to 12
Outputs:
- joined_out: bfloat16 [2304, 1024], P(('dp', 'tensor'))
- grad_patches: float32 [2304, 1024], P(('dp', 'tensor'))
- grad_hires: float32 [192, 48, 1536], P(('dp', 'tensor'))
- grad_ln1_gain: float32 [1024], P(('dp', 'tensor'))
- grad_ln1_bias: float32 [1024], P(('dp', 'tensor'))
- grad_w_qkv: float32 [3, 1024, 1024], P(None, 'dp', 'tensor')
- grad_qv_bias: float32 [2, 1024], P(None, ('tensor', 'dp'))
- grad_w_out: float32 [1024, 1024], P('tensor', 'dp')
- grad_out_bias: float32 [1024], P(('dp', 'tensor'))
- grad_ln2_gain: float32 [1024], P(('dp', 'tensor'))
- grad_ln2_bias: float32 [1024], P(('dp', 'tensor'))
- grad_w_fc1: float32 [1024, 4096], P('dp', 'tensor')
- grad_fc1_bias: float32 [4096], P(('tensor', 'dp'))
- grad_w_fc2: float32 [4096, 1024], P('tensor', 'dp')
- grad_fc2_bias: float32 [1024], P(('dp', 'tensor'))
- grad_dw_weight: float32 [49, 1536], P(None, ('dp', 'tensor'))
- grad_dw_bias: float32 [1536], P(('dp', 'tensor'))
- grad_lnc_gain: float32 [1536], P(('dp', 'tensor'))
- grad_lnc_bias: float32 [1536], P(('dp', 'tensor'))
- grad_w_pw1: float32 [1536, 6144], P('dp', 'tensor')
- grad_pw1_bias: float32 [6144], P(('tensor', 'dp'))
- grad_w_pw2: float32 [6144, 1536], P('tensor', 'dp')
- grad_pw2_bias: float32 [1536], P(('dp', 'tensor'))
- grad_layer_scale: float32 [1536], P(('dp', 'tensor'))
- grad_w_adapt: float32 [1536, 1024], P(('dp', 'tensor'))
- grad_adapt_bias: float32 [1024], P(('dp', 'tensor'))
- grad_adapt_gain: float32 [1024], P(('dp', 'tensor'))
The draws below stay inside these ranges and needn't reach their ends.
Inputs may be any that keep to these rules, and one draw needn't show every extreme that they name: Patch rows valid_rows[b] onward of image b are letterbox padding, never attended to as keys; image 0 has all 24 rows.
All inputs are finite; a program needn't handle non-finite values.
Results may differ from the reference program's by a relative error of at most 0.02.
Values may be sent and summed in bfloat16 or wider, within the bound.
A program may use at most 256 MiB of HBM per device.

```python
import math
import jax
import jax.numpy as jnp
from jax import lax

D = 1024
HEADS = 16
HEAD_DIM = 64
FF = 4096
C = 1536
CH_HIDDEN = 6144
SIDE = 24
KERNEL = 7
HSIDE = 48
IMAGES = 4
PATCHES = 2304
HROWS = 192


def draw_valid_rows(key, part):
    values = jax.random.randint(key, (IMAGES,), SIDE // 2, SIDE + 1)
    return jnp.where(jnp.arange(IMAGES) == 0, SIDE, values).astype(jnp.int32)


def with_spikes(array, key, source, target, parts, factor):
    owner, partner = [(jnp.arange(array.shape[position]) // (array.shape[position] // parts)).reshape([-1 if axis == position else 1 for axis in range(array.ndim)]) for position in (source, target)]
    chosen = jax.random.permutation(key, parts)[partner]
    strong = (owner == chosen) | (owner == (partner + parts // 2) % parts)
    return jnp.where(strong, factor * array, array)


def shard_levels(own_key, dims, cuts, least, largest):
    loudness = 1.0
    for position, shards_of in cuts:
        steps = jax.random.uniform(jax.random.fold_in(jax.random.fold_in(own_key, 6), position), (shards_of,), jnp.float32, least / len(cuts), largest / len(cuts))
        loudness = loudness * jnp.repeat(jnp.exp(steps), dims[position] // shards_of).reshape((-1,) + (1,) * (len(dims) - 1 - position))
    return loudness


def bell_draw(key, shape, deviation, most, split=(), held_as=jnp.bfloat16):
    drawn = deviation * jax.random.normal(key, shape, jnp.float32)
    if split:
        drawn = drawn * shard_levels(key, shape, split, -0.22, 0.18)
    return jnp.clip(drawn, -most, most).astype(held_as)


def bell_draw_with(key, dims, deviation, limit, pieces, heavy, kind=jnp.bfloat16):
    drawn = deviation * jax.random.normal(key, dims, jnp.float32)
    if pieces:
        drawn = drawn * shard_levels(key, dims, pieces, -0.22, 0.18)
    return jnp.clip(with_spikes(drawn, jax.random.fold_in(key, 3), *heavy), -limit, limit).astype(kind)


def setup_inputs(seed: int = 0) -> dict:
    key_list = jax.random.split(jax.random.key(seed), 29)
    return {
        "patches": bell_draw(key_list[0], (PATCHES, D), 1.0, 6.0, ((0, 32),)),
        "hires": bell_draw(key_list[1], (HROWS, HSIDE, C), 1.0, 6.0, ((0, 32),)),
        "valid_rows": draw_valid_rows(jax.random.fold_in(key_list[28], 71), 0),
        "ln1_gain": jnp.clip(1.0 + 0.15 * jax.random.normal(key_list[3], (D,), jnp.float32), 0.25, 1.75),
        "ln1_bias": bell_draw(key_list[4], (D,), 0.3, 1.75, (), jnp.float32),
        "w_qkv": bell_draw(key_list[5], (3, D, D), D ** -0.5, 0.1875, ((2, 4),)),
        "qv_bias": bell_draw(key_list[6], (2, D), 0.3, 1.75, ((1, 4),), jnp.float32),
        "w_out": bell_draw(key_list[7], (D, D), (max(D // 200, 1)) ** -0.5, 2.5, ((0, 4),)),
        "out_bias": bell_draw(key_list[8], (D,), 0.3, 1.75, (), jnp.float32),
        "ln2_gain": jnp.clip(1.0 + 0.15 * jax.random.normal(key_list[9], (D,), jnp.float32), 0.25, 1.75),
        "ln2_bias": bell_draw(key_list[10], (D,), 0.3, 1.75, (), jnp.float32),
        "w_fc1": bell_draw(key_list[11], (D, FF), D ** -0.5, 0.1875, ((1, 4),)),
        "fc1_bias": bell_draw(key_list[12], (FF,), 0.5, 3.0, ((0, 4),), jnp.float32),
        "w_fc2": bell_draw(key_list[13], (FF, D), (FF // 2) ** -0.5, 0.125, ((0, 4),)),
        "fc2_bias": bell_draw(key_list[14], (D,), 0.3, 1.75, (), jnp.float32),
        "dw_weight": bell_draw(key_list[15], (KERNEL * KERNEL, C), (KERNEL * KERNEL) ** -0.5, 0.875, (), jnp.float32),
        "dw_bias": bell_draw(key_list[16], (C,), 0.3, 1.75, (), jnp.float32),
        "lnc_gain": jnp.clip(1.0 + 0.15 * jax.random.normal(key_list[17], (C,), jnp.float32), 0.25, 1.75),
        "lnc_bias": bell_draw(key_list[18], (C,), 0.3, 1.75, (), jnp.float32),
        "w_pw1": bell_draw(key_list[19], (C, CH_HIDDEN), C ** -0.5, 0.15625, ((1, 4),)),
        "pw1_bias": bell_draw(key_list[20], (CH_HIDDEN,), 0.5, 3.0, ((0, 4),), jnp.float32),
        "w_pw2": bell_draw(key_list[21], (CH_HIDDEN, C), (CH_HIDDEN // 2) ** -0.5, 0.109375, ((0, 4),)),
        "pw2_bias": bell_draw(key_list[22], (C,), 0.3, 1.75, (), jnp.float32),
        "layer_scale": jnp.clip(jnp.exp(jax.random.uniform(key_list[23], (C,), jnp.float32, math.log(0.3), math.log(1.5))), 0.3, 1.5),
        "w_adapt": bell_draw(key_list[24], (C, D), C ** -0.5, 0.15625),
        "adapt_bias": bell_draw(key_list[25], (D,), 0.3, 1.75, (), jnp.float32),
        "adapt_gain": jnp.clip(jax.random.uniform(key_list[26], (D,), jnp.float32, 0.5, 1.5), 0.5, 1.5),
        "grad_out": bell_draw_with(key_list[27], (PATCHES, D), 1.0, 12.0, ((0, 32),), (0, 1, 32, 2.75)),
    }


highest = lax.Precision.HIGHEST
vit_eps = 1e-05
map_eps = 1e-06
masked_score = -1e+30

@jax.custom_vjp
def low(v):
    return lax.optimization_barrier(v.astype(jnp.bfloat16)).astype(jnp.float32)

@jax.custom_vjp
def low_back(v):
    return v

def low_keep(v):
    return (low(v), None)

def low_pass(kept, grad):
    return (grad,)

def back_keep(v):
    return (v, None)

def back_low(kept, grad):
    return (low(grad),)
low.defvjp(low_keep, low_pass)
low_back.defvjp(back_keep, back_low)

def matmul(left_side, right_side):
    return jnp.dot(left_side, right_side, precision=highest, preferred_element_type=jnp.float32)

def layer_norm(values, gain_vec, bias_vec, epsilon):
    centered = values - lax.optimization_barrier(jnp.mean(values, axis=-1, keepdims=True))
    variance = lax.optimization_barrier(jnp.mean(centered * centered, axis=-1, keepdims=True))
    return centered * lax.rsqrt(variance + epsilon) * gain_vec + bias_vec

def gelu_exact(values):
    return jax.nn.gelu(values, approximate=False)

def depthwise(padded, tap_table, rows_here, cols_here):
    running = jnp.zeros((rows_here, cols_here, padded.shape[2]), jnp.float32)
    for row_tap in range(KERNEL):
        for col_tap in range(KERNEL):
            window = padded[row_tap:row_tap + rows_here, col_tap:col_tap + cols_here]
            running = running + window * tap_table[row_tap * KERNEL + col_tap]
    return running

def image_forward(params, patch_img, map_img, image_valid):
    ln1_gain, ln1_bias, w_qkv, qv_bias, w_out, out_bias, ln2_gain, ln2_bias, w_fc1, fc1_bias, w_fc2, fc2_bias, dw_weight, dw_bias, lnc_gain, lnc_bias, w_pw1, pw1_bias, w_pw2, pw2_bias, layer_scale, w_adapt, adapt_bias, adapt_gain = params
    rim_width = KERNEL // 2
    padded_map = jnp.pad(map_img, ((rim_width, rim_width), (rim_width, rim_width), (0, 0)))
    conv_map = depthwise(padded_map, dw_weight, HSIDE, HSIDE) + dw_bias
    normed_map = low(layer_norm(conv_map.reshape(HSIDE * HSIDE, C), lnc_gain, lnc_bias, map_eps))
    map_pre = low_back(matmul(normed_map, w_pw1) + pw1_bias)
    map_hidden = low(gelu_exact(map_pre))
    map_branch = low_back(matmul(map_hidden, w_pw2) + pw2_bias)
    map_out = map_img.reshape(HSIDE * HSIDE, C) + layer_scale * map_branch
    pooled = low(lax.optimization_barrier(jnp.mean(map_out.reshape(SIDE, 2, SIDE, 2, C), axis=(1, 3))).reshape(SIDE * SIDE, C))
    adapted = low_back(matmul(pooled, w_adapt) + adapt_bias)
    attn_in = low(layer_norm(patch_img, ln1_gain, ln1_bias, vit_eps))
    queries = low(low_back(matmul(attn_in, w_qkv[0]) + qv_bias[0]))
    keys_all = low(low_back(matmul(attn_in, w_qkv[1])))
    values_all = low(low_back(matmul(attn_in, w_qkv[2]) + qv_bias[1]))
    head_shape = (SIDE * SIDE, HEADS, HEAD_DIM)
    raw_scores = jnp.einsum('qhd,khd->hqk', queries.reshape(head_shape), keys_all.reshape(head_shape), precision=highest) * HEAD_DIM ** (-0.5)
    key_live = jnp.arange(SIDE * SIDE) // SIDE < image_valid
    scores = jnp.where(key_live[None, None, :], low_back(raw_scores), masked_score)
    probabilities = low(jax.nn.softmax(scores, axis=-1))
    attended = jnp.einsum('hqk,khd->qhd', probabilities, values_all.reshape(head_shape), precision=highest).reshape(SIDE * SIDE, D)
    attended = low(low_back(attended))
    projected = low_back(matmul(attended, w_out) + out_bias)
    middle = patch_img + projected
    mlp_in = low(layer_norm(middle, ln2_gain, ln2_bias, vit_eps))
    mlp_pre = low_back(matmul(mlp_in, w_fc1) + fc1_bias)
    mlp_hidden = low(gelu_exact(mlp_pre))
    mlp_branch = low_back(matmul(mlp_hidden, w_fc2) + fc2_bias)
    return middle + mlp_branch + adapt_gain * adapted

def reference(patches, hires, valid_rows, ln1_gain, ln1_bias, w_qkv, qv_bias, w_out, out_bias, ln2_gain, ln2_bias, w_fc1, fc1_bias, w_fc2, fc2_bias, dw_weight, dw_bias, lnc_gain, lnc_bias, w_pw1, pw1_bias, w_pw2, pw2_bias, layer_scale, w_adapt, adapt_bias, adapt_gain, grad_out):
    params = tuple((item.astype(jnp.float32) for item in (ln1_gain, ln1_bias, w_qkv, qv_bias, w_out, out_bias, ln2_gain, ln2_bias, w_fc1, fc1_bias, w_fc2, fc2_bias, dw_weight, dw_bias, lnc_gain, lnc_bias, w_pw1, pw1_bias, w_pw2, pw2_bias, layer_scale, w_adapt, adapt_bias, adapt_gain)))
    image_inputs = patches.astype(jnp.float32).reshape(IMAGES, SIDE * SIDE, D)
    image_maps = hires.astype(jnp.float32).reshape(IMAGES, HSIDE, HSIDE, C)

    def forward(weights, inputs, map_stack):

        def one_image(items):
            return image_forward(weights, items[0], items[1], items[2])
        return lax.map(jax.checkpoint(one_image), (inputs, map_stack, valid_rows))
    outputs, pull_back = jax.vjp(forward, params, image_inputs, image_maps)
    weight_grads, input_grads, map_grads = pull_back(grad_out.astype(jnp.float32).reshape(IMAGES, SIDE * SIDE, D))
    g_ln1_gain, g_ln1_bias, g_w_qkv, g_qv_bias, g_w_out, g_out_bias, g_ln2_gain, g_ln2_bias, g_w_fc1, g_fc1_bias, g_w_fc2, g_fc2_bias, g_dw_weight, g_dw_bias, g_lnc_gain, g_lnc_bias, g_w_pw1, g_pw1_bias, g_w_pw2, g_pw2_bias, g_layer_scale, g_w_adapt, g_adapt_bias, g_adapt_gain = weight_grads
    return (outputs.reshape(PATCHES, D).astype(jnp.bfloat16), input_grads.reshape(PATCHES, D), map_grads.reshape(HROWS, HSIDE, C), g_ln1_gain, g_ln1_bias, g_w_qkv, g_qv_bias, g_w_out, g_out_bias, g_ln2_gain, g_ln2_bias, g_w_fc1, g_fc1_bias, g_w_fc2, g_fc2_bias, g_dw_weight, g_dw_bias, g_lnc_gain, g_lnc_bias, g_w_pw1, g_pw1_bias, g_w_pw2, g_pw2_bias, g_layer_scale, g_w_adapt, g_adapt_bias, g_adapt_gain)
```

```python
from functools import partial

import jax
import numpy as np
import jax.numpy as jnp
from jax import lax
from jax.experimental import pallas as pl
from jax.experimental.pallas import tpu as pltpu
from jax.sharding import PartitionSpec as P

HEAD_DIM = 64
SIDE = 24
KERNEL = 7
IMG_SPAN = 2


vit_eps = 1e-05
map_eps = 1e-06
masked_score = -1e30
ROOT_HALF = 0.7071067811865476
NORMAL_PEAK = 0.3989422804014327


def padded_2(value, sides, width):
    for axis, dim in sides:
        count, length = (lax.axis_size(axis), value.shape[dim])
        up = [(i, (i + 1) % count) for i in range(count)]
        down = [(j, i) for i, j in up]
        last = lax.slice_in_dim(value, length - width, length, axis=dim)
        first = lax.slice_in_dim(value, 0, width, axis=dim)
        before = lax.ppermute(last, axis, up)
        after = lax.ppermute(first, axis, down)
        value = jnp.concatenate([before, value, after], axis=dim)
    return value


def partner_2(block, axis, apart):
    count = lax.axis_size(axis)
    route = []
    for low in range(count):
        high = low | 1 << apart
        if high != low and high < count:
            route += [(low, high), (high, low)]
    return lax.ppermute(block, axis, route)


def layer_norm(values, gain_vec, bias_vec, epsilon):
    centered = values - jnp.mean(values, axis=-1, keepdims=True)
    variance = jnp.mean(centered * centered, axis=-1, keepdims=True)
    return centered * lax.rsqrt(variance + epsilon) * gain_vec + bias_vec


def gelu_exact(values):
    return jax.nn.gelu(values, approximate=False)


def contract_rows(left_side, right_side):
    return lax.dot_general(
        left_side, right_side, (((0,), (0,)), ((), ())), preferred_element_type=jnp.float32
    )


def contract_cols(left_side, right_side):
    return lax.dot_general(
        left_side, right_side, (((1,), (1,)), ((), ())), preferred_element_type=jnp.float32
    )


MESH_ID = pl.DeviceIdType.MESH
VMEM_SPEC = pl.BlockSpec(memory_space=pltpu.VMEM)
LANES = 128
SUB = 8
VMEM_BYTES = 60 * 1024 * 1024


def kernel_params(collective_id=None):
    if collective_id is None:
        return pltpu.CompilerParams(vmem_limit_bytes=VMEM_BYTES)
    return pltpu.CompilerParams(
        vmem_limit_bytes=VMEM_BYTES, collective_id=collective_id, has_side_effects=True
    )


def halo_route():
    count = lax.axis_size("tensor")
    d, t = lax.axis_index("dp"), lax.axis_index("tensor")
    odd = lax.rem(d, IMG_SPAN)
    up = (d + (t + 1) // count, lax.rem(t + 1, count))
    down = (d - 1 + (t + count - 1) // count, lax.rem(t + count - 1, count))
    up_here = (t + 1) // count + odd < 2
    down_here = t + odd > 0
    return up, down, up_here, down_here


def halo_barrier(route):
    up, down, up_here, down_here = route
    barrier = pltpu.get_barrier_semaphore()

    @pl.when(up_here)
    def _():
        pl.semaphore_signal(barrier, inc=1, device_id=up, device_id_type=MESH_ID)

    @pl.when(down_here)
    def _():
        pl.semaphore_signal(barrier, inc=1, device_id=down, device_id_type=MESH_ID)

    count = lax.axis_size("tensor")
    d, t = lax.axis_index("dp"), lax.axis_index("tensor")
    odd = lax.rem(d, IMG_SPAN)
    ups = 1 - ((t + 1) // count + odd) // 2
    downs = (t + odd + count) // (count + 1)
    pl.semaphore_wait(barrier, ups + downs)


def halo_copies(route, first_rows, last_rows, low_ref, high_ref, send_sem, recv_sem):
    up, down, up_here, down_here = route
    to_up = pltpu.make_async_remote_copy(
        last_rows, low_ref, send_sem.at[0], recv_sem.at[0], device_id=up, device_id_type=MESH_ID
    )
    to_down = pltpu.make_async_remote_copy(
        first_rows, high_ref, send_sem.at[1], recv_sem.at[1], device_id=down, device_id_type=MESH_ID
    )
    return to_up, to_down


def halo_start(route, copies):
    @pl.when(route[2])
    def _():
        copies[0].start()

    @pl.when(route[3])
    def _():
        copies[1].start()


def halo_finish(route, copies):
    @pl.when(route[2])
    def _():
        copies[0].wait_send()
        copies[1].wait_recv()

    @pl.when(route[3])
    def _():
        copies[1].wait_send()
        copies[0].wait_recv()


def halo_store(route, extended, low_ref, high_ref, rows, cols, rim):
    @pl.when(route[3])
    def _():
        extended[0:rim, SUB : SUB + cols, :] = low_ref[...].astype(jnp.float32)

    @pl.when(route[2])
    def _():
        extended[rim + rows : 2 * rim + rows, SUB : SUB + cols, :] = high_ref[...].astype(
            jnp.float32
        )


def conv_rows(extended, taps_ref, rows, cols, channels, flipped, emit):
    span = KERNEL * KERNEL - 1

    def lane_block(block, carry):
        lanes = pl.ds(pl.multiple_of(block * LANES, LANES), LANES)
        for tile in range(cols // SUB):
            sums = [None] * rows
            for e in range(KERNEL):
                first = SUB * tile + SUB - KERNEL // 2 + e
                cells = [
                    extended[r, first : first + SUB, lanes] for r in range(rows + KERNEL - 1)
                ]
                for a in range(KERNEL):
                    index = a * KERNEL + e
                    tap = taps_ref[pl.ds(span - index if flipped else index, 1), lanes]
                    for i in range(rows):
                        term = cells[i + a] * tap
                        sums[i] = term if sums[i] is None else sums[i] + term
            for i in range(rows):
                emit(i, tile, lanes, sums[i])
        return carry

    lax.fori_loop(0, channels // LANES, lane_block, 0)


def conv_forward_kernel(
    own_ref, taps_ref, bias_ref, gain_ref, shift_ref,
    normed_ref, conv_ref, low_ref, high_ref,
    extended, send_sem, recv_sem,
):
    rows, cols, channels = own_ref.shape
    rim = KERNEL // 2
    route = halo_route()
    halo_barrier(route)
    copies = halo_copies(
        route, own_ref.at[pl.ds(0, rim)], own_ref.at[pl.ds(rows - rim, rim)],
        low_ref, high_ref, send_sem, recv_sem,
    )
    halo_start(route, copies)
    for edge in (0, SUB + cols):
        extended[:, edge : edge + SUB, :] = jnp.zeros(
            (rows + 2 * rim, SUB, channels), jnp.float32
        )
    extended[rim : rim + rows, SUB : SUB + cols, :] = own_ref[...].astype(jnp.float32)
    halo_finish(route, copies)

    @pl.when(jnp.logical_not(route[3]))
    def _():
        low_ref[...] = jnp.zeros_like(low_ref)
        extended[0:rim, SUB : SUB + cols, :] = jnp.zeros((rim, cols, channels), jnp.float32)

    @pl.when(jnp.logical_not(route[2]))
    def _():
        high_ref[...] = jnp.zeros_like(high_ref)
        extended[rim + rows : 2 * rim + rows, SUB : SUB + cols, :] = jnp.zeros(
            (rim, cols, channels), jnp.float32
        )

    halo_store(route, extended, low_ref, high_ref, rows, cols, rim)

    def emit(i, tile, lanes, value):
        first = i * cols + tile * SUB
        conv_ref[first : first + SUB, lanes] = value + bias_ref[:, lanes]

    conv_rows(extended, taps_ref, rows, cols, channels, False, emit)
    step = 2 * SUB

    def norm_block(block, carry):
        here = pl.ds(pl.multiple_of(block * step, step), step)
        values = conv_ref[here, :]
        centered = values - jnp.mean(values, axis=-1, keepdims=True)
        variance = jnp.mean(centered * centered, axis=-1, keepdims=True)
        scaled = centered * lax.rsqrt(variance + map_eps) * gain_ref[...] + shift_ref[...]
        normed_ref[here, :] = scaled.astype(jnp.bfloat16)
        return carry

    lax.fori_loop(0, rows * cols // step, norm_block, 0)


def conv_forward(hires, taps, bias, gain, shift):
    rows, cols, channels = hires.shape
    rim = KERNEL // 2
    cells = rows * cols
    return pl.pallas_call(
        conv_forward_kernel,
        out_shape=(
            jax.ShapeDtypeStruct((cells, channels), jnp.bfloat16),
            jax.ShapeDtypeStruct((cells, channels), jnp.float32),
            jax.ShapeDtypeStruct((rim, cols, channels), jnp.bfloat16),
            jax.ShapeDtypeStruct((rim, cols, channels), jnp.bfloat16),
        ),
        in_specs=[VMEM_SPEC] * 5,
        out_specs=(VMEM_SPEC,) * 4,
        scratch_shapes=[
            pltpu.VMEM((rows + 2 * rim, cols + 2 * SUB, channels), jnp.float32),
            pltpu.SemaphoreType.DMA((2,)),
            pltpu.SemaphoreType.DMA((2,)),
        ],
        compiler_params=kernel_params(0),
        name="conv_forward",
    )(hires, taps, bias[None], gain[None], shift[None])


def conv_backward_kernel(
    dy_ref, conv_ref, gain_ref, own_ref, low_ref, high_ref, taps_ref, pooled_grad_ref, spread_ref,
    out_ref, tap_grad_ref, sums_ref,
    extended, grads, first_low, last_low, low_in, high_in, send_sem, recv_sem,
):
    rows, cols, channels = own_ref.shape
    rim = KERNEL // 2
    route = halo_route()
    halo_barrier(route)
    sums_ref[...] = jnp.zeros_like(sums_ref)
    step = 2 * SUB
    per_row = cols // step

    def grad_block(block, carry):
        here = pl.ds(pl.multiple_of(block * step, step), step)
        values = conv_ref[here, :]
        dy = dy_ref[here, :]
        centered = values - jnp.mean(values, axis=-1, keepdims=True)
        variance = jnp.mean(centered * centered, axis=-1, keepdims=True)
        scale = lax.rsqrt(variance + map_eps)
        xhat = centered * scale
        scaled = dy * gain_ref[...]
        grad = scale * (
            scaled
            - jnp.mean(scaled, axis=-1, keepdims=True)
            - xhat * jnp.mean(scaled * xhat, axis=-1, keepdims=True)
        )
        row = block // per_row
        col = SUB + lax.rem(block, per_row) * step
        for half in range(2):
            grads[rim + row, pl.ds(pl.multiple_of(col + half * SUB, SUB), SUB), :] = grad[
                half * SUB : (half + 1) * SUB
            ]
        sums_ref[0:1, :] += jnp.sum(dy * xhat, axis=0, keepdims=True)
        sums_ref[1:2, :] += jnp.sum(dy, axis=0, keepdims=True)
        sums_ref[2:3, :] += jnp.sum(grad, axis=0, keepdims=True)
        return carry

    lax.fori_loop(0, rows * per_row, grad_block, 0)
    first_low[...] = grads[rim : 2 * rim, SUB : SUB + cols, :].astype(jnp.bfloat16)
    last_low[...] = grads[rows : rows + rim, SUB : SUB + cols, :].astype(jnp.bfloat16)
    copies = halo_copies(route, first_low, last_low, low_in, high_in, send_sem, recv_sem)
    halo_start(route, copies)
    for edge in (0, SUB + cols):
        zero = jnp.zeros((rows + 2 * rim, SUB, channels), jnp.float32)
        extended[:, edge : edge + SUB, :] = zero
        grads[:, edge : edge + SUB, :] = zero
    extended[0:rim, SUB : SUB + cols, :] = low_ref[...].astype(jnp.float32)
    extended[rim : rim + rows, SUB : SUB + cols, :] = own_ref[...].astype(jnp.float32)
    extended[rim + rows : 2 * rim + rows, SUB : SUB + cols, :] = high_ref[...].astype(jnp.float32)

    def tap_block(block, carry):
        lanes = pl.ds(pl.multiple_of(block * LANES, LANES), LANES)
        for e in range(KERNEL):
            sums = [None] * KERNEL
            for tile in range(cols // SUB):
                first = SUB * tile + SUB - rim + e
                cells = [
                    extended[r, first : first + SUB, lanes] for r in range(rows + KERNEL - 1)
                ]
                given = [
                    grads[rim + i, SUB * tile + SUB : SUB * tile + 2 * SUB, lanes]
                    for i in range(rows)
                ]
                for a in range(KERNEL):
                    for i in range(rows):
                        term = cells[i + a] * given[i]
                        sums[a] = term if sums[a] is None else sums[a] + term
            for a in range(KERNEL):
                tap_grad_ref[pl.ds(a * KERNEL + e, 1), lanes] = jnp.sum(
                    sums[a], axis=0, keepdims=True
                )
        return carry

    lax.fori_loop(0, channels // LANES, tap_block, 0)
    for pair in range(rows // 2):
        half = cols // 2
        wide = jnp.dot(
            spread_ref[...],
            pooled_grad_ref[pair * half : (pair + 1) * half, :],
            precision=lax.Precision.HIGHEST,
            preferred_element_type=jnp.float32,
        )
        for i in range(2):
            out_ref[2 * pair + i] = wide
    halo_finish(route, copies)

    @pl.when(jnp.logical_not(route[3]))
    def _():
        grads[0:rim, SUB : SUB + cols, :] = jnp.zeros((rim, cols, channels), jnp.float32)

    @pl.when(jnp.logical_not(route[2]))
    def _():
        grads[rim + rows : 2 * rim + rows, SUB : SUB + cols, :] = jnp.zeros(
            (rim, cols, channels), jnp.float32
        )

    halo_store(route, grads, low_in, high_in, rows, cols, rim)

    def emit(i, tile, lanes, value):
        out_ref[i, tile * SUB : (tile + 1) * SUB, lanes] += value

    conv_rows(grads, taps_ref, rows, cols, channels, True, emit)


def conv_backward(normed_grad, conv, gain, hires, low_rim, high_rim, taps, grad_pooled):
    rows, cols, channels = hires.shape
    rim = KERNEL // 2
    place = np.arange(cols)[:, None] // 2 == np.arange(cols // 2)[None, :]
    spread = jnp.asarray(np.where(place, 0.25, 0.0), jnp.float32)
    wide = pltpu.VMEM((rows + 2 * rim, cols + 2 * SUB, channels), jnp.float32)
    rim_low = pltpu.VMEM((rim, cols, channels), jnp.bfloat16)
    return pl.pallas_call(
        conv_backward_kernel,
        out_shape=(
            jax.ShapeDtypeStruct((rows, cols, channels), jnp.float32),
            jax.ShapeDtypeStruct((KERNEL * KERNEL, channels), jnp.float32),
            jax.ShapeDtypeStruct((SUB, channels), jnp.float32),
        ),
        in_specs=[VMEM_SPEC] * 9,
        out_specs=(VMEM_SPEC,) * 3,
        scratch_shapes=[
            wide, wide, rim_low, rim_low, rim_low, rim_low,
            pltpu.SemaphoreType.DMA((2,)),
            pltpu.SemaphoreType.DMA((2,)),
        ],
        compiler_params=kernel_params(1),
        name="conv_backward",
    )(normed_grad, conv, gain[None], hires, low_rim, high_rim, taps, grad_pooled, spread)


def mirror(index, low_half, last):
    return index + (1 - low_half) * (last - 2 * index)


def map_kernel(
    own_ref, w1_ref, b1_ref, w2_ref, branch_grad_ref, pool_ref, spread_ref,
    grad_ref, branch_ref, gw1_ref, gw2_ref, gb1_ref,
    rows_all, pre_grads, stash, from_below, from_above, pooled, hidden_grads, low_pre,
    ag_recv, ag_up, ag_down, up_recv, up_send, down_recv, down_send,
):
    count, cells, channels = rows_all.shape
    hidden = w1_ref.shape[1]
    parts = ag_recv.shape[1]
    chunk = cells // parts
    quarter = chunk // 4
    last = count - 1
    d, t = lax.axis_index("dp"), lax.axis_index("tensor")
    low_half = 1 - t // 2
    place = mirror(t, low_half, last)
    above, below = (d, t + 1), (d, t - 1)
    barrier = pltpu.get_barrier_semaphore()

    @pl.when(t < last)
    def _():
        pl.semaphore_signal(barrier, inc=1, device_id=above, device_id_type=MESH_ID)

    @pl.when(t > 0)
    def _():
        pl.semaphore_signal(barrier, inc=1, device_id=below, device_id_type=MESH_ID)

    pl.semaphore_wait(barrier, 1 + place)

    def rows_of(p):
        return pl.ds(pl.multiple_of(p * chunk, chunk), chunk)

    def gather_copy(j, p, target, send):
        return pltpu.make_async_remote_copy(
            rows_all.at[j, rows_of(p)], rows_all.at[j, rows_of(p)],
            send.at[j, p], ag_recv.at[j, p], device_id=target, device_id_type=MESH_ID,
        )

    def sum_copy(j, p, going_up):
        landing = from_below if going_up else from_above
        return pltpu.make_async_remote_copy(
            stash.at[j, rows_of(p)], landing.at[j, rows_of(p)],
            (up_send if going_up else down_send).at[j, p],
            (up_recv if going_up else down_recv).at[j, p],
            device_id=above if going_up else below, device_id_type=MESH_ID,
        )

    rows_all[t] = own_ref[...]
    for p in range(parts):
        @pl.when(t < last)
        def _():
            gather_copy(t, p, above, ag_up).start()

        @pl.when(t > 0)
        def _():
            gather_copy(t, p, below, ag_down).start()

    hidden_grads[...] = contract_cols(branch_grad_ref[...], w2_ref[...])
    gb1_ref[...] = jnp.zeros_like(gb1_ref)
    block = 256

    def one_chunk(q, carry):
        n, p = q // parts, lax.rem(q, parts)
        near = n + place * (1 - 2 * n) * (1 - n // 2)
        j = mirror(near, low_half, last)

        @pl.when(n > 0)
        def _():
            gather_copy(j, p, above, ag_up).wait_recv()

            @pl.when(jnp.logical_and(j < t, t < last))
            def _():
                gather_copy(j, p, above, ag_up).start()

            @pl.when(jnp.logical_and(j > t, t > 0))
            def _():
                gather_copy(j, p, below, ag_down).start()

        given = rows_all[j, rows_of(p), :]
        small = pl.ds(pl.multiple_of((j * parts + p) * quarter, SUB), quarter)
        for first in range(0, hidden, block):
            here = slice(first, first + block)
            pre = (
                jnp.dot(given, w1_ref[:, here], preferred_element_type=jnp.float32)
                + b1_ref[:, here]
            )
            wide_grad = hidden_grads[small, here]
            high = wide_grad.astype(jnp.bfloat16)
            rest = (wide_grad - high.astype(jnp.float32)).astype(jnp.bfloat16)
            spread_grad = jnp.dot(
                spread_ref[...], high, preferred_element_type=jnp.float32
            ) + jnp.dot(spread_ref[...], rest, preferred_element_type=jnp.float32)
            below_curve = 0.5 + 0.5 * lax.erf(pre * ROOT_HALF)
            slope = below_curve + pre * jnp.exp(-0.5 * pre * pre) * NORMAL_PEAK
            active = (pre * below_curve).astype(jnp.bfloat16)
            pooled[small, here] = jnp.dot(
                pool_ref[...], active, preferred_element_type=jnp.float32
            )
            pre_low = (spread_grad * slope).astype(jnp.bfloat16)
            gb1_ref[:, here] += jnp.sum(pre_low.astype(jnp.float32), axis=0, keepdims=True)
            low_pre[:, here] = pre_low
        pre_all = low_pre[...]
        pre_grads[j, rows_of(p), :] = pre_all
        partial_grad = contract_cols(pre_all, w1_ref[...])

        @pl.when(n == 0)
        def _():
            grad_ref[rows_of(p), :] = partial_grad

        @pl.when(n > 0)
        def _():
            stash[j, rows_of(p), :] = partial_grad.astype(jnp.bfloat16)

            @pl.when(t == 0)
            def _():
                sum_copy(j, p, True).start()

            @pl.when(t == last)
            def _():
                sum_copy(j, p, False).start()

        return carry

    lax.fori_loop(0, count * parts, one_chunk, 0)

    def pass_on(j, p, going_up):
        copy = sum_copy(j, p, going_up)
        copy.wait_recv()
        landing = from_below if going_up else from_above
        stash[j, rows_of(p), :] = (
            stash[j, rows_of(p), :].astype(jnp.float32)
            + landing[j, rows_of(p), :].astype(jnp.float32)
        ).astype(jnp.bfloat16)
        copy.start()

    middle = place == 1

    def forward_up(s, carry):
        j, p = t + 1 + s // parts, lax.rem(s, parts)
        pass_on(j, p, True)
        return carry

    def forward_down(s, carry):
        j, p = t - 1 - s // parts, lax.rem(s, parts)
        pass_on(j, p, False)
        return carry

    @pl.when(jnp.logical_and(middle, low_half == 1))
    def _():
        lax.fori_loop(0, (count - 2) * parts, forward_up, 0)
        lax.fori_loop(0, parts, forward_down, 0)

    @pl.when(jnp.logical_and(middle, low_half == 0))
    def _():
        lax.fori_loop(0, (count - 2) * parts, forward_down, 0)
        lax.fori_loop(0, parts, forward_up, 0)

    wide = 384
    rows_flat = rows_all.reshape(count * cells, channels)
    pre_flat = pre_grads.reshape(count * cells, hidden)
    for first in range(0, channels, wide):
        gw1_ref[first : first + wide, :] = contract_rows(
            rows_flat[:, first : first + wide], pre_flat[...]
        ).astype(jnp.bfloat16)
    pooled_low = pooled[...].astype(jnp.bfloat16)
    branch_ref[...] = jnp.dot(
        pooled_low, w2_ref[...], preferred_element_type=jnp.float32
    ).astype(jnp.bfloat16)
    for first in range(0, channels, wide):
        gw2_ref[first : first + wide, :] = (
            4.0 * contract_rows(branch_grad_ref[:, first : first + wide], pooled_low)
        ).astype(jnp.bfloat16)

    def finish(p, carry):
        @pl.when(t > 0)
        def _():
            sum_copy(t, p, True).wait_recv()
            grad_ref[rows_of(p), :] += from_below[t, rows_of(p), :].astype(jnp.float32)

        @pl.when(t < last)
        def _():
            sum_copy(t, p, False).wait_recv()
            grad_ref[rows_of(p), :] += from_above[t, rows_of(p), :].astype(jnp.float32)

        return carry

    lax.fori_loop(0, parts, finish, 0)

    def drain(q, carry):
        j, p = q // parts, lax.rem(q, parts)

        @pl.when(jnp.logical_and(j <= t, t < last))
        def _():
            gather_copy(j, p, above, ag_up).wait_send()

        @pl.when(jnp.logical_and(j >= t, t > 0))
        def _():
            gather_copy(j, p, below, ag_down).wait_send()

        @pl.when(j > t)
        def _():
            sum_copy(j, p, True).wait_send()

        @pl.when(j < t)
        def _():
            sum_copy(j, p, False).wait_send()

        return carry

    lax.fori_loop(0, count * parts, drain, 0)


def map_block(normed_low, w_pw1, pw1_bias, w_pw2, branch_grad_all, count, map_cols):
    cells, channels = normed_low.shape
    hidden = w_pw1.shape[1]
    chunk = 2 * map_cols
    parts = cells // chunk
    quarter = chunk // 4
    patches = branch_grad_all.shape[0]
    cell_patch = (np.arange(chunk) % map_cols) // 2
    match = np.arange(quarter)[:, None] == cell_patch[None, :]
    pool = jnp.asarray(np.where(match, 0.25, 0.0), jnp.bfloat16)
    spread = jnp.asarray(match.T, jnp.bfloat16)
    low_all = pltpu.VMEM((count, cells, channels), jnp.bfloat16)
    sems = pltpu.SemaphoreType.DMA((count, parts))
    return pl.pallas_call(
        map_kernel,
        out_shape=(
            jax.ShapeDtypeStruct((cells, channels), jnp.float32),
            jax.ShapeDtypeStruct((patches, channels), jnp.bfloat16),
            jax.ShapeDtypeStruct((channels, hidden), jnp.bfloat16),
            jax.ShapeDtypeStruct((channels, hidden), jnp.bfloat16),
            jax.ShapeDtypeStruct((1, hidden), jnp.float32),
        ),
        in_specs=[VMEM_SPEC] * 7,
        out_specs=(VMEM_SPEC,) * 5,
        scratch_shapes=[
            low_all,
            pltpu.VMEM((count, cells, hidden), jnp.bfloat16),
            low_all,
            low_all,
            low_all,
            pltpu.VMEM((patches, hidden), jnp.float32),
            pltpu.VMEM((patches, hidden), jnp.float32),
            pltpu.VMEM((chunk, hidden), jnp.bfloat16),
        ]
        + [sems] * 7,
        compiler_params=kernel_params(2),
        name="map_block",
    )(normed_low, w_pw1, pw1_bias[None], w_pw2, branch_grad_all, pool, spread)


def rows_in(local_rows):
    return lax.all_gather(local_rows, "tensor", axis=0, tiled=True)


def rows_out(hidden_low, weight):
    return lax.psum_scatter(
        jnp.dot(hidden_low, weight, preferred_element_type=jnp.float32).astype(jnp.bfloat16),
        "tensor",
        scatter_dimension=0,
        tiled=True,
    ).astype(jnp.float32)


def grads_in(local_grad):
    return lax.all_gather(local_grad, "tensor", axis=0, tiled=True)


def grads_out(grad_pairs):
    running = None
    for grad_low, weight in grad_pairs:
        product = contract_cols(grad_low, weight)
        running = product if running is None else running + product
    return lax.psum_scatter(
        running.astype(jnp.bfloat16), "tensor", scatter_dimension=0, tiled=True
    ).astype(jnp.float32)


def dp_rows(partial_grad):
    return lax.psum_scatter(
        partial_grad.astype(jnp.bfloat16), "dp", scatter_dimension=0, tiled=True
    ).astype(jnp.float32)


def dp_cols(partial_grad, count):
    rows, width = partial_grad.shape
    cut = partial_grad.astype(jnp.bfloat16).reshape(rows, count, width // count).transpose(1, 0, 2)
    return lax.psum_scatter(cut, "dp", scatter_dimension=0, tiled=False).astype(jnp.float32)


def scores_of(query_heads, key_heads, key_live, score_scale):
    raw_scores = (
        jnp.einsum("qhd,khd->hqk", query_heads, key_heads, preferred_element_type=jnp.float32)
        * score_scale
    )
    return jnp.where(key_live[None, None, :], raw_scores, masked_score)


def local(
    patches,
    hires,
    valid_rows,
    ln1_gain,
    ln1_bias,
    w_qkv,
    qv_bias,
    w_out,
    out_bias,
    ln2_gain,
    ln2_bias,
    w_fc1,
    fc1_bias,
    w_fc2,
    fc2_bias,
    dw_weight,
    dw_bias,
    lnc_gain,
    lnc_bias,
    w_pw1,
    pw1_bias,
    w_pw2,
    pw2_bias,
    layer_scale,
    w_adapt,
    adapt_bias,
    adapt_gain,
    grad_out,
):
    tensor_count = lax.axis_size("tensor")
    data_index = lax.axis_index("dp")
    tensor_index = lax.axis_index("tensor")
    last_tensor = tensor_count - 1
    odd_half = data_index % IMG_SPAN == 1
    image_index = data_index // IMG_SPAN
    rim_width = KERNEL // 2
    map_rows, map_cols, channels = hires.shape
    patch_rows = patches.shape[0]
    map_cells = map_rows * map_cols
    score_scale = HEAD_DIM ** (-0.5)
    normed_low, conv_flat, low_rim, high_rim = conv_forward(
        hires, dw_weight, dw_bias, lnc_gain, lnc_bias
    )
    half_patches = patch_rows * tensor_count
    hidden_units = w_pw1.shape[1]
    mlp_grad_all = grads_in(grad_out)
    adapt_grad_all = (mlp_grad_all.astype(jnp.float32) * adapt_gain).astype(jnp.bfloat16)
    grad_pooled_all = contract_cols(adapt_grad_all, w_adapt)
    branch_grad_all = (layer_scale * (grad_pooled_all * 0.25)).astype(jnp.bfloat16)
    normed_grad, branch_partial, grad_w_pw1, grad_w_pw2, grad_pw1_bias = map_block(
        normed_low, w_pw1, pw1_bias, w_pw2, branch_grad_all, tensor_count, map_cols
    )
    grad_pw1_bias = grad_pw1_bias[0]
    branch_mean = (
        lax.psum_scatter(branch_partial, "tensor", scatter_dimension=0, tiled=True).astype(
            jnp.float32
        )
        + pw2_bias
    )
    map_mean = (
        hires.astype(jnp.float32)
        .reshape(map_rows // 2, 2, map_cols // 2, 2, channels)
        .sum(axis=(1, 3))
        .reshape(patch_rows, channels)
        * 0.25
    )
    pooled_low = (map_mean + layer_scale * branch_mean).astype(jnp.bfloat16)
    adapted = jnp.dot(pooled_low, w_adapt, preferred_element_type=jnp.float32) + adapt_bias
    inputs = patches.astype(jnp.float32)
    attn_in = layer_norm(inputs, ln1_gain, ln1_bias, vit_eps).astype(jnp.bfloat16)
    attn_all = rows_in(attn_in)
    queries = (jnp.dot(attn_all, w_qkv[0], preferred_element_type=jnp.float32) + qv_bias[0]).astype(
        jnp.bfloat16
    )
    keys_own = jnp.dot(attn_all, w_qkv[1], preferred_element_type=jnp.float32).astype(jnp.bfloat16)
    values_own = (
        jnp.dot(attn_all, w_qkv[2], preferred_element_type=jnp.float32) + qv_bias[1]
    ).astype(jnp.bfloat16)
    pair_rows = partner_2(jnp.stack([keys_own, values_own]), "dp", 0)
    keys_all = jnp.concatenate([keys_own, pair_rows[0]], 0)
    values_all = jnp.concatenate([values_own, pair_rows[1]], 0)
    half_rows = keys_own.shape[0]
    heads_here = queries.shape[1] // HEAD_DIM
    own_first = data_index % IMG_SPAN * half_rows
    other_first = (1 - data_index % IMG_SPAN) * half_rows
    key_place = jnp.concatenate(
        [own_first + jnp.arange(half_rows), other_first + jnp.arange(half_rows)]
    )
    image_valid = jnp.sum(jnp.where(jnp.arange(valid_rows.shape[0]) == image_index, valid_rows, 0))
    key_live = key_place // SIDE < image_valid
    query_heads = queries.reshape(half_rows, heads_here, HEAD_DIM)
    key_heads = keys_all.reshape(2 * half_rows, heads_here, HEAD_DIM)
    value_heads = values_all.reshape(2 * half_rows, heads_here, HEAD_DIM)
    scores = scores_of(query_heads, key_heads, key_live, score_scale)
    score_peak = jnp.max(scores, axis=-1, keepdims=True)
    weights_raw = jnp.exp(scores - score_peak)
    totals = jnp.sum(weights_raw, axis=-1, keepdims=True)
    probabilities = weights_raw / totals
    log_total = score_peak + jnp.log(totals)
    attended = jnp.einsum(
        "hqk,khd->qhd",
        probabilities.astype(jnp.bfloat16),
        value_heads,
        preferred_element_type=jnp.float32,
    )
    attended_low = attended.reshape(half_rows, heads_here * HEAD_DIM).astype(jnp.bfloat16)
    projected = rows_out(attended_low, w_out) + out_bias
    middle = inputs + projected
    mlp_in = layer_norm(middle, ln2_gain, ln2_bias, vit_eps).astype(jnp.bfloat16)
    mlp_all = rows_in(mlp_in)
    mlp_pre = jnp.dot(mlp_all, w_fc1, preferred_element_type=jnp.float32) + fc1_bias
    mlp_hidden = gelu_exact(mlp_pre).astype(jnp.bfloat16)
    mlp_branch = rows_out(mlp_hidden, w_fc2) + fc2_bias
    vit_out = middle + mlp_branch
    joined_out = (vit_out + adapt_gain * adapted).astype(jnp.bfloat16)
    upstream = grad_out.astype(jnp.float32)
    grad_adapt_gain = jnp.sum(upstream * adapted, 0)
    adapt_grad = (upstream * adapt_gain).astype(jnp.bfloat16)
    grad_adapt_bias = jnp.sum(adapt_grad.astype(jnp.float32), 0)
    grad_pooled = contract_cols(adapt_grad, w_adapt)
    grad_fc2_bias = jnp.sum(upstream, 0)
    data_count = lax.axis_size("dp")
    adapt_rows = channels // (data_count * tensor_count)
    pooled_split = pooled_low.reshape(patch_rows, data_count, tensor_count, adapt_rows)
    pooled_split = pooled_split.transpose(2, 0, 1, 3).reshape(tensor_count, patch_rows, data_count * adapt_rows)
    pooled_mine = lax.all_to_all(pooled_split, "tensor", 0, 0, tiled=False).reshape(half_patches, data_count * adapt_rows)
    grad_w_adapt = contract_rows(pooled_mine, adapt_grad_all)
    grad_w_fc2 = contract_rows(mlp_hidden, mlp_grad_all)
    hidden_grad = contract_cols(mlp_grad_all, w_fc2)
    unused_out, gelu_pull = jax.vjp(gelu_exact, mlp_pre)
    pre_grad = gelu_pull(hidden_grad)[0].astype(jnp.bfloat16)
    grad_fc1_bias = jnp.sum(pre_grad.astype(jnp.float32), 0)
    grad_w_fc1 = contract_rows(mlp_all, pre_grad)
    mlp_in_grad = grads_out(((pre_grad, w_fc1),))
    unused_out, norm_two_pull = jax.vjp(
        partial(layer_norm, epsilon=vit_eps), middle, ln2_gain, ln2_bias
    )
    middle_part, grad_ln2_gain, grad_ln2_bias = norm_two_pull(mlp_in_grad)
    middle_grad = upstream + middle_part
    proj_grad = middle_grad.astype(jnp.bfloat16)
    grad_out_bias = jnp.sum(proj_grad.astype(jnp.float32), 0)
    proj_grad_all = grads_in(proj_grad)
    grad_w_out = contract_rows(attended_low, proj_grad_all)
    attended_grad = contract_cols(proj_grad_all, w_out).astype(jnp.bfloat16)
    head_grad = attended_grad.reshape(half_rows, heads_here, HEAD_DIM)
    probs_again = jnp.exp(scores_of(query_heads, key_heads, key_live, score_scale) - log_total)
    value_grad = jnp.einsum(
        "hqk,qhd->khd",
        probs_again.astype(jnp.bfloat16),
        head_grad,
        preferred_element_type=jnp.float32,
    )
    prob_grad = jnp.einsum(
        "qhd,khd->hqk", head_grad, value_heads, preferred_element_type=jnp.float32
    )
    row_dot = jnp.sum(probs_again * prob_grad, axis=-1, keepdims=True)
    score_grad = (probs_again * (prob_grad - row_dot)).astype(jnp.bfloat16)
    query_grad = (
        jnp.einsum("hqk,khd->qhd", score_grad, key_heads, preferred_element_type=jnp.float32)
        * score_scale
    )
    key_grad = (
        jnp.einsum("hqk,qhd->khd", score_grad, query_heads, preferred_element_type=jnp.float32)
        * score_scale
    )
    local_width = heads_here * HEAD_DIM
    query_low = query_grad.reshape(half_rows, local_width).astype(jnp.bfloat16)
    key_grad = key_grad.reshape(2 * half_rows, local_width)
    value_grad = value_grad.reshape(2 * half_rows, local_width)
    returned = partner_2(
        jnp.stack([key_grad[half_rows:], value_grad[half_rows:]]).astype(jnp.bfloat16), "dp", 0
    ).astype(jnp.float32)
    key_low = (key_grad[:half_rows] + returned[0]).astype(jnp.bfloat16)
    value_low = (value_grad[:half_rows] + returned[1]).astype(jnp.bfloat16)
    grad_qv_bias = jnp.stack(
        [jnp.sum(query_low.astype(jnp.float32), 0), jnp.sum(value_low.astype(jnp.float32), 0)]
    )
    grad_w_qkv = jnp.stack(
        [
            contract_rows(attn_all, query_low),
            contract_rows(attn_all, key_low),
            contract_rows(attn_all, value_low),
        ]
    )
    attn_in_grad = grads_out(((query_low, w_qkv[0]), (key_low, w_qkv[1]), (value_low, w_qkv[2])))
    unused_out, norm_one_pull = jax.vjp(
        partial(layer_norm, epsilon=vit_eps), inputs, ln1_gain, ln1_bias
    )
    input_part, grad_ln1_gain, grad_ln1_bias = norm_one_pull(attn_in_grad)
    grad_patches = middle_grad + input_part
    grad_layer_scale = jnp.sum(grad_pooled * branch_mean, 0)
    branch_grad = (layer_scale * (grad_pooled * 0.25)).astype(jnp.bfloat16)
    grad_pw2_bias = 4.0 * jnp.sum(branch_grad.astype(jnp.float32), 0)
    grad_hires, grad_dw_weight, norm_sums = conv_backward(
        normed_grad, conv_flat, lnc_gain, hires, low_rim, high_rim, dw_weight, grad_pooled
    )
    grad_lnc_gain, grad_lnc_bias, grad_dw_bias = norm_sums[0], norm_sums[1], norm_sums[2]
    reduced_qkv = lax.psum_scatter(grad_w_qkv.astype(jnp.bfloat16), "dp", scatter_dimension=1, tiled=True).astype(jnp.float32)
    reduced_out = dp_cols(grad_w_out, data_count)
    reduced_fc1 = dp_rows(grad_w_fc1)
    reduced_fc2 = dp_cols(grad_w_fc2, data_count)
    reduced_pw1 = dp_rows(grad_w_pw1)
    reduced_pw2 = dp_rows(grad_w_pw2).T
    shared_w_adapt = dp_rows(grad_w_adapt)
    here = (jnp.arange(tensor_count) == tensor_index).astype(jnp.float32)
    pieces = []
    for item in (grad_qv_bias, grad_fc1_bias[None], grad_pw1_bias[None]):
        rows, width = item.shape
        cut = item.reshape(rows, data_count, 1, width // data_count) * here[None, None, :, None]
        pieces.append(cut.transpose(1, 2, 0, 3).reshape(data_count * tensor_count, -1))
    for item in (
        grad_ln1_gain, grad_ln1_bias, grad_out_bias, grad_ln2_gain, grad_ln2_bias, grad_fc2_bias,
        grad_dw_bias, grad_lnc_gain, grad_lnc_bias, grad_pw2_bias, grad_layer_scale,
        grad_adapt_bias, grad_adapt_gain,
    ):
        pieces.append(item.reshape(data_count * tensor_count, -1))
    taps = KERNEL * KERNEL
    pieces.append(
        grad_dw_weight.reshape(taps, data_count * tensor_count, -1).transpose(1, 0, 2).reshape(data_count * tensor_count, -1)
    )
    widths = [piece.shape[1] for piece in pieces]
    packed = lax.psum_scatter(
        jnp.concatenate(pieces, 1), ("dp", "tensor"), scatter_dimension=0, tiled=True
    )[0]
    parts, first = [], 0
    for width in widths:
        parts.append(packed[first : first + width])
        first += width
    (
        reduced_qv_bias, reduced_fc1_bias, reduced_pw1_bias,
        shared_ln1_gain, shared_ln1_bias, shared_out_bias, shared_ln2_gain, shared_ln2_bias, shared_fc2_bias,
        shared_dw_bias, shared_lnc_gain, shared_lnc_bias, shared_pw2_bias, shared_layer_scale,
        shared_adapt_bias, shared_adapt_gain, shared_dw_weight,
    ) = parts
    reduced_qv_bias = reduced_qv_bias.reshape(2, -1)
    shared_dw_weight = shared_dw_weight.reshape(taps, -1)
    return (
        joined_out,
        grad_patches,
        grad_hires,
        shared_ln1_gain,
        shared_ln1_bias,
        reduced_qkv,
        reduced_qv_bias,
        reduced_out,
        shared_out_bias,
        shared_ln2_gain,
        shared_ln2_bias,
        reduced_fc1,
        reduced_fc1_bias,
        reduced_fc2,
        shared_fc2_bias,
        shared_dw_weight,
        shared_dw_bias,
        shared_lnc_gain,
        shared_lnc_bias,
        reduced_pw1,
        reduced_pw1_bias,
        reduced_pw2,
        shared_pw2_bias,
        shared_layer_scale,
        shared_w_adapt,
        shared_adapt_bias,
        shared_adapt_gain,
    )


def solution(mesh):
    return jax.shard_map(
        local,
        mesh=mesh,
        in_specs=(
            P(("dp", "tensor"), None),
            P(("dp", "tensor"), None, None),
            P(),
            P(),
            P(),
            P(None, None, "tensor"),
            P(None, "tensor"),
            P("tensor", None),
            P(),
            P(),
            P(),
            P(None, "tensor"),
            P("tensor"),
            P("tensor", None),
            P(),
            P(),
            P(),
            P(),
            P(),
            P(None, "tensor"),
            P("tensor"),
            P("tensor", None),
            P(),
            P(),
            P(),
            P(),
            P(),
            P(("dp", "tensor"), None),
        ),
        out_specs=(
            P(("dp", "tensor"), None),
            P(("dp", "tensor"), None),
            P(("dp", "tensor"), None, None),
            P(("dp", "tensor")),
            P(("dp", "tensor")),
            P(None, "dp", "tensor"),
            P(None, ("tensor", "dp")),
            P("tensor", "dp"),
            P(("dp", "tensor")),
            P(("dp", "tensor")),
            P(("dp", "tensor")),
            P("dp", "tensor"),
            P(("tensor", "dp")),
            P("tensor", "dp"),
            P(("dp", "tensor")),
            P(None, ("dp", "tensor")),
            P(("dp", "tensor")),
            P(("dp", "tensor")),
            P(("dp", "tensor")),
            P("dp", "tensor"),
            P(("tensor", "dp")),
            P("tensor", "dp"),
            P(("dp", "tensor")),
            P(("dp", "tensor")),
            P(("dp", "tensor"), None),
            P(("dp", "tensor")),
            P(("dp", "tensor")),
        ),
        check_vma=False,
    )
```

```python
from functools import partial

import jax
import numpy as np
import jax.numpy as jnp
from jax import lax
from jax.experimental import pallas as pl
from jax.experimental.pallas import tpu as pltpu
from jax.sharding import PartitionSpec as P

HEAD_DIM = 64
SIDE = 24
KERNEL = 7
IMG_SPAN = 2


vit_eps = 1e-05
map_eps = 1e-06
masked_score = -1e30
ROOT_HALF = 0.7071067811865476
NORMAL_PEAK = 0.3989422804014327


def padded_2(value, sides, width):
    for axis, dim in sides:
        count, length = (lax.axis_size(axis), value.shape[dim])
        up = [(i, (i + 1) % count) for i in range(count)]
        down = [(j, i) for i, j in up]
        last = lax.slice_in_dim(value, length - width, length, axis=dim)
        first = lax.slice_in_dim(value, 0, width, axis=dim)
        before = lax.ppermute(last, axis, up)
        after = lax.ppermute(first, axis, down)
        value = jnp.concatenate([before, value, after], axis=dim)
    return value


def partner_2(block, axis, apart):
    count = lax.axis_size(axis)
    route = []
    for low in range(count):
        high = low | 1 << apart
        if high != low and high < count:
            route += [(low, high), (high, low)]
    return lax.ppermute(block, axis, route)


def layer_norm(values, gain_vec, bias_vec, epsilon):
    centered = values - jnp.mean(values, axis=-1, keepdims=True)
    variance = jnp.mean(centered * centered, axis=-1, keepdims=True)
    return centered * lax.rsqrt(variance + epsilon) * gain_vec + bias_vec


def gelu_exact(values):
    return jax.nn.gelu(values, approximate=False)


def contract_rows(left_side, right_side):
    return lax.dot_general(
        left_side, right_side, (((0,), (0,)), ((), ())), preferred_element_type=jnp.float32
    )


def contract_cols(left_side, right_side):
    return lax.dot_general(
        left_side, right_side, (((1,), (1,)), ((), ())), preferred_element_type=jnp.float32
    )


MESH_ID = pl.DeviceIdType.MESH
VMEM_SPEC = pl.BlockSpec(memory_space=pltpu.VMEM)
LANES = 128
SUB = 8
VMEM_BYTES = 60 * 1024 * 1024


def kernel_params(collective_id=None):
    if collective_id is None:
        return pltpu.CompilerParams(vmem_limit_bytes=VMEM_BYTES)
    return pltpu.CompilerParams(
        vmem_limit_bytes=VMEM_BYTES, collective_id=collective_id, has_side_effects=True
    )


def halo_route():
    count = lax.axis_size("tensor")
    d, t = lax.axis_index("dp"), lax.axis_index("tensor")
    odd = lax.rem(d, IMG_SPAN)
    up = (d + (t + 1) // count, lax.rem(t + 1, count))
    down = (d - 1 + (t + count - 1) // count, lax.rem(t + count - 1, count))
    up_here = (t + 1) // count + odd < 2
    down_here = t + odd > 0
    return up, down, up_here, down_here


def halo_barrier(route):
    up, down, up_here, down_here = route
    barrier = pltpu.get_barrier_semaphore()

    @pl.when(up_here)
    def _():
        pl.semaphore_signal(barrier, inc=1, device_id=up, device_id_type=MESH_ID)

    @pl.when(down_here)
    def _():
        pl.semaphore_signal(barrier, inc=1, device_id=down, device_id_type=MESH_ID)

    count = lax.axis_size("tensor")
    d, t = lax.axis_index("dp"), lax.axis_index("tensor")
    odd = lax.rem(d, IMG_SPAN)
    ups = 1 - ((t + 1) // count + odd) // 2
    downs = (t + odd + count) // (count + 1)
    pl.semaphore_wait(barrier, ups + downs)


def halo_copies(route, first_rows, last_rows, low_ref, high_ref, send_sem, recv_sem):
    up, down, up_here, down_here = route
    to_up = pltpu.make_async_remote_copy(
        last_rows, low_ref, send_sem.at[0], recv_sem.at[0], device_id=up, device_id_type=MESH_ID
    )
    to_down = pltpu.make_async_remote_copy(
        first_rows, high_ref, send_sem.at[1], recv_sem.at[1], device_id=down, device_id_type=MESH_ID
    )
    return to_up, to_down


def halo_start(route, copies):
    @pl.when(route[2])
    def _():
        copies[0].start()

    @pl.when(route[3])
    def _():
        copies[1].start()


def halo_finish(route, copies):
    @pl.when(route[2])
    def _():
        copies[0].wait_send()
        copies[1].wait_recv()

    @pl.when(route[3])
    def _():
        copies[1].wait_send()
        copies[0].wait_recv()


def halo_store(route, extended, low_ref, high_ref, rows, cols, rim):
    @pl.when(route[3])
    def _():
        extended[0:rim, SUB : SUB + cols, :] = low_ref[...].astype(jnp.float32)

    @pl.when(route[2])
    def _():
        extended[rim + rows : 2 * rim + rows, SUB : SUB + cols, :] = high_ref[...].astype(
            jnp.float32
        )


def conv_rows(extended, taps_ref, rows, cols, channels, flipped, emit):
    span = KERNEL * KERNEL - 1

    def lane_block(block, carry):
        lanes = pl.ds(pl.multiple_of(block * LANES, LANES), LANES)
        for tile in range(cols // SUB):
            sums = [None] * rows
            for e in range(KERNEL):
                first = SUB * tile + SUB - KERNEL // 2 + e
                cells = [
                    extended[r, first : first + SUB, lanes] for r in range(rows + KERNEL - 1)
                ]
                for a in range(KERNEL):
                    index = a * KERNEL + e
                    tap = taps_ref[pl.ds(span - index if flipped else index, 1), lanes]
                    for i in range(rows):
                        term = cells[i + a] * tap
                        sums[i] = term if sums[i] is None else sums[i] + term
            for i in range(rows):
                emit(i, tile, lanes, sums[i])
        return carry

    lax.fori_loop(0, channels // LANES, lane_block, 0)


def conv_forward_kernel(
    own_ref, taps_ref, bias_ref, gain_ref, shift_ref,
    normed_ref, conv_ref, low_ref, high_ref,
    extended, send_sem, recv_sem,
):
    rows, cols, channels = own_ref.shape
    rim = KERNEL // 2
    route = halo_route()
    halo_barrier(route)
    copies = halo_copies(
        route, own_ref.at[pl.ds(0, rim)], own_ref.at[pl.ds(rows - rim, rim)],
        low_ref, high_ref, send_sem, recv_sem,
    )
    halo_start(route, copies)
    for edge in (0, SUB + cols):
        extended[:, edge : edge + SUB, :] = jnp.zeros(
            (rows + 2 * rim, SUB, channels), jnp.float32
        )
    extended[rim : rim + rows, SUB : SUB + cols, :] = own_ref[...].astype(jnp.float32)
    halo_finish(route, copies)

    @pl.when(jnp.logical_not(route[3]))
    def _():
        low_ref[...] = jnp.zeros_like(low_ref)
        extended[0:rim, SUB : SUB + cols, :] = jnp.zeros((rim, cols, channels), jnp.float32)

    @pl.when(jnp.logical_not(route[2]))
    def _():
        high_ref[...] = jnp.zeros_like(high_ref)
        extended[rim + rows : 2 * rim + rows, SUB : SUB + cols, :] = jnp.zeros(
            (rim, cols, channels), jnp.float32
        )

    halo_store(route, extended, low_ref, high_ref, rows, cols, rim)

    def emit(i, tile, lanes, value):
        first = i * cols + tile * SUB
        conv_ref[first : first + SUB, lanes] = value + bias_ref[:, lanes]

    conv_rows(extended, taps_ref, rows, cols, channels, False, emit)
    step = 2 * SUB

    def norm_block(block, carry):
        here = pl.ds(pl.multiple_of(block * step, step), step)
        values = conv_ref[here, :]
        centered = values - jnp.mean(values, axis=-1, keepdims=True)
        variance = jnp.mean(centered * centered, axis=-1, keepdims=True)
        scaled = centered * lax.rsqrt(variance + map_eps) * gain_ref[...] + shift_ref[...]
        normed_ref[here, :] = scaled.astype(jnp.bfloat16)
        return carry

    lax.fori_loop(0, rows * cols // step, norm_block, 0)


def conv_forward(hires, taps, bias, gain, shift):
    rows, cols, channels = hires.shape
    rim = KERNEL // 2
    cells = rows * cols
    return pl.pallas_call(
        conv_forward_kernel,
        out_shape=(
            jax.ShapeDtypeStruct((cells, channels), jnp.bfloat16),
            jax.ShapeDtypeStruct((cells, channels), jnp.float32),
            jax.ShapeDtypeStruct((rim, cols, channels), jnp.bfloat16),
            jax.ShapeDtypeStruct((rim, cols, channels), jnp.bfloat16),
        ),
        in_specs=[VMEM_SPEC] * 5,
        out_specs=(VMEM_SPEC,) * 4,
        scratch_shapes=[
            pltpu.VMEM((rows + 2 * rim, cols + 2 * SUB, channels), jnp.float32),
            pltpu.SemaphoreType.DMA((2,)),
            pltpu.SemaphoreType.DMA((2,)),
        ],
        compiler_params=kernel_params(0),
        name="conv_forward",
    )(hires, taps, bias[None], gain[None], shift[None])


def conv_backward_kernel(
    dy_ref, conv_ref, gain_ref, own_ref, low_ref, high_ref, taps_ref, pooled_grad_ref, spread_ref,
    out_ref, tap_grad_ref, sums_ref,
    extended, grads, first_low, last_low, low_in, high_in, send_sem, recv_sem,
):
    rows, cols, channels = own_ref.shape
    rim = KERNEL // 2
    route = halo_route()
    halo_barrier(route)
    sums_ref[...] = jnp.zeros_like(sums_ref)
    step = 2 * SUB
    per_row = cols // step

    def grad_block(block, carry):
        here = pl.ds(pl.multiple_of(block * step, step), step)
        values = conv_ref[here, :]
        dy = dy_ref[here, :]
        centered = values - jnp.mean(values, axis=-1, keepdims=True)
        variance = jnp.mean(centered * centered, axis=-1, keepdims=True)
        scale = lax.rsqrt(variance + map_eps)
        xhat = centered * scale
        scaled = dy * gain_ref[...]
        grad = scale * (
            scaled
            - jnp.mean(scaled, axis=-1, keepdims=True)
            - xhat * jnp.mean(scaled * xhat, axis=-1, keepdims=True)
        )
        row = block // per_row
        col = SUB + lax.rem(block, per_row) * step
        for half in range(2):
            grads[rim + row, pl.ds(pl.multiple_of(col + half * SUB, SUB), SUB), :] = grad[
                half * SUB : (half + 1) * SUB
            ]
        sums_ref[0:1, :] += jnp.sum(dy * xhat, axis=0, keepdims=True)
        sums_ref[1:2, :] += jnp.sum(dy, axis=0, keepdims=True)
        sums_ref[2:3, :] += jnp.sum(grad, axis=0, keepdims=True)
        return carry

    lax.fori_loop(0, rows * per_row, grad_block, 0)
    first_low[...] = grads[rim : 2 * rim, SUB : SUB + cols, :].astype(jnp.bfloat16)
    last_low[...] = grads[rows : rows + rim, SUB : SUB + cols, :].astype(jnp.bfloat16)
    copies = halo_copies(route, first_low, last_low, low_in, high_in, send_sem, recv_sem)
    halo_start(route, copies)
    for edge in (0, SUB + cols):
        zero = jnp.zeros((rows + 2 * rim, SUB, channels), jnp.float32)
        extended[:, edge : edge + SUB, :] = zero
        grads[:, edge : edge + SUB, :] = zero
    extended[0:rim, SUB : SUB + cols, :] = low_ref[...].astype(jnp.float32)
    extended[rim : rim + rows, SUB : SUB + cols, :] = own_ref[...].astype(jnp.float32)
    extended[rim + rows : 2 * rim + rows, SUB : SUB + cols, :] = high_ref[...].astype(jnp.float32)

    def tap_block(block, carry):
        lanes = pl.ds(pl.multiple_of(block * LANES, LANES), LANES)
        for e in range(KERNEL):
            sums = [None] * KERNEL
            for tile in range(cols // SUB):
                first = SUB * tile + SUB - rim + e
                cells = [
                    extended[r, first : first + SUB, lanes] for r in range(rows + KERNEL - 1)
                ]
                given = [
                    grads[rim + i, SUB * tile + SUB : SUB * tile + 2 * SUB, lanes]
                    for i in range(rows)
                ]
                for a in range(KERNEL):
                    for i in range(rows):
                        term = cells[i + a] * given[i]
                        sums[a] = term if sums[a] is None else sums[a] + term
            for a in range(KERNEL):
                tap_grad_ref[pl.ds(a * KERNEL + e, 1), lanes] = jnp.sum(
                    sums[a], axis=0, keepdims=True
                )
        return carry

    lax.fori_loop(0, channels // LANES, tap_block, 0)
    for pair in range(rows // 2):
        half = cols // 2
        wide = jnp.dot(
            spread_ref[...],
            pooled_grad_ref[pair * half : (pair + 1) * half, :],
            precision=lax.Precision.HIGHEST,
            preferred_element_type=jnp.float32,
        )
        for i in range(2):
            out_ref[2 * pair + i] = wide
    halo_finish(route, copies)

    @pl.when(jnp.logical_not(route[3]))
    def _():
        grads[0:rim, SUB : SUB + cols, :] = jnp.zeros((rim, cols, channels), jnp.float32)

    @pl.when(jnp.logical_not(route[2]))
    def _():
        grads[rim + rows : 2 * rim + rows, SUB : SUB + cols, :] = jnp.zeros(
            (rim, cols, channels), jnp.float32
        )

    halo_store(route, grads, low_in, high_in, rows, cols, rim)

    def emit(i, tile, lanes, value):
        out_ref[i, tile * SUB : (tile + 1) * SUB, lanes] += value

    conv_rows(grads, taps_ref, rows, cols, channels, True, emit)


def conv_backward(normed_grad, conv, gain, hires, low_rim, high_rim, taps, grad_pooled):
    rows, cols, channels = hires.shape
    rim = KERNEL // 2
    place = np.arange(cols)[:, None] // 2 == np.arange(cols // 2)[None, :]
    spread = jnp.asarray(np.where(place, 0.25, 0.0), jnp.float32)
    wide = pltpu.VMEM((rows + 2 * rim, cols + 2 * SUB, channels), jnp.float32)
    rim_low = pltpu.VMEM((rim, cols, channels), jnp.bfloat16)
    return pl.pallas_call(
        conv_backward_kernel,
        out_shape=(
            jax.ShapeDtypeStruct((rows, cols, channels), jnp.float32),
            jax.ShapeDtypeStruct((KERNEL * KERNEL, channels), jnp.float32),
            jax.ShapeDtypeStruct((SUB, channels), jnp.float32),
        ),
        in_specs=[VMEM_SPEC] * 9,
        out_specs=(VMEM_SPEC,) * 3,
        scratch_shapes=[
            wide, wide, rim_low, rim_low, rim_low, rim_low,
            pltpu.SemaphoreType.DMA((2,)),
            pltpu.SemaphoreType.DMA((2,)),
        ],
        compiler_params=kernel_params(1),
        name="conv_backward",
    )(normed_grad, conv, gain[None], hires, low_rim, high_rim, taps, grad_pooled, spread)


def mirror(index, low_half, last):
    return index + (1 - low_half) * (last - 2 * index)


def map_kernel(
    own_ref, w1_ref, b1_ref, w2_ref, branch_grad_ref, pool_ref, spread_ref,
    grad_ref, branch_ref, gw1_ref, gw2_ref, gb1_ref,
    rows_all, pre_grads, stash, from_below, from_above, pooled, hidden_grads, low_pre,
    ag_recv, ag_up, ag_down, up_recv, up_send, down_recv, down_send,
):
    count, cells, channels = rows_all.shape
    hidden = w1_ref.shape[1]
    parts = ag_recv.shape[1]
    chunk = cells // parts
    quarter = chunk // 4
    last = count - 1
    d, t = lax.axis_index("dp"), lax.axis_index("tensor")
    low_half = 1 - t // 2
    place = mirror(t, low_half, last)
    above, below = (d, t + 1), (d, t - 1)
    barrier = pltpu.get_barrier_semaphore()

    @pl.when(t < last)
    def _():
        pl.semaphore_signal(barrier, inc=1, device_id=above, device_id_type=MESH_ID)

    @pl.when(t > 0)
    def _():
        pl.semaphore_signal(barrier, inc=1, device_id=below, device_id_type=MESH_ID)

    pl.semaphore_wait(barrier, 1 + place)

    def rows_of(p):
        return pl.ds(pl.multiple_of(p * chunk, chunk), chunk)

    def gather_copy(j, p, target, send):
        return pltpu.make_async_remote_copy(
            rows_all.at[j, rows_of(p)], rows_all.at[j, rows_of(p)],
            send.at[j, p], ag_recv.at[j, p], device_id=target, device_id_type=MESH_ID,
        )

    def sum_copy(j, p, going_up):
        landing = from_below if going_up else from_above
        return pltpu.make_async_remote_copy(
            stash.at[j, rows_of(p)], landing.at[j, rows_of(p)],
            (up_send if going_up else down_send).at[j, p],
            (up_recv if going_up else down_recv).at[j, p],
            device_id=above if going_up else below, device_id_type=MESH_ID,
        )

    rows_all[t] = own_ref[...]
    for p in range(parts):
        @pl.when(t < last)
        def _():
            gather_copy(t, p, above, ag_up).start()

        @pl.when(t > 0)
        def _():
            gather_copy(t, p, below, ag_down).start()

    hidden_grads[...] = contract_cols(branch_grad_ref[...], w2_ref[...])
    gb1_ref[...] = jnp.zeros_like(gb1_ref)
    block = 256

    def one_chunk(q, carry):
        n, p = q // parts, lax.rem(q, parts)
        near = n + place * (1 - 2 * n) * (1 - n // 2)
        j = mirror(near, low_half, last)

        @pl.when(n > 0)
        def _():
            gather_copy(j, p, above, ag_up).wait_recv()

            @pl.when(jnp.logical_and(j < t, t < last))
            def _():
                gather_copy(j, p, above, ag_up).start()

            @pl.when(jnp.logical_and(j > t, t > 0))
            def _():
                gather_copy(j, p, below, ag_down).start()

        given = rows_all[j, rows_of(p), :]
        small = pl.ds(pl.multiple_of((j * parts + p) * quarter, SUB), quarter)
        for first in range(0, hidden, block):
            here = slice(first, first + block)
            pre = (
                jnp.dot(given, w1_ref[:, here], preferred_element_type=jnp.float32)
                + b1_ref[:, here]
            )
            wide_grad = hidden_grads[small, here]
            high = wide_grad.astype(jnp.bfloat16)
            rest = (wide_grad - high.astype(jnp.float32)).astype(jnp.bfloat16)
            spread_grad = jnp.dot(
                spread_ref[...], high, preferred_element_type=jnp.float32
            ) + jnp.dot(spread_ref[...], rest, preferred_element_type=jnp.float32)
            below_curve = 0.5 + 0.5 * lax.erf(pre * ROOT_HALF)
            slope = below_curve + pre * jnp.exp(-0.5 * pre * pre) * NORMAL_PEAK
            active = (pre * below_curve).astype(jnp.bfloat16)
            pooled[small, here] = jnp.dot(
                pool_ref[...], active, preferred_element_type=jnp.float32
            )
            pre_low = (spread_grad * slope).astype(jnp.bfloat16)
            gb1_ref[:, here] += jnp.sum(pre_low.astype(jnp.float32), axis=0, keepdims=True)
            low_pre[:, here] = pre_low
        pre_all = low_pre[...]
        pre_grads[j, rows_of(p), :] = pre_all
        partial_grad = contract_cols(pre_all, w1_ref[...])

        @pl.when(n == 0)
        def _():
            grad_ref[rows_of(p), :] = partial_grad

        @pl.when(n > 0)
        def _():
            stash[j, rows_of(p), :] = partial_grad.astype(jnp.bfloat16)

            @pl.when(t == 0)
            def _():
                sum_copy(j, p, True).start()

            @pl.when(t == last)
            def _():
                sum_copy(j, p, False).start()

        return carry

    lax.fori_loop(0, count * parts, one_chunk, 0)

    def pass_on(j, p, going_up):
        copy = sum_copy(j, p, going_up)
        copy.wait_recv()
        landing = from_below if going_up else from_above
        stash[j, rows_of(p), :] = (
            stash[j, rows_of(p), :].astype(jnp.float32)
            + landing[j, rows_of(p), :].astype(jnp.float32)
        ).astype(jnp.bfloat16)
        copy.start()

    middle = place == 1

    def forward_up(s, carry):
        j, p = t + 1 + s // parts, lax.rem(s, parts)
        pass_on(j, p, True)
        return carry

    def forward_down(s, carry):
        j, p = t - 1 - s // parts, lax.rem(s, parts)
        pass_on(j, p, False)
        return carry

    @pl.when(jnp.logical_and(middle, low_half == 1))
    def _():
        lax.fori_loop(0, (count - 2) * parts, forward_up, 0)
        lax.fori_loop(0, parts, forward_down, 0)

    @pl.when(jnp.logical_and(middle, low_half == 0))
    def _():
        lax.fori_loop(0, (count - 2) * parts, forward_down, 0)
        lax.fori_loop(0, parts, forward_up, 0)

    wide = 384
    rows_flat = rows_all.reshape(count * cells, channels)
    pre_flat = pre_grads.reshape(count * cells, hidden)
    for first in range(0, channels, wide):
        gw1_ref[first : first + wide, :] = contract_rows(
            rows_flat[:, first : first + wide], pre_flat[...]
        ).astype(jnp.bfloat16)
    pooled_low = pooled[...].astype(jnp.bfloat16)
    branch_ref[...] = jnp.dot(
        pooled_low, w2_ref[...], preferred_element_type=jnp.float32
    ).astype(jnp.bfloat16)
    for first in range(0, channels, wide):
        gw2_ref[first : first + wide, :] = (
            4.0 * contract_rows(branch_grad_ref[:, first : first + wide], pooled_low)
        ).astype(jnp.bfloat16)

    def finish(p, carry):
        @pl.when(t > 0)
        def _():
            sum_copy(t, p, True).wait_recv()
            grad_ref[rows_of(p), :] += from_below[t, rows_of(p), :].astype(jnp.float32)

        @pl.when(t < last)
        def _():
            sum_copy(t, p, False).wait_recv()
            grad_ref[rows_of(p), :] += from_above[t, rows_of(p), :].astype(jnp.float32)

        return carry

    lax.fori_loop(0, parts, finish, 0)

    def drain(q, carry):
        j, p = q // parts, lax.rem(q, parts)

        @pl.when(jnp.logical_and(j <= t, t < last))
        def _():
            gather_copy(j, p, above, ag_up).wait_send()

        @pl.when(jnp.logical_and(j >= t, t > 0))
        def _():
            gather_copy(j, p, below, ag_down).wait_send()

        @pl.when(j > t)
        def _():
            sum_copy(j, p, True).wait_send()

        @pl.when(j < t)
        def _():
            sum_copy(j, p, False).wait_send()

        return carry

    lax.fori_loop(0, count * parts, drain, 0)


def map_block(normed_low, w_pw1, pw1_bias, w_pw2, branch_grad_all, count, map_cols):
    cells, channels = normed_low.shape
    hidden = w_pw1.shape[1]
    chunk = 2 * map_cols
    parts = cells // chunk
    quarter = chunk // 4
    patches = branch_grad_all.shape[0]
    cell_patch = (np.arange(chunk) % map_cols) // 2
    match = np.arange(quarter)[:, None] == cell_patch[None, :]
    pool = jnp.asarray(np.where(match, 0.25, 0.0), jnp.bfloat16)
    spread = jnp.asarray(match.T, jnp.bfloat16)
    low_all = pltpu.VMEM((count, cells, channels), jnp.bfloat16)
    sems = pltpu.SemaphoreType.DMA((count, parts))
    return pl.pallas_call(
        map_kernel,
        out_shape=(
            jax.ShapeDtypeStruct((cells, channels), jnp.float32),
            jax.ShapeDtypeStruct((patches, channels), jnp.bfloat16),
            jax.ShapeDtypeStruct((channels, hidden), jnp.bfloat16),
            jax.ShapeDtypeStruct((channels, hidden), jnp.bfloat16),
            jax.ShapeDtypeStruct((1, hidden), jnp.float32),
        ),
        in_specs=[VMEM_SPEC] * 7,
        out_specs=(VMEM_SPEC,) * 5,
        scratch_shapes=[
            low_all,
            pltpu.VMEM((count, cells, hidden), jnp.bfloat16),
            low_all,
            low_all,
            low_all,
            pltpu.VMEM((patches, hidden), jnp.float32),
            pltpu.VMEM((patches, hidden), jnp.float32),
            pltpu.VMEM((chunk, hidden), jnp.bfloat16),
        ]
        + [sems] * 7,
        compiler_params=kernel_params(2),
        name="map_block",
    )(normed_low, w_pw1, pw1_bias[None], w_pw2, branch_grad_all, pool, spread)


def bits_of(count):
    return count.bit_length() - 1


class Halving:
    def __init__(self, source, landings, send, recv, top_first):
        self.count = lax.axis_size("dp")
        self.d, self.t = lax.axis_index("dp"), lax.axis_index("tensor")
        self.source, self.landings = source, landings
        self.send, self.recv, self.top_first = send, recv, top_first
        self.stages = bits_of(self.count)

    def plan(self, stage):
        here = self.source if stage == 0 else self.landings[stage - 1]
        half = self.count >> (stage + 1)
        top = self.top_first and stage > 0
        bit = self.stages - stage if top else stage
        own = lax.rem(self.d // (1 << bit), 2)
        partner = self.d + (1 - 2 * own) * (1 << bit)
        base = self.count - 2 * half

        def place(i, value):
            return value * half + i if top else 2 * i + value

        def copy(i):
            return pltpu.make_async_remote_copy(
                here.at[place(i, 1 - own)], self.landings[stage].at[i],
                self.send.at[base + i], self.recv.at[base + i],
                device_id=(partner, self.t), device_id_type=MESH_ID,
            )

        return here, half, own, place, copy

    def start(self, stage):
        here, half, own, place, copy = self.plan(stage)

        def body(i, carry):
            copy(i).start()
            return carry

        lax.fori_loop(0, half, body, 0)

    def finish(self, stage, out=None):
        here, half, own, place, copy = self.plan(stage)
        landing = self.landings[stage]
        rows = landing.shape[1]

        def body(i, carry):
            copy(i).wait()
            total = here[place(i, own)].astype(jnp.float32) + landing[i].astype(jnp.float32)
            if out is None:
                landing[i] = total.astype(jnp.bfloat16)
            else:
                out[...] = total
            return carry

        lax.fori_loop(0, half, body, 0)


def halving_scratch(count, rows, cols):
    landings = []
    half = count // 2
    while half >= 1:
        landings.append(pltpu.VMEM((half, rows, cols), jnp.bfloat16))
        half //= 2
    return landings + [pltpu.SemaphoreType.DMA((count - 1,))] * 2


class Ring:
    def __init__(self):
        self.count = lax.axis_size("tensor")
        self.d, self.t = lax.axis_index("dp"), lax.axis_index("tensor")

    def at(self, k):
        return lax.rem(self.t + k, self.count)

    def share_copy(self, buffer, sems, k, source):
        return pltpu.make_async_remote_copy(
            buffer.at[source], buffer.at[source], sems.at[0, k], sems.at[1, source],
            device_id=(self.d, self.at(k)), device_id_type=MESH_ID,
        )

    def share_start(self, buffer, sems):
        for k in range(1, self.count):
            self.share_copy(buffer, sems, k, self.t).start()

    def share_finish(self, buffer, sems):
        for k in range(1, self.count):
            self.share_copy(buffer, sems, k, self.t).wait_send()
        for k in range(1, self.count):
            self.share_copy(buffer, sems, k, self.at(k)).wait_recv()

    def give_copy(self, parts, landing, sems, k, slot, part):
        return pltpu.make_async_remote_copy(
            parts.at[part], landing.at[slot], sems.at[0, k], sems.at[1, slot],
            device_id=(self.d, self.at(k)), device_id_type=MESH_ID,
        )

    def give_start(self, parts, landing, sems):
        for k in range(1, self.count):
            self.give_copy(parts, landing, sems, k, self.t, self.at(k)).start()

    def give_finish(self, parts, landing, sems):
        for k in range(1, self.count):
            self.give_copy(parts, landing, sems, k, self.t, self.at(k)).wait_send()
        for k in range(1, self.count):
            self.give_copy(parts, landing, sems, k, self.at(k), self.at(k)).wait_recv()

    def total(self, parts, landing):
        value = parts[self.t].astype(jnp.float32)
        for k in range(1, self.count):
            value = value + landing[self.at(k)].astype(jnp.float32)
        return value


def norm_parts(values, epsilon):
    centered = values - jnp.mean(values, axis=-1, keepdims=True)
    variance = jnp.mean(centered * centered, axis=-1, keepdims=True)
    scale = lax.rsqrt(variance + epsilon)
    return centered * scale, scale


def norm_pull(grad, xhat, scale, gain):
    scaled = grad * gain
    return scale * (
        scaled
        - jnp.mean(scaled, axis=-1, keepdims=True)
        - xhat * jnp.mean(scaled * xhat, axis=-1, keepdims=True)
    )


def row_sum(values):
    return jnp.sum(values, axis=0, keepdims=True)


def flat_low(buffer):
    count, rows, cols = buffer.shape
    return buffer[...].astype(jnp.float32).reshape(count * rows, cols).astype(jnp.bfloat16)


def fill_parts(parts, value):
    count, rows, _ = parts.shape
    for j in range(count):
        parts[j] = value[j * rows : (j + 1) * rows].astype(jnp.bfloat16)


def vit_kernel(
    patches_ref, attn_ref, given_ref, map_mean_ref, grad_pooled_ref, branch_parts, gw1_ref, gw2_ref,
    ln1_gain, wqkv_ref, qv_bias, wout_ref, out_bias, ln2_gain, ln2_bias,
    wfc1_ref, fc1_bias, wfc2_ref, fc2_bias, wadapt_ref, adapt_bias, adapt_gain,
    pw2_bias, layer_scale, live_ref, pick_ref,
    joined_ref, grad_patches_ref, red1_ref, red2_ref, gfc1_ref, gfc2_ref, gout_ref, gqkv_ref,
    gadapt_ref, sums_model, sums_map, sums_heads, sums_ff,
    keys_all, values_all, kv_own, kv_other, queries, hidden_grad, probs, attended, middle_keep,
    hidden, pre_grad, dqkv, dkv_send, dkv_other, mlp_flat, proj_flat, upstream_keep,
    proj_parts, proj_land, mlp_all, in_parts, in_land, out_parts, out_land, proj_all,
    attn_parts, attn_land, branch_land, pool_parts, pool_land,
    *rest,
):
    ring = Ring()
    count, d, t = ring.count, ring.d, ring.t
    stages = bits_of(lax.axis_size("dp"))
    job_refs = stages + 2
    job1 = Halving(gw1_ref, rest[:stages], rest[stages], rest[stages + 1], False)
    rest = rest[job_refs:]
    job2 = Halving(gw2_ref, rest[:stages], rest[stages], rest[stages + 1], True)
    (
        proj_sems, mlp_sems, in_sems, out_sems, share_sems, attn_sems, branch_sems, pool_sems, pair_sems,
    ) = rest[job_refs:]
    rows, model = patches_ref.shape
    half_rows, width = queries.shape
    heads = width // HEAD_DIM
    scale = HEAD_DIM**-0.5
    partner = d + 1 - 2 * lax.rem(d, 2)

    barrier = pltpu.get_barrier_semaphore()
    for k in range(1, count):
        pl.semaphore_signal(barrier, inc=1, device_id=(d, ring.at(k)), device_id_type=MESH_ID)
    for bit in range(stages):
        step = 1 << bit
        other = d + (1 - 2 * lax.rem(d // step, 2)) * step
        pl.semaphore_signal(barrier, inc=1, device_id=(other, t), device_id_type=MESH_ID)
    pl.semaphore_wait(barrier, count - 1 + stages)

    job1.start(0)
    job2.start(0)
    sums_model[...] = jnp.zeros_like(sums_model)
    sums_map[...] = jnp.zeros_like(sums_map)
    sums_heads[...] = jnp.zeros_like(sums_heads)
    sums_ff[...] = jnp.zeros_like(sums_ff)

    attn = attn_ref[...]
    own_keys = jnp.dot(attn, wqkv_ref[1], preferred_element_type=jnp.float32).astype(jnp.bfloat16)
    own_values = (
        jnp.dot(attn, wqkv_ref[2], preferred_element_type=jnp.float32) + qv_bias[1:2, :]
    ).astype(jnp.bfloat16)
    kv_own[:, 0:width] = own_keys
    kv_own[:, width : 2 * width] = own_values

    def pair_copy(source, target, slot):
        return pltpu.make_async_remote_copy(
            source, target, pair_sems.at[0, slot], pair_sems.at[1, slot],
            device_id=(partner, t), device_id_type=MESH_ID,
        )

    pair_copy(kv_own, kv_other, 0).start()
    ring.give_start(branch_parts, branch_land, branch_sems)
    queries[...] = (
        jnp.dot(attn, wqkv_ref[0], preferred_element_type=jnp.float32) + qv_bias[0:1, :]
    ).astype(jnp.bfloat16)
    keys_all[0:half_rows, :] = own_keys
    values_all[0:half_rows, :] = own_values
    hidden_grad[...] = contract_cols(given_ref[...], wfc2_ref[...])
    pair_copy(kv_own, kv_other, 0).wait()
    keys_all[half_rows : 2 * half_rows, :] = kv_other[:, 0:width]
    values_all[half_rows : 2 * half_rows, :] = kv_other[:, width : 2 * width]
    live = live_ref[...] > 0.5
    for h in range(heads):
        here = slice(h * HEAD_DIM, (h + 1) * HEAD_DIM)
        raw = contract_cols(queries[:, here], keys_all[:, here]) * scale
        scores = jnp.where(live, raw, masked_score)
        grown = jnp.exp(scores - jnp.max(scores, axis=-1, keepdims=True))
        prob = grown * (1.0 / jnp.sum(grown, axis=-1, keepdims=True))
        probs[h] = prob
        attended[:, here] = jnp.dot(
            prob.astype(jnp.bfloat16), values_all[:, here], preferred_element_type=jnp.float32
        ).astype(jnp.bfloat16)
    fill_parts(
        proj_parts, jnp.dot(attended[...], wout_ref[...], preferred_element_type=jnp.float32)
    )
    ring.give_start(proj_parts, proj_land, proj_sems)
    job1.finish(0)
    job1.start(1)
    job2.finish(0)
    job2.start(1)
    ring.give_finish(proj_parts, proj_land, proj_sems)
    inputs = patches_ref[...].astype(jnp.float32)
    middle = inputs + (ring.total(proj_parts, proj_land) + out_bias[...])
    middle_keep[...] = middle
    xhat, _ = norm_parts(middle, vit_eps)
    mlp_all[t] = (xhat * ln2_gain[...] + ln2_bias[...]).astype(jnp.bfloat16)
    ring.share_start(mlp_all, mlp_sems)

    ring.give_finish(branch_parts, branch_land, branch_sems)
    branch = ring.total(branch_parts, branch_land) + pw2_bias[...]
    pooled = (map_mean_ref[...] + layer_scale[...] * branch).astype(jnp.bfloat16)
    pooled_grad = grad_pooled_ref[...]
    sums_map[0:1, :] = 4.0 * row_sum(
        (layer_scale[...] * (pooled_grad * 0.25)).astype(jnp.bfloat16).astype(jnp.float32)
    )
    sums_map[1:2, :] = row_sum(pooled_grad * branch)
    channels = pooled.shape[1]
    per_peer = channels // count
    place = lax.broadcasted_iota(jnp.int32, (channels, per_peer), 0)
    for j in range(count):
        choose = jnp.where(place == pick_ref[j : j + 1, :], 1.0, 0.0).astype(jnp.bfloat16)
        pool_parts[j] = jnp.dot(pooled, choose, preferred_element_type=jnp.float32).astype(
            jnp.bfloat16
        )
    ring.give_start(pool_parts, pool_land, pool_sems)
    adapted = (
        jnp.dot(pooled, wadapt_ref[...], preferred_element_type=jnp.float32) + adapt_bias[...]
    )
    upstream = upstream_keep[...].astype(jnp.float32)
    sums_model[5:6, :] = row_sum(upstream)
    sums_model[6:7, :] = row_sum(
        (upstream * adapt_gain[...]).astype(jnp.bfloat16).astype(jnp.float32)
    )
    sums_model[7:8, :] = row_sum(upstream * adapted)
    adapted_part = adapt_gain[...] * adapted

    ring.share_finish(mlp_all, mlp_sems)
    mlp_flat[...] = flat_low(mlp_all)
    units = wfc1_ref.shape[1]
    block = 256
    for first in range(0, units, block):
        cols = slice(first, first + block)
        pre = (
            jnp.dot(mlp_flat[...], wfc1_ref[:, cols], preferred_element_type=jnp.float32)
            + fc1_bias[:, cols]
        )
        below_curve = 0.5 + 0.5 * lax.erf(pre * ROOT_HALF)
        slope = below_curve + pre * jnp.exp(-0.5 * pre * pre) * NORMAL_PEAK
        hidden[:, cols] = (pre * below_curve).astype(jnp.bfloat16)
        pre_low = (hidden_grad[:, cols] * slope).astype(jnp.bfloat16)
        pre_grad[:, cols] = pre_low
        sums_ff[0:1, cols] = row_sum(pre_low.astype(jnp.float32))
    fill_parts(in_parts, contract_cols(pre_grad[...], wfc1_ref[...]))
    ring.give_start(in_parts, in_land, in_sems)
    fill_parts(
        out_parts, jnp.dot(hidden[...], wfc2_ref[...], preferred_element_type=jnp.float32)
    )
    ring.give_start(out_parts, out_land, out_sems)
    gfc1_ref[...] = contract_rows(mlp_flat[...], pre_grad[...]).astype(jnp.bfloat16)
    ring.give_finish(in_parts, in_land, in_sems)
    mlp_in_grad = ring.total(in_parts, in_land)
    middle = middle_keep[...]
    xhat, rs = norm_parts(middle, vit_eps)
    sums_model[3:4, :] = row_sum(mlp_in_grad * xhat)
    sums_model[4:5, :] = row_sum(mlp_in_grad)
    middle_grad = upstream + norm_pull(mlp_in_grad, xhat, rs, ln2_gain[...])
    grad_patches_ref[...] = middle_grad
    proj_low = middle_grad.astype(jnp.bfloat16)
    sums_model[2:3, :] = row_sum(proj_low.astype(jnp.float32))
    proj_all[t] = proj_low
    ring.share_start(proj_all, share_sems)
    gfc2_ref[...] = contract_rows(given_ref[...], hidden[...]).astype(jnp.bfloat16)
    job1.finish(1)
    job1.start(2)
    job2.finish(1)
    job2.start(2)
    for stage in range(2, stages - 1):
        job1.finish(stage)
        job1.start(stage + 1)
        job2.finish(stage)
        job2.start(stage + 1)
    ring.give_finish(out_parts, out_land, out_sems)
    vit_out = middle + (ring.total(out_parts, out_land) + fc2_bias[...])
    joined_ref[...] = (vit_out + adapted_part).astype(jnp.bfloat16)

    ring.share_finish(proj_all, share_sems)
    proj_flat[...] = flat_low(proj_all)
    attended_grad = contract_cols(proj_flat[...], wout_ref[...]).astype(jnp.bfloat16)
    for h in range(heads):
        here = slice(h * HEAD_DIM, (h + 1) * HEAD_DIM)
        there = slice(width + h * HEAD_DIM, width + (h + 1) * HEAD_DIM)
        head_grad = attended_grad[:, here]
        prob = probs[h]
        value_part = contract_rows(prob.astype(jnp.bfloat16), head_grad)
        prob_grad = contract_cols(head_grad, values_all[:, here])
        dot_rows = jnp.sum(prob * prob_grad, axis=-1, keepdims=True)
        score_grad = (prob * (prob_grad - dot_rows)).astype(jnp.bfloat16)
        dqkv[:, here] = (
            jnp.dot(score_grad, keys_all[:, here], preferred_element_type=jnp.float32) * scale
        ).astype(jnp.bfloat16)
        key_part = contract_rows(score_grad, queries[:, here]) * scale
        dkv_send[:, here] = key_part[half_rows:].astype(jnp.bfloat16)
        dkv_send[:, there] = value_part[half_rows:].astype(jnp.bfloat16)
        hidden_grad[:, here] = key_part[:half_rows]
        hidden_grad[:, there] = value_part[:half_rows]
    pair_copy(dkv_send, dkv_other, 1).start()
    gout_ref[...] = contract_rows(proj_flat[...], attended[...]).astype(jnp.bfloat16)
    pair_copy(dkv_send, dkv_other, 1).wait()
    kv_grad = (hidden_grad[:, 0 : 2 * width] + dkv_other[...].astype(jnp.float32)).astype(
        jnp.bfloat16
    )
    dqkv[:, width : 3 * width] = kv_grad
    attn_grad = contract_cols(dqkv[:, 0:width], wqkv_ref[0])
    for part in (1, 2):
        attn_grad += contract_cols(dqkv[:, part * width : (part + 1) * width], wqkv_ref[part])
    fill_parts(attn_parts, attn_grad)
    ring.give_start(attn_parts, attn_land, attn_sems)
    sums_heads[0:1, :] = row_sum(dqkv[:, 0:width].astype(jnp.float32))
    sums_heads[1:2, :] = row_sum(dqkv[:, 2 * width : 3 * width].astype(jnp.float32))
    gqkv_ref[...] = contract_rows(attn_ref[...], dqkv[...]).astype(jnp.bfloat16)
    ring.give_finish(pool_parts, pool_land, pool_sems)
    pool_land[t] = pool_parts[t]
    adapt_grad = (given_ref[...].astype(jnp.float32) * adapt_gain[...]).astype(jnp.bfloat16)
    gadapt_ref[...] = contract_rows(flat_low(pool_land), adapt_grad).astype(jnp.bfloat16)
    job1.finish(stages - 1, red1_ref)
    job2.finish(stages - 1, red2_ref)
    ring.give_finish(attn_parts, attn_land, attn_sems)
    attn_in_grad = ring.total(attn_parts, attn_land)
    xhat, rs = norm_parts(inputs, vit_eps)
    sums_model[0:1, :] = row_sum(attn_in_grad * xhat)
    sums_model[1:2, :] = row_sum(attn_in_grad)
    grad_patches_ref[...] += norm_pull(attn_in_grad, xhat, rs, ln1_gain[...])


def vit_block(
    patches, attn_all, grad_all, grad_own, map_mean, grad_pooled, branch_partial, gw1, gw2,
    ln1_gain, w_qkv, qv_bias, w_out, out_bias, ln2_gain, ln2_bias,
    w_fc1, fc1_bias, w_fc2, fc2_bias, w_adapt, adapt_bias, adapt_gain, pw2_bias, layer_scale,
    key_live,
):
    count = lax.axis_size("tensor")
    data = lax.axis_size("dp")
    rows, model = patches.shape
    half_rows = rows * count
    width = w_out.shape[0]
    heads = width // HEAD_DIM
    units = w_fc1.shape[1]
    channels = w_adapt.shape[0]
    map_rows, map_cols = gw1.shape[0] // data, gw1.shape[1]
    stage_rows = channels // (data * count)
    place = np.arange(channels // count)
    pick = np.stack(
        [(place // stage_rows * count + j) * stage_rows + place % stage_rows for j in range(count)]
    ).astype(np.int32)
    f32, low = jnp.float32, jnp.bfloat16

    def vmem(*shape, dtype=low):
        return pltpu.VMEM(shape, dtype)

    shard = vmem(count, rows, model)
    scratch = [
        vmem(2 * half_rows, width), vmem(2 * half_rows, width),
        vmem(half_rows, 2 * width), vmem(half_rows, 2 * width), vmem(half_rows, width),
        vmem(half_rows, units, dtype=f32), vmem(heads, half_rows, 2 * half_rows, dtype=f32),
        vmem(half_rows, width), vmem(rows, model, dtype=f32),
        vmem(half_rows, units), vmem(half_rows, units), vmem(half_rows, 3 * width),
        vmem(half_rows, 2 * width), vmem(half_rows, 2 * width),
        vmem(half_rows, model), vmem(half_rows, model),
    ]
    shards = [shard] * 10 + [
        vmem(count, rows, channels),
        vmem(count, rows, channels // count), vmem(count, rows, channels // count),
    ]
    job = halving_scratch(data, map_rows, map_cols)
    sems = [pltpu.SemaphoreType.DMA((2, count))] * 9

    def kernel(*refs):
        ins, rest = refs[:27], refs[27:]
        grad_own_ref = ins[26]
        outs, others = rest[:13], rest[13:]
        vit_kernel(*ins[:26], *outs, *others[:16], grad_own_ref, *others[16:])

    def out(*shape, dtype=low):
        return jax.ShapeDtypeStruct(shape, dtype)

    return pl.pallas_call(
        kernel,
        out_shape=(
            out(rows, model), out(rows, model, dtype=f32),
            out(map_rows, map_cols, dtype=f32), out(map_rows, map_cols, dtype=f32),
            out(model, units), out(model, units), out(model, width), out(model, 3 * width),
            out(channels // count, model),
            out(SUB, model, dtype=f32), out(SUB, channels, dtype=f32),
            out(SUB, width, dtype=f32), out(SUB, units, dtype=f32),
        ),
        in_specs=[VMEM_SPEC] * 27,
        out_specs=(VMEM_SPEC,) * 13,
        scratch_shapes=scratch + shards + job + job + sems,
        compiler_params=kernel_params(3),
        name="vit_block",
    )(
        patches, attn_all, grad_all, map_mean, grad_pooled,
        branch_partial.reshape(count, rows, channels),
        gw1.reshape(data, map_rows, map_cols), gw2.reshape(data, map_rows, map_cols),
        ln1_gain[None], w_qkv, qv_bias, w_out, out_bias[None], ln2_gain[None], ln2_bias[None],
        w_fc1, fc1_bias[None], w_fc2, fc2_bias[None], w_adapt, adapt_bias[None], adapt_gain[None],
        pw2_bias[None], layer_scale[None], key_live, jnp.asarray(pick), grad_own,
    )


def rows_in(local_rows):
    return lax.all_gather(local_rows, "tensor", axis=0, tiled=True)


def rows_out(hidden_low, weight):
    return lax.psum_scatter(
        jnp.dot(hidden_low, weight, preferred_element_type=jnp.float32).astype(jnp.bfloat16),
        "tensor",
        scatter_dimension=0,
        tiled=True,
    ).astype(jnp.float32)


def grads_in(local_grad):
    return lax.all_gather(local_grad, "tensor", axis=0, tiled=True)


def grads_out(grad_pairs):
    running = None
    for grad_low, weight in grad_pairs:
        product = contract_cols(grad_low, weight)
        running = product if running is None else running + product
    return lax.psum_scatter(
        running.astype(jnp.bfloat16), "tensor", scatter_dimension=0, tiled=True
    ).astype(jnp.float32)


def dp_rows(partial_grad):
    return lax.psum_scatter(
        partial_grad.astype(jnp.bfloat16), "dp", scatter_dimension=0, tiled=True
    ).astype(jnp.float32)


def dp_cols(partial_grad, count):
    rows, width = partial_grad.shape
    cut = partial_grad.astype(jnp.bfloat16).reshape(rows, count, width // count).transpose(1, 0, 2)
    return lax.psum_scatter(cut, "dp", scatter_dimension=0, tiled=False).astype(jnp.float32)


def scores_of(query_heads, key_heads, key_live, score_scale):
    raw_scores = (
        jnp.einsum("qhd,khd->hqk", query_heads, key_heads, preferred_element_type=jnp.float32)
        * score_scale
    )
    return jnp.where(key_live[None, None, :], raw_scores, masked_score)


def local(
    patches,
    hires,
    valid_rows,
    ln1_gain,
    ln1_bias,
    w_qkv,
    qv_bias,
    w_out,
    out_bias,
    ln2_gain,
    ln2_bias,
    w_fc1,
    fc1_bias,
    w_fc2,
    fc2_bias,
    dw_weight,
    dw_bias,
    lnc_gain,
    lnc_bias,
    w_pw1,
    pw1_bias,
    w_pw2,
    pw2_bias,
    layer_scale,
    w_adapt,
    adapt_bias,
    adapt_gain,
    grad_out,
):
    tensor_count = lax.axis_size("tensor")
    data_index = lax.axis_index("dp")
    tensor_index = lax.axis_index("tensor")
    last_tensor = tensor_count - 1
    odd_half = data_index % IMG_SPAN == 1
    image_index = data_index // IMG_SPAN
    rim_width = KERNEL // 2
    map_rows, map_cols, channels = hires.shape
    patch_rows = patches.shape[0]
    map_cells = map_rows * map_cols
    score_scale = HEAD_DIM ** (-0.5)
    normed_low, conv_flat, low_rim, high_rim = conv_forward(
        hires, dw_weight, dw_bias, lnc_gain, lnc_bias
    )
    half_patches = patch_rows * tensor_count
    hidden_units = w_pw1.shape[1]
    mlp_grad_all = grads_in(grad_out)
    adapt_grad_all = (mlp_grad_all.astype(jnp.float32) * adapt_gain).astype(jnp.bfloat16)
    grad_pooled_all = contract_cols(adapt_grad_all, w_adapt)
    branch_grad_all = (layer_scale * (grad_pooled_all * 0.25)).astype(jnp.bfloat16)
    normed_grad, branch_partial, grad_w_pw1, grad_w_pw2, grad_pw1_bias = map_block(
        normed_low, w_pw1, pw1_bias, w_pw2, branch_grad_all, tensor_count, map_cols
    )
    grad_pw1_bias = grad_pw1_bias[0]
    map_mean = (
        hires.astype(jnp.float32)
        .reshape(map_rows // 2, 2, map_cols // 2, 2, channels)
        .sum(axis=(1, 3))
        .reshape(patch_rows, channels)
        * 0.25
    )
    grad_pooled = lax.dynamic_slice_in_dim(grad_pooled_all, tensor_index * patch_rows, patch_rows)
    inputs = patches.astype(jnp.float32)
    attn_all = rows_in(layer_norm(inputs, ln1_gain, ln1_bias, vit_eps).astype(jnp.bfloat16))
    half_rows = half_patches
    own_first = data_index % IMG_SPAN * half_rows
    other_first = (1 - data_index % IMG_SPAN) * half_rows
    key_place = jnp.concatenate(
        [own_first + jnp.arange(half_rows), other_first + jnp.arange(half_rows)]
    )
    image_valid = jnp.sum(jnp.where(jnp.arange(valid_rows.shape[0]) == image_index, valid_rows, 0))
    key_live = (key_place // SIDE < image_valid).astype(jnp.float32)[None]
    data_count = lax.axis_size("dp")
    (
        joined_out, grad_patches, reduced_pw1, reduced_pw2, gfc1, gfc2, gout, gqkv, gadapt,
        sums_model, sums_map, sums_heads, sums_ff,
    ) = vit_block(
        patches, attn_all, mlp_grad_all, grad_out, map_mean, grad_pooled, branch_partial,
        grad_w_pw1, grad_w_pw2,
        ln1_gain, w_qkv, qv_bias, w_out, out_bias, ln2_gain, ln2_bias,
        w_fc1, fc1_bias, w_fc2, fc2_bias, w_adapt, adapt_bias, adapt_gain, pw2_bias, layer_scale,
        key_live,
    )
    reduced_pw2 = reduced_pw2.T
    (
        grad_ln1_gain, grad_ln1_bias, grad_out_bias, grad_ln2_gain, grad_ln2_bias, grad_fc2_bias,
        grad_adapt_bias, grad_adapt_gain,
    ) = [sums_model[i] for i in range(8)]
    grad_pw2_bias, grad_layer_scale = sums_map[0], sums_map[1]
    grad_qv_bias, grad_fc1_bias = sums_heads[:2], sums_ff[0]
    grad_hires, grad_dw_weight, norm_sums = conv_backward(
        normed_grad, conv_flat, lnc_gain, hires, low_rim, high_rim, dw_weight, grad_pooled
    )
    grad_lnc_gain, grad_lnc_bias, grad_dw_bias = norm_sums[0], norm_sums[1], norm_sums[2]
    width = w_out.shape[0]
    reduced_qkv = dp_rows(gqkv).reshape(-1, 3, width).transpose(1, 0, 2)
    reduced_out = dp_rows(gout).T
    reduced_fc1 = dp_rows(gfc1)
    reduced_fc2 = dp_rows(gfc2).T
    shared_w_adapt = dp_rows(gadapt)
    here = (jnp.arange(tensor_count) == tensor_index).astype(jnp.float32)
    pieces = []
    for item in (grad_qv_bias, grad_fc1_bias[None], grad_pw1_bias[None]):
        rows, width = item.shape
        cut = item.reshape(rows, data_count, 1, width // data_count) * here[None, None, :, None]
        pieces.append(cut.transpose(1, 2, 0, 3).reshape(data_count * tensor_count, -1))
    for item in (
        grad_ln1_gain, grad_ln1_bias, grad_out_bias, grad_ln2_gain, grad_ln2_bias, grad_fc2_bias,
        grad_dw_bias, grad_lnc_gain, grad_lnc_bias, grad_pw2_bias, grad_layer_scale,
        grad_adapt_bias, grad_adapt_gain,
    ):
        pieces.append(item.reshape(data_count * tensor_count, -1))
    taps = KERNEL * KERNEL
    pieces.append(
        grad_dw_weight.reshape(taps, data_count * tensor_count, -1).transpose(1, 0, 2).reshape(data_count * tensor_count, -1)
    )
    widths = [piece.shape[1] for piece in pieces]
    packed = lax.psum_scatter(
        jnp.concatenate(pieces, 1), ("dp", "tensor"), scatter_dimension=0, tiled=True
    )[0]
    parts, first = [], 0
    for width in widths:
        parts.append(packed[first : first + width])
        first += width
    (
        reduced_qv_bias, reduced_fc1_bias, reduced_pw1_bias,
        shared_ln1_gain, shared_ln1_bias, shared_out_bias, shared_ln2_gain, shared_ln2_bias, shared_fc2_bias,
        shared_dw_bias, shared_lnc_gain, shared_lnc_bias, shared_pw2_bias, shared_layer_scale,
        shared_adapt_bias, shared_adapt_gain, shared_dw_weight,
    ) = parts
    reduced_qv_bias = reduced_qv_bias.reshape(2, -1)
    shared_dw_weight = shared_dw_weight.reshape(taps, -1)
    return (
        joined_out,
        grad_patches,
        grad_hires,
        shared_ln1_gain,
        shared_ln1_bias,
        reduced_qkv,
        reduced_qv_bias,
        reduced_out,
        shared_out_bias,
        shared_ln2_gain,
        shared_ln2_bias,
        reduced_fc1,
        reduced_fc1_bias,
        reduced_fc2,
        shared_fc2_bias,
        shared_dw_weight,
        shared_dw_bias,
        shared_lnc_gain,
        shared_lnc_bias,
        reduced_pw1,
        reduced_pw1_bias,
        reduced_pw2,
        shared_pw2_bias,
        shared_layer_scale,
        shared_w_adapt,
        shared_adapt_bias,
        shared_adapt_gain,
    )


def solution(mesh):
    return jax.shard_map(
        local,
        mesh=mesh,
        in_specs=(
            P(("dp", "tensor"), None),
            P(("dp", "tensor"), None, None),
            P(),
            P(),
            P(),
            P(None, None, "tensor"),
            P(None, "tensor"),
            P("tensor", None),
            P(),
            P(),
            P(),
            P(None, "tensor"),
            P("tensor"),
            P("tensor", None),
            P(),
            P(),
            P(),
            P(),
            P(),
            P(None, "tensor"),
            P("tensor"),
            P("tensor", None),
            P(),
            P(),
            P(),
            P(),
            P(),
            P(("dp", "tensor"), None),
        ),
        out_specs=(
            P(("dp", "tensor"), None),
            P(("dp", "tensor"), None),
            P(("dp", "tensor"), None, None),
            P(("dp", "tensor")),
            P(("dp", "tensor")),
            P(None, "dp", "tensor"),
            P(None, ("tensor", "dp")),
            P("tensor", "dp"),
            P(("dp", "tensor")),
            P(("dp", "tensor")),
            P(("dp", "tensor")),
            P("dp", "tensor"),
            P(("tensor", "dp")),
            P("tensor", "dp"),
            P(("dp", "tensor")),
            P(None, ("dp", "tensor")),
            P(("dp", "tensor")),
            P(("dp", "tensor")),
            P(("dp", "tensor")),
            P("dp", "tensor"),
            P(("tensor", "dp")),
            P("tensor", "dp"),
            P(("dp", "tensor")),
            P(("dp", "tensor")),
            P(("dp", "tensor"), None),
            P(("dp", "tensor")),
            P(("dp", "tensor")),
        ),
        check_vma=False,
    )
```

```python
from functools import partial

import jax
import jax.numpy as jnp
import numpy as np
from jax import lax
from jax.experimental import pallas as pl
from jax.experimental.pallas import tpu as pltpu
from jax.sharding import PartitionSpec as P

HEAD_DIM = 64
SIDE = 24
KERNEL = 7
IMG_SPAN = 2


vit_eps = 1e-05
map_eps = 1e-06
masked_score = -1e30
ROOT_HALF = 0.7071067811865476
NORMAL_PEAK = 0.3989422804014327


def contract_rows(left_side, right_side):
    return lax.dot_general(
        left_side, right_side, (((0,), (0,)), ((), ())), preferred_element_type=jnp.float32
    )


def contract_cols(left_side, right_side):
    return lax.dot_general(
        left_side, right_side, (((1,), (1,)), ((), ())), preferred_element_type=jnp.float32
    )


def bits_of(count):
    return count.bit_length() - 1


class Halving:
    def __init__(self, source, landings, send, recv, top_first):
        self.count = lax.axis_size("dp")
        self.d, self.t = lax.axis_index("dp"), lax.axis_index("tensor")
        self.source, self.landings = source, landings
        self.send, self.recv, self.top_first = send, recv, top_first
        self.stages = bits_of(self.count)

    def plan(self, stage):
        here = self.source if stage == 0 else self.landings[stage - 1]
        half = self.count >> (stage + 1)
        top = self.top_first and stage > 0
        bit = self.stages - stage if top else stage
        own = lax.rem(self.d // (1 << bit), 2)
        partner = self.d + (1 - 2 * own) * (1 << bit)
        base = self.count - 2 * half

        def place(i, value):
            return value * half + i if top else 2 * i + value

        def copy(i):
            return pltpu.make_async_remote_copy(
                here.at[place(i, 1 - own)], self.landings[stage].at[i],
                self.send.at[base + i], self.recv.at[base + i],
                device_id=(partner, self.t), device_id_type=MESH_ID,
            )

        return here, half, own, place, copy

    def start(self, stage):
        here, half, own, place, copy = self.plan(stage)

        def body(i, carry):
            copy(i).start()
            return carry

        lax.fori_loop(0, half, body, 0)

    def finish(self, stage, out=None):
        here, half, own, place, copy = self.plan(stage)
        landing = self.landings[stage]
        rows = landing.shape[1]

        def body(i, carry):
            copy(i).wait()
            total = here[place(i, own)].astype(jnp.float32) + landing[i].astype(jnp.float32)
            if out is None:
                landing[i] = total.astype(jnp.bfloat16)
            else:
                out[...] = total
            return carry

        lax.fori_loop(0, half, body, 0)


def halving_scratch(count, rows, cols):
    landings = []
    half = count // 2
    while half >= 1:
        landings.append(pltpu.VMEM((half, rows, cols), jnp.bfloat16))
        half //= 2
    return landings + [pltpu.SemaphoreType.DMA((count - 1,))] * 2


class Ring:
    def __init__(self):
        self.count = lax.axis_size("tensor")
        self.d, self.t = lax.axis_index("dp"), lax.axis_index("tensor")

    def at(self, k):
        return lax.rem(self.t + k, self.count)

    def share_copy(self, buffer, sems, k, source):
        return pltpu.make_async_remote_copy(
            buffer.at[source], buffer.at[source], sems.at[0, k], sems.at[1, source],
            device_id=(self.d, self.at(k)), device_id_type=MESH_ID,
        )

    def share_start(self, buffer, sems):
        for k in range(1, self.count):
            self.share_copy(buffer, sems, k, self.t).start()

    def share_finish(self, buffer, sems):
        for k in range(1, self.count):
            self.share_copy(buffer, sems, k, self.t).wait_send()
        for k in range(1, self.count):
            self.share_copy(buffer, sems, k, self.at(k)).wait_recv()

    def give_copy(self, parts, landing, sems, k, slot, part):
        return pltpu.make_async_remote_copy(
            parts.at[part], landing.at[slot], sems.at[0, k], sems.at[1, slot],
            device_id=(self.d, self.at(k)), device_id_type=MESH_ID,
        )

    def give_start(self, parts, landing, sems):
        for k in range(1, self.count):
            self.give_copy(parts, landing, sems, k, self.t, self.at(k)).start()

    def give_finish(self, parts, landing, sems):
        for k in range(1, self.count):
            self.give_copy(parts, landing, sems, k, self.t, self.at(k)).wait_send()
        for k in range(1, self.count):
            self.give_copy(parts, landing, sems, k, self.at(k), self.at(k)).wait_recv()

    def total(self, parts, landing):
        value = parts[self.t].astype(jnp.float32)
        for k in range(1, self.count):
            value = value + landing[self.at(k)].astype(jnp.float32)
        return value


def norm_parts(values, epsilon):
    centered = values - jnp.mean(values, axis=-1, keepdims=True)
    variance = jnp.mean(centered * centered, axis=-1, keepdims=True)
    scale = lax.rsqrt(variance + epsilon)
    return centered * scale, scale


def norm_pull(grad, xhat, scale, gain):
    scaled = grad * gain
    return scale * (
        scaled
        - jnp.mean(scaled, axis=-1, keepdims=True)
        - xhat * jnp.mean(scaled * xhat, axis=-1, keepdims=True)
    )


def row_sum(values):
    return jnp.sum(values, axis=0, keepdims=True)


def flat_low(buffer):
    count, rows, cols = buffer.shape
    return buffer[...].astype(jnp.float32).reshape(count * rows, cols).astype(jnp.bfloat16)


def fill_parts(parts, value):
    count, rows, _ = parts.shape
    for j in range(count):
        parts[j] = value[j * rows : (j + 1) * rows].astype(jnp.bfloat16)


MESH_ID = pl.DeviceIdType.MESH
VMEM_SPEC = pl.BlockSpec(memory_space=pltpu.VMEM)
LANES = 128
SUB = 8
VMEM_BYTES = 60 * 1024 * 1024


def kernel_params(collective_id=None):
    if collective_id is None:
        return pltpu.CompilerParams(vmem_limit_bytes=VMEM_BYTES)
    return pltpu.CompilerParams(
        vmem_limit_bytes=VMEM_BYTES, collective_id=collective_id, has_side_effects=True
    )


def halo_route():
    count = lax.axis_size("tensor")
    d, t = lax.axis_index("dp"), lax.axis_index("tensor")
    odd = lax.rem(d, IMG_SPAN)
    up = (d + (t + 1) // count, lax.rem(t + 1, count))
    down = (d - 1 + (t + count - 1) // count, lax.rem(t + count - 1, count))
    up_here = (t + 1) // count + odd < 2
    down_here = t + odd > 0
    return up, down, up_here, down_here


def seam_here():
    count = lax.axis_size("tensor")
    d, t = lax.axis_index("dp"), lax.axis_index("tensor")
    odd = lax.rem(d, IMG_SPAN)
    at_last = (t + 1) // count
    at_first = 1 - (t + count - 1) // count
    return at_last * (1 - odd) + at_first * odd


def meet(data_peers):
    count = lax.axis_size("tensor")
    d, t = lax.axis_index("dp"), lax.axis_index("tensor")
    odd = lax.rem(d, IMG_SPAN)
    barrier = pltpu.get_barrier_semaphore()
    for k in range(1, count):
        pl.semaphore_signal(
            barrier, inc=1, device_id=(d, lax.rem(t + k, count)), device_id_type=MESH_ID
        )
    for peer in data_peers:
        pl.semaphore_signal(barrier, inc=1, device_id=(peer, t), device_id_type=MESH_ID)
    seam = seam_here()

    @pl.when(seam > 0)
    def _():
        pl.semaphore_signal(
            barrier, inc=1, device_id=(d + 1 - 2 * odd, count - 1 - t), device_id_type=MESH_ID
        )

    pl.semaphore_wait(barrier, count - 1 + len(data_peers) + seam)


def as_row(ref):
    return ref[...].reshape(1, ref.shape[0])


def halo_copies(route, first_rows, last_rows, low_ref, high_ref, send_sem, recv_sem):
    up, down, up_here, down_here = route
    to_up = pltpu.make_async_remote_copy(
        last_rows, low_ref, send_sem.at[0], recv_sem.at[0], device_id=up, device_id_type=MESH_ID
    )
    to_down = pltpu.make_async_remote_copy(
        first_rows, high_ref, send_sem.at[1], recv_sem.at[1], device_id=down, device_id_type=MESH_ID
    )
    return to_up, to_down


def halo_start(route, copies):
    @pl.when(route[2])
    def _():
        copies[0].start()

    @pl.when(route[3])
    def _():
        copies[1].start()


def halo_finish(route, copies):
    @pl.when(route[2])
    def _():
        copies[0].wait_send()
        copies[1].wait_recv()

    @pl.when(route[3])
    def _():
        copies[1].wait_send()
        copies[0].wait_recv()


def halo_store(route, extended, low_ref, high_ref, rows, cols, rim):
    @pl.when(route[3])
    def _():
        extended[0:rim, SUB : SUB + cols, :] = low_ref[...].astype(jnp.float32)

    @pl.when(route[2])
    def _():
        extended[rim + rows : 2 * rim + rows, SUB : SUB + cols, :] = high_ref[...].astype(
            jnp.float32
        )


def conv_rows(extended, taps_ref, rows, cols, channels, flipped, emit):
    span = KERNEL * KERNEL - 1

    def lane_block(block, carry):
        lanes = pl.ds(pl.multiple_of(block * LANES, LANES), LANES)
        for tile in range(cols // SUB):
            sums = [None] * rows
            for e in range(KERNEL):
                first = SUB * tile + SUB - KERNEL // 2 + e
                cells = [
                    extended[r, first : first + SUB, lanes] for r in range(rows + KERNEL - 1)
                ]
                for a in range(KERNEL):
                    index = a * KERNEL + e
                    tap = taps_ref[pl.ds(span - index if flipped else index, 1), lanes]
                    for i in range(rows):
                        term = cells[i + a] * tap
                        sums[i] = term if sums[i] is None else sums[i] + term
            for i in range(rows):
                emit(i, tile, lanes, sums[i])
        return carry

    lax.fori_loop(0, channels // LANES, lane_block, 0)


def conv_forward_kernel(
    own_ref, taps_ref, bias_1d, gain_1d, shift_1d, pool_ref, patches_ref, upstream_ref,
    ln1_gain, ln1_bias,
    normed_ref, conv_ref, low_ref, high_ref, attn_ref, given_ref, mean_ref,
    extended, vectors, attn_all, given_all, send_sem, recv_sem, attn_sems, given_sems,
):
    rows, cols, channels = own_ref.shape
    rim = KERNEL // 2
    route = halo_route()
    ring = Ring()
    meet(())
    copies = halo_copies(
        route, own_ref.at[pl.ds(0, rim)], own_ref.at[pl.ds(rows - rim, rim)],
        low_ref, high_ref, send_sem, recv_sem,
    )
    halo_start(route, copies)
    given_all[ring.t] = upstream_ref[...]
    xhat, _ = norm_parts(patches_ref[...].astype(jnp.float32), vit_eps)
    attn_all[ring.t] = (xhat * as_row(ln1_gain) + as_row(ln1_bias)).astype(jnp.bfloat16)
    vectors[0:1, :] = as_row(bias_1d)
    vectors[1:2, :] = as_row(gain_1d)
    vectors[2:3, :] = as_row(shift_1d)
    bias_ref, gain_ref, shift_ref = vectors.at[0:1], vectors.at[1:2], vectors.at[2:3]
    quarter = pool_ref.shape[0]
    for pair in range(rows // 2):
        mean_ref[pair * quarter : (pair + 1) * quarter, :] = jnp.dot(
            pool_ref[...],
            own_ref[2 * pair : 2 * pair + 2].reshape(2 * cols, channels),
            preferred_element_type=jnp.float32,
        )
    for edge in (0, SUB + cols):
        extended[:, edge : edge + SUB, :] = jnp.zeros(
            (rows + 2 * rim, SUB, channels), jnp.float32
        )
    extended[rim : rim + rows, SUB : SUB + cols, :] = own_ref[...].astype(jnp.float32)
    halo_finish(route, copies)
    ring.share_start(given_all, given_sems)
    ring.share_start(attn_all, attn_sems)

    @pl.when(jnp.logical_not(route[3]))
    def _():
        low_ref[...] = jnp.zeros_like(low_ref)
        extended[0:rim, SUB : SUB + cols, :] = jnp.zeros((rim, cols, channels), jnp.float32)

    @pl.when(jnp.logical_not(route[2]))
    def _():
        high_ref[...] = jnp.zeros_like(high_ref)
        extended[rim + rows : 2 * rim + rows, SUB : SUB + cols, :] = jnp.zeros(
            (rim, cols, channels), jnp.float32
        )

    halo_store(route, extended, low_ref, high_ref, rows, cols, rim)

    def emit(i, tile, lanes, value):
        first = i * cols + tile * SUB
        conv_ref[first : first + SUB, lanes] = value + bias_ref[:, lanes]

    conv_rows(extended, taps_ref, rows, cols, channels, False, emit)
    step = 2 * SUB

    def norm_block(block, carry):
        here = pl.ds(pl.multiple_of(block * step, step), step)
        values = conv_ref[here, :]
        centered = values - jnp.mean(values, axis=-1, keepdims=True)
        variance = jnp.mean(centered * centered, axis=-1, keepdims=True)
        scaled = centered * lax.rsqrt(variance + map_eps) * gain_ref[...] + shift_ref[...]
        normed_ref[here, :] = scaled.astype(jnp.bfloat16)
        return carry

    lax.fori_loop(0, rows * cols // step, norm_block, 0)
    ring.share_finish(given_all, given_sems)
    given_ref[...] = flat_low(given_all)
    ring.share_finish(attn_all, attn_sems)
    attn_ref[...] = flat_low(attn_all)


def pool_matrix(map_cols):
    chunk = 2 * map_cols
    cell_patch = (np.arange(chunk) % map_cols) // 2
    return np.arange(chunk // 4)[:, None] == cell_patch[None, :]


def conv_forward(hires, taps, bias, gain, shift, patches, upstream, ln1_gain, ln1_bias):
    rows, cols, channels = hires.shape
    rim = KERNEL // 2
    cells = rows * cols
    count = lax.axis_size("tensor")
    patch_rows, model = patches.shape
    pool = jnp.asarray(np.where(pool_matrix(cols), 0.25, 0.0), jnp.bfloat16)
    flat = jax.ShapeDtypeStruct((count * patch_rows, model), jnp.bfloat16)
    return pl.pallas_call(
        conv_forward_kernel,
        out_shape=(
            jax.ShapeDtypeStruct((cells, channels), jnp.bfloat16),
            jax.ShapeDtypeStruct((cells, channels), jnp.float32),
            jax.ShapeDtypeStruct((rim, cols, channels), jnp.bfloat16),
            jax.ShapeDtypeStruct((rim, cols, channels), jnp.bfloat16),
            flat,
            flat,
            jax.ShapeDtypeStruct((patch_rows, channels), jnp.float32),
        ),
        in_specs=[VMEM_SPEC] * 10,
        out_specs=(VMEM_SPEC,) * 7,
        scratch_shapes=[
            pltpu.VMEM((rows + 2 * rim, cols + 2 * SUB, channels), jnp.float32),
            pltpu.VMEM((SUB, channels), jnp.float32),
            pltpu.VMEM((count, patch_rows, model), jnp.bfloat16),
            pltpu.VMEM((count, patch_rows, model), jnp.bfloat16),
            pltpu.SemaphoreType.DMA((2,)),
            pltpu.SemaphoreType.DMA((2,)),
            pltpu.SemaphoreType.DMA((2, count)),
            pltpu.SemaphoreType.DMA((2, count)),
        ],
        compiler_params=kernel_params(0),
        name="conv_forward",
    )(hires, taps, bias, gain, shift, pool, patches, upstream, ln1_gain, ln1_bias)


def conv_backward_kernel(
    dy_ref, conv_ref, gain_1d, own_ref, low_ref, high_ref, taps_ref, pooled_grad_ref, spread_ref,
    sums_model, sums_map, sums_heads, sums_ff, pw1_sums, job_sources,
    out_ref, ring_total_ref, data_total_ref, job_outs,
    extended, grads, first_low, last_low, low_in, high_in, sums_ref, tap_grad_ref, gain_ref,
    packed, landed, ring_all, send_sem, recv_sem, pack_send, pack_recv, ring_sems, job_scratch,
):
    rows, cols, channels = own_ref.shape
    rim = KERNEL // 2
    route = halo_route()
    ring = Ring()
    d, t = ring.d, ring.t
    data = lax.axis_size("dp")
    stages = bits_of(data)
    meet([lax.rem(d + k, data) for k in range(1, data)])
    jobs = [
        Halving(source, scratch[:stages], scratch[stages], scratch[stages + 1], top)
        for source, scratch, top in zip(job_sources, job_scratch, JOB_ORDERS)
    ]
    for job in jobs:
        job.start(0)
    gain_ref[0:1, :] = as_row(gain_1d)
    sums_ref[...] = jnp.zeros_like(sums_ref)
    step = 2 * SUB
    per_row = cols // step

    def grad_block(block, carry):
        here = pl.ds(pl.multiple_of(block * step, step), step)
        values = conv_ref[here, :]
        dy = dy_ref[here, :]
        centered = values - jnp.mean(values, axis=-1, keepdims=True)
        variance = jnp.mean(centered * centered, axis=-1, keepdims=True)
        scale = lax.rsqrt(variance + map_eps)
        xhat = centered * scale
        scaled = dy * gain_ref[0:1, :]
        grad = scale * (
            scaled
            - jnp.mean(scaled, axis=-1, keepdims=True)
            - xhat * jnp.mean(scaled * xhat, axis=-1, keepdims=True)
        )
        row = block // per_row
        col = SUB + lax.rem(block, per_row) * step
        for half in range(2):
            grads[rim + row, pl.ds(pl.multiple_of(col + half * SUB, SUB), SUB), :] = grad[
                half * SUB : (half + 1) * SUB
            ]
        sums_ref[0:1, :] += jnp.sum(dy * xhat, axis=0, keepdims=True)
        sums_ref[1:2, :] += jnp.sum(dy, axis=0, keepdims=True)
        sums_ref[2:3, :] += jnp.sum(grad, axis=0, keepdims=True)
        return carry

    lax.fori_loop(0, rows * per_row, grad_block, 0)
    first_low[...] = grads[rim : 2 * rim, SUB : SUB + cols, :].astype(jnp.bfloat16)
    last_low[...] = grads[rows : rows + rim, SUB : SUB + cols, :].astype(jnp.bfloat16)
    copies = halo_copies(route, first_low, last_low, low_in, high_in, send_sem, recv_sem)
    halo_start(route, copies)
    for job in jobs:
        job.finish(0)
        job.start(1)
    for edge in (0, SUB + cols):
        zero = jnp.zeros((rows + 2 * rim, SUB, channels), jnp.float32)
        extended[:, edge : edge + SUB, :] = zero
        grads[:, edge : edge + SUB, :] = zero
    extended[0:rim, SUB : SUB + cols, :] = low_ref[...].astype(jnp.float32)
    extended[rim : rim + rows, SUB : SUB + cols, :] = own_ref[...].astype(jnp.float32)
    extended[rim + rows : 2 * rim + rows, SUB : SUB + cols, :] = high_ref[...].astype(jnp.float32)

    def tap_block(block, carry):
        lanes = pl.ds(pl.multiple_of(block * LANES, LANES), LANES)
        for e in range(KERNEL):
            sums = [None] * KERNEL
            for tile in range(cols // SUB):
                first = SUB * tile + SUB - rim + e
                cells = [
                    extended[r, first : first + SUB, lanes] for r in range(rows + KERNEL - 1)
                ]
                given = [
                    grads[rim + i, SUB * tile + SUB : SUB * tile + 2 * SUB, lanes]
                    for i in range(rows)
                ]
                for a in range(KERNEL):
                    for i in range(rows):
                        term = cells[i + a] * given[i]
                        sums[a] = term if sums[a] is None else sums[a] + term
            for a in range(KERNEL):
                tap_grad_ref[pl.ds(a * KERNEL + e, 1), lanes] = jnp.sum(
                    sums[a], axis=0, keepdims=True
                )
        return carry

    lax.fori_loop(0, channels // LANES, tap_block, 0)
    taps = KERNEL * KERNEL
    tap_grad_ref[taps : taps + 3, :] = sums_ref[0:3, :]
    tap_grad_ref[taps + 3 : taps + 5, :] = sums_map[0:2, :]
    tap_grad_ref[taps + 5 : taps + 6, :] = pw1_sums[...]
    tap_grad_ref[taps + 6 : taps + 7, :] = jnp.zeros((1, channels), jnp.float32)
    tall = tap_grad_ref.shape[0]
    zero = jnp.zeros((SUB, LANES), jnp.float32)
    for m in range(data):
        first = window_start(m, channels, data)
        packed[m, 0:tall, :] = tap_grad_ref[:, first : first + 2 * LANES]
        for lane, (row, source) in enumerate(
            ((tall, sums_model), (tall, sums_ff), (tall + SUB, sums_heads))
        ):
            first = lane_start(m, source.shape[1], data)
            side = LANES * (lane % 2)
            packed[m, row : row + SUB, side : side + LANES] = source[:, first : first + LANES]
        packed[m, tall + SUB : tall + 2 * SUB, LANES : 2 * LANES] = zero

    def pack_copy(k, part, slot):
        return pltpu.make_async_remote_copy(
            packed.at[part], landed.at[slot], pack_send.at[k], pack_recv.at[slot],
            device_id=(lax.rem(d + k, data), t), device_id_type=MESH_ID,
        )

    def pack_start(k, carry):
        pack_copy(k, lax.rem(d + k, data), d).start()
        return carry

    lax.fori_loop(1, data, pack_start, 0)
    for stage in range(1, stages - 1):
        for job in jobs:
            job.finish(stage)
            job.start(stage + 1)
    for pair in range(rows // 2):
        half = cols // 2
        wide = jnp.dot(
            spread_ref[...],
            pooled_grad_ref[pair * half : (pair + 1) * half, :],
            precision=lax.Precision.HIGHEST,
            preferred_element_type=jnp.float32,
        )
        for i in range(2):
            out_ref[2 * pair + i] = wide
    halo_finish(route, copies)

    @pl.when(jnp.logical_not(route[3]))
    def _():
        grads[0:rim, SUB : SUB + cols, :] = jnp.zeros((rim, cols, channels), jnp.float32)

    @pl.when(jnp.logical_not(route[2]))
    def _():
        grads[rim + rows : 2 * rim + rows, SUB : SUB + cols, :] = jnp.zeros(
            (rim, cols, channels), jnp.float32
        )

    halo_store(route, grads, low_in, high_in, rows, cols, rim)

    def emit(i, tile, lanes, value):
        out_ref[i, tile * SUB : (tile + 1) * SUB, lanes] += value

    conv_rows(grads, taps_ref, rows, cols, channels, True, emit)
    data_total_ref[...] = packed[d]

    def pack_finish(k, carry):
        pack_copy(k, lax.rem(d + k, data), d).wait_send()
        slot = lax.rem(d + k, data)
        pack_copy(k, slot, slot).wait_recv()
        data_total_ref[...] += landed[slot]
        return carry

    lax.fori_loop(1, data, pack_finish, 0)
    ring_all[t] = data_total_ref[...]
    ring.share_start(ring_all, ring_sems)
    for job, out in zip(jobs, job_outs):
        job.finish(stages - 1, out)
    ring.share_finish(ring_all, ring_sems)
    total = ring_all[0]
    for j in range(1, ring.count):
        total = total + ring_all[j]
    ring_total_ref[...] = total


def window_start(m, width, data):
    return min(m * (width // data) // LANES, width // LANES - 2) * LANES


def lane_start(m, width, data):
    return m * (width // data) // LANES * LANES


JOB_ORDERS = (False, True, False, True, True)


def conv_backward(
    normed_grad, conv, gain, hires, low_rim, high_rim, taps, grad_pooled,
    sums_model, sums_map, sums_heads, sums_ff, pw1_sums, weight_grads,
):
    data = lax.axis_size("dp")
    count = lax.axis_size("tensor")
    sources = [g.reshape(data, g.shape[0] // data, g.shape[1]) for g in weight_grads]
    n_jobs = len(sources)
    rows, cols, channels = hires.shape
    rim = KERNEL // 2
    place = np.arange(cols)[:, None] // 2 == np.arange(cols // 2)[None, :]
    spread = jnp.asarray(np.where(place, 0.25, 0.0), jnp.float32)
    wide = pltpu.VMEM((rows + 2 * rim, cols + 2 * SUB, channels), jnp.float32)
    rim_low = pltpu.VMEM((rim, cols, channels), jnp.bfloat16)
    tall = (KERNEL * KERNEL + SUB - 1) // SUB * SUB
    block = (tall + 2 * SUB, 2 * LANES)
    block_out = jax.ShapeDtypeStruct(block, jnp.float32)
    per_job = bits_of(data) + 2
    fixed = 17

    def kernel(*refs):
        ins, outs = refs[: 14 + n_jobs], refs[14 + n_jobs : 17 + 2 * n_jobs]
        scratch = refs[17 + 2 * n_jobs :]
        jobs = scratch[fixed:]
        conv_backward_kernel(
            *ins[:14], ins[14:], *outs[:3], outs[3:], *scratch[:fixed],
            [jobs[i * per_job : (i + 1) * per_job] for i in range(n_jobs)],
        )

    job_scratch = []
    for source in sources:
        job_scratch += halving_scratch(*source.shape)
    return pl.pallas_call(
        kernel,
        out_shape=(jax.ShapeDtypeStruct((rows, cols, channels), jnp.float32), block_out, block_out)
        + tuple(jax.ShapeDtypeStruct(source.shape[1:], jnp.float32) for source in sources),
        in_specs=[VMEM_SPEC] * (14 + n_jobs),
        out_specs=(VMEM_SPEC,) * (3 + n_jobs),
        scratch_shapes=[
            wide, wide, rim_low, rim_low, rim_low, rim_low,
            pltpu.VMEM((SUB, channels), jnp.float32),
            pltpu.VMEM((tall, channels), jnp.float32),
            pltpu.VMEM((SUB, channels), jnp.float32),
            pltpu.VMEM((data,) + block, jnp.float32),
            pltpu.VMEM((data,) + block, jnp.float32),
            pltpu.VMEM((count,) + block, jnp.float32),
            pltpu.SemaphoreType.DMA((2,)),
            pltpu.SemaphoreType.DMA((2,)),
            pltpu.SemaphoreType.DMA((data,)),
            pltpu.SemaphoreType.DMA((data,)),
            pltpu.SemaphoreType.DMA((2, count)),
        ]
        + job_scratch,
        compiler_params=kernel_params(1),
        name="conv_backward",
    )(
        normed_grad, conv, gain, hires, low_rim, high_rim, taps, grad_pooled, spread,
        sums_model, sums_map, sums_heads, sums_ff, pw1_sums, *sources,
    )


def small_kernel(shapes, ring_total, data_total, *outs):
    channels, model, units, width, tall = shapes
    d, t = lax.axis_index("dp"), lax.axis_index("tensor")
    data, count = lax.axis_size("dp"), lax.axis_size("tensor")
    taps = KERNEL * KERNEL

    def turned(value, first):
        size = value.shape[1]
        return pltpu.roll(value, lax.rem(size - first, size), 1)

    here = channels // (data * count)
    start = jnp.minimum(d * (channels // data) // LANES, channels // LANES - 2) * LANES
    first = d * (channels // data) - start
    wide = turned(ring_total[0:tall, :], first + t * here)
    outs[0][...] = wide[0:taps, 0:here]
    for i in range(5):
        outs[1 + i][...] = wide[taps + i, 0:here]
    step = model // data
    first = d * step - d * step // LANES * LANES + t * (step // count)
    narrow = turned(ring_total[tall : tall + SUB, 0:LANES], first)
    for i in range(8):
        outs[6 + i][...] = narrow[i, 0 : step // count]
    step = outs[14].shape[0]
    first = d * step - jnp.minimum(d * step // LANES, channels // LANES - 2) * LANES
    outs[14][...] = turned(data_total[tall - SUB : tall, :], first)[taps + 5 - tall + SUB, 0:step]
    step = units // data
    first = d * step - d * step // LANES * LANES
    outs[15][...] = turned(data_total[tall : tall + SUB, LANES : 2 * LANES], first)[0, 0:step]
    step = width // data
    first = d * step - d * step // LANES * LANES
    outs[16][...] = turned(data_total[tall + SUB : tall + 2 * SUB, 0:LANES], first)[0:2, 0:step]


def small_outputs(ring_total, data_total, channels, model, units, width):
    data, count = lax.axis_size("dp"), lax.axis_size("tensor")
    taps = KERNEL * KERNEL
    tall = ring_total.shape[0] - 2 * SUB
    shapes = (
        [(taps, channels // (data * count))]
        + [(channels // (data * count),)] * 5
        + [(model // (data * count),)] * 8
        + [(channels // data,), (units // data,), (2, width // data)]
    )
    return pl.pallas_call(
        partial(small_kernel, (channels, model, units, width, tall)),
        out_shape=tuple(jax.ShapeDtypeStruct(shape, jnp.float32) for shape in shapes),
        in_specs=[VMEM_SPEC] * 2,
        out_specs=(VMEM_SPEC,) * len(shapes),
        compiler_params=kernel_params(),
        name="small_outputs",
    )(ring_total, data_total)


def mirror(index, low_half, last):
    return index + (1 - low_half) * (last - 2 * index)


def map_kernel(
    own_ref, w1_ref, b1_1d, w2_ref, given_ref, wadapt_ref, adapt_gain, layer_scale,
    pool_ref, spread_ref,
    grad_ref, branch_ref, gw1_ref, gw2_ref, gb1_ref, pooled_grad_ref,
    b1_ref, branch_grad_ref, pooled_grads, rows_all, pre_grads, stash, from_below, from_above, pooled, hidden_grads, low_pre,
    ag_recv, ag_up, ag_down, up_recv, up_send, down_recv, down_send,
):
    count, cells, channels = rows_all.shape
    hidden = w1_ref.shape[1]
    parts = ag_recv.shape[1]
    chunk = cells // parts
    quarter = chunk // 4
    last = count - 1
    d, t = lax.axis_index("dp"), lax.axis_index("tensor")
    low_half = 1 - t // 2
    place = mirror(t, low_half, last)
    above, below = (d, t + 1), (d, t - 1)
    barrier = pltpu.get_barrier_semaphore()

    @pl.when(t < last)
    def _():
        pl.semaphore_signal(barrier, inc=1, device_id=above, device_id_type=MESH_ID)

    @pl.when(t > 0)
    def _():
        pl.semaphore_signal(barrier, inc=1, device_id=below, device_id_type=MESH_ID)

    pl.semaphore_wait(barrier, 1 + place)

    def rows_of(p):
        return pl.ds(pl.multiple_of(p * chunk, chunk), chunk)

    def gather_copy(j, p, target, send):
        return pltpu.make_async_remote_copy(
            rows_all.at[j, rows_of(p)], rows_all.at[j, rows_of(p)],
            send.at[j, p], ag_recv.at[j, p], device_id=target, device_id_type=MESH_ID,
        )

    def sum_copy(j, p, going_up):
        landing = from_below if going_up else from_above
        return pltpu.make_async_remote_copy(
            stash.at[j, rows_of(p)], landing.at[j, rows_of(p)],
            (up_send if going_up else down_send).at[j, p],
            (up_recv if going_up else down_recv).at[j, p],
            device_id=above if going_up else below, device_id_type=MESH_ID,
        )

    rows_all[t] = own_ref[...]
    for p in range(parts):
        @pl.when(t < last)
        def _():
            gather_copy(t, p, above, ag_up).start()

        @pl.when(t > 0)
        def _():
            gather_copy(t, p, below, ag_down).start()

    b1_ref[0:1, :] = as_row(b1_1d)
    adapt_grad = (given_ref[...].astype(jnp.float32) * as_row(adapt_gain)).astype(jnp.bfloat16)
    pooled_grad = contract_cols(adapt_grad, wadapt_ref[...])
    pooled_grads[...] = pooled_grad
    branch_grad_ref[...] = (as_row(layer_scale) * (pooled_grad * 0.25)).astype(jnp.bfloat16)
    own_rows = pooled_grad_ref.shape[0]
    pooled_grad_ref[...] = pooled_grads[pl.ds(pl.multiple_of(t * own_rows, SUB), own_rows), :]
    hidden_grads[...] = contract_cols(branch_grad_ref[...], w2_ref[...])
    gb1_ref[...] = jnp.zeros_like(gb1_ref)
    block = 256

    def one_chunk(q, carry):
        n, p = q // parts, lax.rem(q, parts)
        near = n + place * (1 - 2 * n) * (1 - n // 2)
        j = mirror(near, low_half, last)

        @pl.when(n > 0)
        def _():
            gather_copy(j, p, above, ag_up).wait_recv()

            @pl.when(jnp.logical_and(j < t, t < last))
            def _():
                gather_copy(j, p, above, ag_up).start()

            @pl.when(jnp.logical_and(j > t, t > 0))
            def _():
                gather_copy(j, p, below, ag_down).start()

        given = rows_all[j, rows_of(p), :]
        small = pl.ds(pl.multiple_of((j * parts + p) * quarter, SUB), quarter)
        for first in range(0, hidden, block):
            here = slice(first, first + block)
            pre = (
                jnp.dot(given, w1_ref[:, here], preferred_element_type=jnp.float32)
                + b1_ref[0:1, here]
            )
            wide_grad = hidden_grads[small, here]
            high = wide_grad.astype(jnp.bfloat16)
            rest = (wide_grad - high.astype(jnp.float32)).astype(jnp.bfloat16)
            spread_grad = jnp.dot(
                spread_ref[...], high, preferred_element_type=jnp.float32
            ) + jnp.dot(spread_ref[...], rest, preferred_element_type=jnp.float32)
            below_curve = 0.5 + 0.5 * lax.erf(pre * ROOT_HALF)
            slope = below_curve + pre * jnp.exp(-0.5 * pre * pre) * NORMAL_PEAK
            active = (pre * below_curve).astype(jnp.bfloat16)
            pooled[small, here] = jnp.dot(
                pool_ref[...], active, preferred_element_type=jnp.float32
            )
            pre_low = (spread_grad * slope).astype(jnp.bfloat16)
            gb1_ref[:, here] += jnp.sum(pre_low.astype(jnp.float32), axis=0, keepdims=True)
            low_pre[:, here] = pre_low
        pre_all = low_pre[...]
        pre_grads[j, rows_of(p), :] = pre_all
        partial_grad = contract_cols(pre_all, w1_ref[...])

        @pl.when(n == 0)
        def _():
            grad_ref[rows_of(p), :] = partial_grad

        @pl.when(n > 0)
        def _():
            stash[j, rows_of(p), :] = partial_grad.astype(jnp.bfloat16)

            @pl.when(t == 0)
            def _():
                sum_copy(j, p, True).start()

            @pl.when(t == last)
            def _():
                sum_copy(j, p, False).start()

        return carry

    lax.fori_loop(0, count * parts, one_chunk, 0)

    def pass_on(j, p, going_up):
        copy = sum_copy(j, p, going_up)
        copy.wait_recv()
        landing = from_below if going_up else from_above
        stash[j, rows_of(p), :] = (
            stash[j, rows_of(p), :].astype(jnp.float32)
            + landing[j, rows_of(p), :].astype(jnp.float32)
        ).astype(jnp.bfloat16)
        copy.start()

    middle = place == 1

    def forward_up(s, carry):
        j, p = t + 1 + s // parts, lax.rem(s, parts)
        pass_on(j, p, True)
        return carry

    def forward_down(s, carry):
        j, p = t - 1 - s // parts, lax.rem(s, parts)
        pass_on(j, p, False)
        return carry

    @pl.when(jnp.logical_and(middle, low_half == 1))
    def _():
        lax.fori_loop(0, (count - 2) * parts, forward_up, 0)
        lax.fori_loop(0, parts, forward_down, 0)

    @pl.when(jnp.logical_and(middle, low_half == 0))
    def _():
        lax.fori_loop(0, (count - 2) * parts, forward_down, 0)
        lax.fori_loop(0, parts, forward_up, 0)

    wide = 384
    rows_flat = rows_all.reshape(count * cells, channels)
    pre_flat = pre_grads.reshape(count * cells, hidden)
    for first in range(0, channels, wide):
        gw1_ref[first : first + wide, :] = contract_rows(
            rows_flat[:, first : first + wide], pre_flat[...]
        ).astype(jnp.bfloat16)
    pooled_low = pooled[...].astype(jnp.bfloat16)
    branch_ref[...] = jnp.dot(
        pooled_low, w2_ref[...], preferred_element_type=jnp.float32
    ).astype(jnp.bfloat16)
    for first in range(0, channels, wide):
        gw2_ref[first : first + wide, :] = (
            4.0 * contract_rows(branch_grad_ref[:, first : first + wide], pooled_low)
        ).astype(jnp.bfloat16)

    def finish(p, carry):
        @pl.when(t > 0)
        def _():
            sum_copy(t, p, True).wait_recv()
            grad_ref[rows_of(p), :] += from_below[t, rows_of(p), :].astype(jnp.float32)

        @pl.when(t < last)
        def _():
            sum_copy(t, p, False).wait_recv()
            grad_ref[rows_of(p), :] += from_above[t, rows_of(p), :].astype(jnp.float32)

        return carry

    lax.fori_loop(0, parts, finish, 0)

    def drain(q, carry):
        j, p = q // parts, lax.rem(q, parts)

        @pl.when(jnp.logical_and(j <= t, t < last))
        def _():
            gather_copy(j, p, above, ag_up).wait_send()

        @pl.when(jnp.logical_and(j >= t, t > 0))
        def _():
            gather_copy(j, p, below, ag_down).wait_send()

        @pl.when(j > t)
        def _():
            sum_copy(j, p, True).wait_send()

        @pl.when(j < t)
        def _():
            sum_copy(j, p, False).wait_send()

        return carry

    lax.fori_loop(0, count * parts, drain, 0)


def map_block(
    normed_low, w_pw1, pw1_bias, w_pw2, grad_all, w_adapt, adapt_gain, layer_scale, map_cols
):
    cells, channels = normed_low.shape
    hidden = w_pw1.shape[1]
    count = lax.axis_size("tensor")
    chunk = 2 * map_cols
    parts = cells // chunk
    patches = grad_all.shape[0]
    match = pool_matrix(map_cols)
    pool = jnp.asarray(np.where(match, 0.25, 0.0), jnp.bfloat16)
    spread = jnp.asarray(match.T, jnp.bfloat16)
    low_all = pltpu.VMEM((count, cells, channels), jnp.bfloat16)
    sems = pltpu.SemaphoreType.DMA((count, parts))
    return pl.pallas_call(
        map_kernel,
        out_shape=(
            jax.ShapeDtypeStruct((cells, channels), jnp.float32),
            jax.ShapeDtypeStruct((patches, channels), jnp.bfloat16),
            jax.ShapeDtypeStruct((channels, hidden), jnp.bfloat16),
            jax.ShapeDtypeStruct((channels, hidden), jnp.bfloat16),
            jax.ShapeDtypeStruct((1, hidden), jnp.float32),
            jax.ShapeDtypeStruct((patches // count, channels), jnp.float32),
        ),
        in_specs=[VMEM_SPEC] * 10,
        out_specs=(VMEM_SPEC,) * 6,
        scratch_shapes=[
            pltpu.VMEM((SUB, hidden), jnp.float32),
            pltpu.VMEM((patches, channels), jnp.bfloat16),
            pltpu.VMEM((patches, channels), jnp.float32),
            low_all,
            pltpu.VMEM((count, cells, hidden), jnp.bfloat16),
            low_all,
            low_all,
            low_all,
            pltpu.VMEM((patches, hidden), jnp.float32),
            pltpu.VMEM((patches, hidden), jnp.float32),
            pltpu.VMEM((chunk, hidden), jnp.bfloat16),
        ]
        + [sems] * 7,
        compiler_params=kernel_params(2),
        name="map_block",
    )(
        normed_low, w_pw1, pw1_bias, w_pw2, grad_all, w_adapt, adapt_gain, layer_scale,
        pool, spread,
    )


def vit_kernel(
    patches_ref, attn_ref, given_ref, map_mean_ref, grad_pooled_ref, branch_parts, gw1_ref, gw2_ref,
    ln1_gain, wqkv_ref, qv_bias, wout_ref, out_bias, ln2_gain, ln2_bias,
    wfc1_ref, fc1_bias, wfc2_ref, fc2_bias, wadapt_ref, adapt_bias, adapt_gain,
    pw2_bias, layer_scale, live_ref, pick_ref,
    joined_ref, grad_patches_ref, red1_ref, red2_ref, gfc1_ref, gfc2_ref, gout_ref, gqkv_ref,
    gadapt_ref, sums_model, sums_map, sums_heads, sums_ff,
    keys_all, values_all, kv_own, kv_other, queries, hidden_grad, probs, attended, middle_keep,
    hidden, pre_grad, dqkv, dkv_send, dkv_other, mlp_flat, proj_flat, upstream_keep,
    proj_parts, proj_land, mlp_all, in_parts, in_land, out_parts, out_land, proj_all,
    attn_parts, attn_land, branch_land, pool_parts, pool_land,
    *rest,
):
    ring = Ring()
    count, d, t = ring.count, ring.d, ring.t
    stages = bits_of(lax.axis_size("dp"))
    job_refs = stages + 2
    job1 = Halving(gw1_ref, rest[:stages], rest[stages], rest[stages + 1], False)
    rest = rest[job_refs:]
    job2 = Halving(gw2_ref, rest[:stages], rest[stages], rest[stages + 1], True)
    (
        proj_sems, mlp_sems, in_sems, out_sems, share_sems, attn_sems, branch_sems, pool_sems, pair_sems,
    ) = rest[job_refs:]
    rows, model = patches_ref.shape
    half_rows, width = queries.shape
    heads = width // HEAD_DIM
    scale = HEAD_DIM**-0.5
    partner = d + 1 - 2 * lax.rem(d, 2)

    barrier = pltpu.get_barrier_semaphore()
    for k in range(1, count):
        pl.semaphore_signal(barrier, inc=1, device_id=(d, ring.at(k)), device_id_type=MESH_ID)
    for bit in range(stages):
        step = 1 << bit
        other = d + (1 - 2 * lax.rem(d // step, 2)) * step
        pl.semaphore_signal(barrier, inc=1, device_id=(other, t), device_id_type=MESH_ID)
    pl.semaphore_wait(barrier, count - 1 + stages)

    job1.start(0)
    job2.start(0)
    sums_model[...] = jnp.zeros_like(sums_model)
    sums_map[...] = jnp.zeros_like(sums_map)
    sums_heads[...] = jnp.zeros_like(sums_heads)
    sums_ff[...] = jnp.zeros_like(sums_ff)

    attn = attn_ref[...]
    own_keys = jnp.dot(attn, wqkv_ref[1], preferred_element_type=jnp.float32).astype(jnp.bfloat16)
    own_values = (
        jnp.dot(attn, wqkv_ref[2], preferred_element_type=jnp.float32) + qv_bias[1:2, :]
    ).astype(jnp.bfloat16)
    kv_own[:, 0:width] = own_keys
    kv_own[:, width : 2 * width] = own_values

    def pair_copy(source, target, slot):
        return pltpu.make_async_remote_copy(
            source, target, pair_sems.at[0, slot], pair_sems.at[1, slot],
            device_id=(partner, t), device_id_type=MESH_ID,
        )

    pair_copy(kv_own, kv_other, 0).start()
    ring.give_start(branch_parts, branch_land, branch_sems)
    queries[...] = (
        jnp.dot(attn, wqkv_ref[0], preferred_element_type=jnp.float32) + qv_bias[0:1, :]
    ).astype(jnp.bfloat16)
    keys_all[0:half_rows, :] = own_keys
    values_all[0:half_rows, :] = own_values
    hidden_grad[...] = contract_cols(given_ref[...], wfc2_ref[...])
    pair_copy(kv_own, kv_other, 0).wait()
    keys_all[half_rows : 2 * half_rows, :] = kv_other[:, 0:width]
    values_all[half_rows : 2 * half_rows, :] = kv_other[:, width : 2 * width]
    live = live_ref[...] > 0.5
    for h in range(heads):
        here = slice(h * HEAD_DIM, (h + 1) * HEAD_DIM)
        raw = contract_cols(queries[:, here], keys_all[:, here]) * scale
        scores = jnp.where(live, raw, masked_score)
        grown = jnp.exp(scores - jnp.max(scores, axis=-1, keepdims=True))
        prob = grown * (1.0 / jnp.sum(grown, axis=-1, keepdims=True))
        probs[h] = prob
        attended[:, here] = jnp.dot(
            prob.astype(jnp.bfloat16), values_all[:, here], preferred_element_type=jnp.float32
        ).astype(jnp.bfloat16)
    fill_parts(
        proj_parts, jnp.dot(attended[...], wout_ref[...], preferred_element_type=jnp.float32)
    )
    ring.give_start(proj_parts, proj_land, proj_sems)
    job1.finish(0)
    job1.start(1)
    job2.finish(0)
    job2.start(1)
    ring.give_finish(proj_parts, proj_land, proj_sems)
    inputs = patches_ref[...].astype(jnp.float32)
    middle = inputs + (ring.total(proj_parts, proj_land) + as_row(out_bias))
    middle_keep[...] = middle
    xhat, _ = norm_parts(middle, vit_eps)
    mlp_all[t] = (xhat * as_row(ln2_gain) + as_row(ln2_bias)).astype(jnp.bfloat16)
    ring.share_start(mlp_all, mlp_sems)

    ring.give_finish(branch_parts, branch_land, branch_sems)
    branch = ring.total(branch_parts, branch_land) + as_row(pw2_bias)
    pooled = (map_mean_ref[...] + as_row(layer_scale) * branch).astype(jnp.bfloat16)
    pooled_grad = grad_pooled_ref[...]
    sums_map[0:1, :] = 4.0 * row_sum(
        (as_row(layer_scale) * (pooled_grad * 0.25)).astype(jnp.bfloat16).astype(jnp.float32)
    )
    sums_map[1:2, :] = row_sum(pooled_grad * branch)
    channels = pooled.shape[1]
    per_peer = channels // count
    place = lax.broadcasted_iota(jnp.int32, (channels, per_peer), 0)
    for j in range(count):
        choose = jnp.where(place == pick_ref[j : j + 1, :], 1.0, 0.0).astype(jnp.bfloat16)
        pool_parts[j] = jnp.dot(pooled, choose, preferred_element_type=jnp.float32).astype(
            jnp.bfloat16
        )
    ring.give_start(pool_parts, pool_land, pool_sems)
    adapted = (
        jnp.dot(pooled, wadapt_ref[...], preferred_element_type=jnp.float32) + as_row(adapt_bias)
    )
    upstream = upstream_keep[...].astype(jnp.float32)
    sums_model[5:6, :] = row_sum(upstream)
    sums_model[6:7, :] = row_sum(
        (upstream * as_row(adapt_gain)).astype(jnp.bfloat16).astype(jnp.float32)
    )
    sums_model[7:8, :] = row_sum(upstream * adapted)
    adapted_part = as_row(adapt_gain) * adapted

    ring.share_finish(mlp_all, mlp_sems)
    mlp_flat[...] = flat_low(mlp_all)
    units = wfc1_ref.shape[1]
    block = 256
    for first in range(0, units, block):
        cols = slice(first, first + block)
        pre = (
            jnp.dot(mlp_flat[...], wfc1_ref[:, cols], preferred_element_type=jnp.float32)
            + as_row(fc1_bias)[:, cols]
        )
        below_curve = 0.5 + 0.5 * lax.erf(pre * ROOT_HALF)
        slope = below_curve + pre * jnp.exp(-0.5 * pre * pre) * NORMAL_PEAK
        hidden[:, cols] = (pre * below_curve).astype(jnp.bfloat16)
        pre_low = (hidden_grad[:, cols] * slope).astype(jnp.bfloat16)
        pre_grad[:, cols] = pre_low
        sums_ff[0:1, cols] = row_sum(pre_low.astype(jnp.float32))
    fill_parts(in_parts, contract_cols(pre_grad[...], wfc1_ref[...]))
    ring.give_start(in_parts, in_land, in_sems)
    fill_parts(
        out_parts, jnp.dot(hidden[...], wfc2_ref[...], preferred_element_type=jnp.float32)
    )
    ring.give_start(out_parts, out_land, out_sems)
    gfc1_ref[...] = contract_rows(mlp_flat[...], pre_grad[...]).astype(jnp.bfloat16)
    ring.give_finish(in_parts, in_land, in_sems)
    mlp_in_grad = ring.total(in_parts, in_land)
    middle = middle_keep[...]
    xhat, rs = norm_parts(middle, vit_eps)
    sums_model[3:4, :] = row_sum(mlp_in_grad * xhat)
    sums_model[4:5, :] = row_sum(mlp_in_grad)
    middle_grad = upstream + norm_pull(mlp_in_grad, xhat, rs, as_row(ln2_gain))
    grad_patches_ref[...] = middle_grad
    proj_low = middle_grad.astype(jnp.bfloat16)
    sums_model[2:3, :] = row_sum(proj_low.astype(jnp.float32))
    proj_all[t] = proj_low
    ring.share_start(proj_all, share_sems)
    gfc2_ref[...] = contract_rows(given_ref[...], hidden[...]).astype(jnp.bfloat16)
    job1.finish(1)
    job1.start(2)
    job2.finish(1)
    job2.start(2)
    for stage in range(2, stages - 1):
        job1.finish(stage)
        job1.start(stage + 1)
        job2.finish(stage)
        job2.start(stage + 1)
    ring.give_finish(out_parts, out_land, out_sems)
    vit_out = middle + (ring.total(out_parts, out_land) + as_row(fc2_bias))
    joined_ref[...] = (vit_out + adapted_part).astype(jnp.bfloat16)

    ring.share_finish(proj_all, share_sems)
    proj_flat[...] = flat_low(proj_all)
    attended_grad = contract_cols(proj_flat[...], wout_ref[...]).astype(jnp.bfloat16)
    for h in range(heads):
        here = slice(h * HEAD_DIM, (h + 1) * HEAD_DIM)
        there = slice(width + h * HEAD_DIM, width + (h + 1) * HEAD_DIM)
        head_grad = attended_grad[:, here]
        prob = probs[h]
        value_part = contract_rows(prob.astype(jnp.bfloat16), head_grad)
        prob_grad = contract_cols(head_grad, values_all[:, here])
        dot_rows = jnp.sum(prob * prob_grad, axis=-1, keepdims=True)
        score_grad = (prob * (prob_grad - dot_rows)).astype(jnp.bfloat16)
        dqkv[:, here] = (
            jnp.dot(score_grad, keys_all[:, here], preferred_element_type=jnp.float32) * scale
        ).astype(jnp.bfloat16)
        key_part = contract_rows(score_grad, queries[:, here]) * scale
        dkv_send[:, here] = key_part[half_rows:].astype(jnp.bfloat16)
        dkv_send[:, there] = value_part[half_rows:].astype(jnp.bfloat16)
        hidden_grad[:, here] = key_part[:half_rows]
        hidden_grad[:, there] = value_part[:half_rows]
    pair_copy(dkv_send, dkv_other, 1).start()
    gout_ref[...] = contract_rows(proj_flat[...], attended[...]).astype(jnp.bfloat16)
    pair_copy(dkv_send, dkv_other, 1).wait()
    kv_grad = (hidden_grad[:, 0 : 2 * width] + dkv_other[...].astype(jnp.float32)).astype(
        jnp.bfloat16
    )
    dqkv[:, width : 3 * width] = kv_grad
    attn_grad = contract_cols(dqkv[:, 0:width], wqkv_ref[0])
    for part in (1, 2):
        attn_grad += contract_cols(dqkv[:, part * width : (part + 1) * width], wqkv_ref[part])
    fill_parts(attn_parts, attn_grad)
    ring.give_start(attn_parts, attn_land, attn_sems)
    sums_heads[0:1, :] = row_sum(dqkv[:, 0:width].astype(jnp.float32))
    sums_heads[1:2, :] = row_sum(dqkv[:, 2 * width : 3 * width].astype(jnp.float32))
    gqkv_ref[...] = contract_rows(attn_ref[...], dqkv[...]).astype(jnp.bfloat16)
    ring.give_finish(pool_parts, pool_land, pool_sems)
    pool_land[t] = pool_parts[t]
    adapt_grad = (given_ref[...].astype(jnp.float32) * as_row(adapt_gain)).astype(jnp.bfloat16)
    gadapt_ref[...] = contract_rows(flat_low(pool_land), adapt_grad).astype(jnp.bfloat16)
    job1.finish(stages - 1, red1_ref)
    job2.finish(stages - 1, red2_ref)
    ring.give_finish(attn_parts, attn_land, attn_sems)
    attn_in_grad = ring.total(attn_parts, attn_land)
    xhat, rs = norm_parts(inputs, vit_eps)
    sums_model[0:1, :] = row_sum(attn_in_grad * xhat)
    sums_model[1:2, :] = row_sum(attn_in_grad)
    grad_patches_ref[...] += norm_pull(attn_in_grad, xhat, rs, as_row(ln1_gain))


def vit_block(
    patches, attn_all, grad_all, grad_own, map_mean, grad_pooled, branch_partial, gw1, gw2,
    ln1_gain, w_qkv, qv_bias, w_out, out_bias, ln2_gain, ln2_bias,
    w_fc1, fc1_bias, w_fc2, fc2_bias, w_adapt, adapt_bias, adapt_gain, pw2_bias, layer_scale,
    key_live,
):
    count = lax.axis_size("tensor")
    data = lax.axis_size("dp")
    rows, model = patches.shape
    half_rows = rows * count
    width = w_out.shape[0]
    heads = width // HEAD_DIM
    units = w_fc1.shape[1]
    channels = w_adapt.shape[0]
    map_rows, map_cols = gw1.shape[0] // data, gw1.shape[1]
    stage_rows = channels // (data * count)
    place = np.arange(channels // count)
    pick = np.stack(
        [(place // stage_rows * count + j) * stage_rows + place % stage_rows for j in range(count)]
    ).astype(np.int32)
    f32, low = jnp.float32, jnp.bfloat16

    def vmem(*shape, dtype=low):
        return pltpu.VMEM(shape, dtype)

    shard = vmem(count, rows, model)
    scratch = [
        vmem(2 * half_rows, width), vmem(2 * half_rows, width),
        vmem(half_rows, 2 * width), vmem(half_rows, 2 * width), vmem(half_rows, width),
        vmem(half_rows, units, dtype=f32), vmem(heads, half_rows, 2 * half_rows, dtype=f32),
        vmem(half_rows, width), vmem(rows, model, dtype=f32),
        vmem(half_rows, units), vmem(half_rows, units), vmem(half_rows, 3 * width),
        vmem(half_rows, 2 * width), vmem(half_rows, 2 * width),
        vmem(half_rows, model), vmem(half_rows, model),
    ]
    shards = [shard] * 10 + [
        vmem(count, rows, channels),
        vmem(count, rows, channels // count), vmem(count, rows, channels // count),
    ]
    job = halving_scratch(data, map_rows, map_cols)
    sems = [pltpu.SemaphoreType.DMA((2, count))] * 9

    def kernel(*refs):
        ins, rest = refs[:27], refs[27:]
        grad_own_ref = ins[26]
        outs, others = rest[:13], rest[13:]
        vit_kernel(*ins[:26], *outs, *others[:16], grad_own_ref, *others[16:])

    def out(*shape, dtype=low):
        return jax.ShapeDtypeStruct(shape, dtype)

    return pl.pallas_call(
        kernel,
        out_shape=(
            out(rows, model), out(rows, model, dtype=f32),
            out(map_rows, map_cols, dtype=f32), out(map_rows, map_cols, dtype=f32),
            out(model, units), out(model, units), out(model, width), out(model, 3 * width),
            out(channels // count, model),
            out(SUB, model, dtype=f32), out(SUB, channels, dtype=f32),
            out(SUB, width, dtype=f32), out(SUB, units, dtype=f32),
        ),
        in_specs=[VMEM_SPEC] * 27,
        out_specs=(VMEM_SPEC,) * 13,
        scratch_shapes=scratch + shards + job + job + sems,
        compiler_params=kernel_params(3),
        name="vit_block",
    )(
        patches, attn_all, grad_all, map_mean, grad_pooled,
        branch_partial.reshape(count, rows, channels),
        gw1.reshape(data, map_rows, map_cols), gw2.reshape(data, map_rows, map_cols),
        ln1_gain, w_qkv, qv_bias, w_out, out_bias, ln2_gain, ln2_bias,
        w_fc1, fc1_bias, w_fc2, fc2_bias, w_adapt, adapt_bias, adapt_gain,
        pw2_bias, layer_scale, key_live, jnp.asarray(pick), grad_own,
    )


def local(
    patches,
    hires,
    valid_rows,
    ln1_gain,
    ln1_bias,
    w_qkv,
    qv_bias,
    w_out,
    out_bias,
    ln2_gain,
    ln2_bias,
    w_fc1,
    fc1_bias,
    w_fc2,
    fc2_bias,
    dw_weight,
    dw_bias,
    lnc_gain,
    lnc_bias,
    w_pw1,
    pw1_bias,
    w_pw2,
    pw2_bias,
    layer_scale,
    w_adapt,
    adapt_bias,
    adapt_gain,
    grad_out,
):
    data_index = lax.axis_index("dp")
    image_index = data_index // IMG_SPAN
    map_cols, channels = hires.shape[1:]
    patch_rows, model = patches.shape
    half_rows = patch_rows * lax.axis_size("tensor")
    normed_low, conv_flat, low_rim, high_rim, attn_all, grad_all, map_mean = conv_forward(
        hires, dw_weight, dw_bias, lnc_gain, lnc_bias, patches, grad_out, ln1_gain, ln1_bias
    )
    normed_grad, branch_partial, gpw1, gpw2, pw1_sums, grad_pooled = map_block(
        normed_low, w_pw1, pw1_bias, w_pw2, grad_all, w_adapt, adapt_gain, layer_scale, map_cols
    )
    own_first = data_index % IMG_SPAN * half_rows
    other_first = (1 - data_index % IMG_SPAN) * half_rows
    key_place = jnp.concatenate(
        [own_first + jnp.arange(half_rows), other_first + jnp.arange(half_rows)]
    )
    image_valid = jnp.sum(jnp.where(jnp.arange(valid_rows.shape[0]) == image_index, valid_rows, 0))
    key_live = (key_place // SIDE < image_valid).astype(jnp.float32)[None]
    (
        joined_out, grad_patches, reduced_pw1, reduced_pw2, gfc1, gfc2, gout, gqkv, gadapt,
        sums_model, sums_map, sums_heads, sums_ff,
    ) = vit_block(
        patches, attn_all, grad_all, grad_out, map_mean, grad_pooled, branch_partial, gpw1, gpw2,
        ln1_gain, w_qkv, qv_bias, w_out, out_bias, ln2_gain, ln2_bias,
        w_fc1, fc1_bias, w_fc2, fc2_bias, w_adapt, adapt_bias, adapt_gain, pw2_bias, layer_scale,
        key_live,
    )
    (
        grad_hires, ring_total, data_total,
        reduced_fc1, reduced_fc2, reduced_qkv, reduced_out, reduced_adapt,
    ) = conv_backward(
        normed_grad, conv_flat, lnc_gain, hires, low_rim, high_rim, dw_weight, grad_pooled,
        sums_model, sums_map, sums_heads, sums_ff, pw1_sums, (gfc1, gfc2, gqkv, gout, gadapt),
    )
    width = w_out.shape[0]
    (
        grad_dw_weight,
        grad_lnc_gain, grad_lnc_bias, grad_dw_bias, grad_pw2_bias, grad_layer_scale,
        grad_ln1_gain, grad_ln1_bias, grad_out_bias, grad_ln2_gain, grad_ln2_bias, grad_fc2_bias,
        grad_adapt_bias, grad_adapt_gain,
        grad_pw1_bias, grad_fc1_bias, grad_qv_bias,
    ) = small_outputs(ring_total, data_total, channels, model, w_fc1.shape[1], width)
    return (
        joined_out,
        grad_patches,
        grad_hires,
        grad_ln1_gain,
        grad_ln1_bias,
        reduced_qkv.reshape(-1, 3, width).transpose(1, 0, 2),
        grad_qv_bias,
        reduced_out.T,
        grad_out_bias,
        grad_ln2_gain,
        grad_ln2_bias,
        reduced_fc1,
        grad_fc1_bias,
        reduced_fc2.T,
        grad_fc2_bias,
        grad_dw_weight,
        grad_dw_bias,
        grad_lnc_gain,
        grad_lnc_bias,
        reduced_pw1,
        grad_pw1_bias,
        reduced_pw2.T,
        grad_pw2_bias,
        grad_layer_scale,
        reduced_adapt,
        grad_adapt_bias,
        grad_adapt_gain,
    )


def solution(mesh):
    return jax.shard_map(
        local,
        mesh=mesh,
        in_specs=(
            P(("dp", "tensor"), None),
            P(("dp", "tensor"), None, None),
            P(),
            P(),
            P(),
            P(None, None, "tensor"),
            P(None, "tensor"),
            P("tensor", None),
            P(),
            P(),
            P(),
            P(None, "tensor"),
            P("tensor"),
            P("tensor", None),
            P(),
            P(),
            P(),
            P(),
            P(),
            P(None, "tensor"),
            P("tensor"),
            P("tensor", None),
            P(),
            P(),
            P(),
            P(),
            P(),
            P(("dp", "tensor"), None),
        ),
        out_specs=(
            P(("dp", "tensor"), None),
            P(("dp", "tensor"), None),
            P(("dp", "tensor"), None, None),
            P(("dp", "tensor")),
            P(("dp", "tensor")),
            P(None, "dp", "tensor"),
            P(None, ("tensor", "dp")),
            P("tensor", "dp"),
            P(("dp", "tensor")),
            P(("dp", "tensor")),
            P(("dp", "tensor")),
            P("dp", "tensor"),
            P(("tensor", "dp")),
            P("tensor", "dp"),
            P(("dp", "tensor")),
            P(None, ("dp", "tensor")),
            P(("dp", "tensor")),
            P(("dp", "tensor")),
            P(("dp", "tensor")),
            P("dp", "tensor"),
            P(("tensor", "dp")),
            P("tensor", "dp"),
            P(("dp", "tensor")),
            P(("dp", "tensor")),
            P(("dp", "tensor"), None),
            P(("dp", "tensor")),
            P(("dp", "tensor")),
        ),
        check_vma=False,
    )
```

```python
from functools import partial

import jax
import jax.numpy as jnp
import numpy as np
from jax import lax
from jax.experimental import pallas as pl
from jax.experimental.pallas import tpu as pltpu
from jax.sharding import PartitionSpec as P

HEAD_DIM = 64
SIDE = 24
KERNEL = 7
IMG_SPAN = 2


vit_eps = 1e-05
map_eps = 1e-06
masked_score = -1e30
ROOT_HALF = 0.7071067811865476
NORMAL_PEAK = 0.3989422804014327


def contract_rows(left_side, right_side):
    return lax.dot_general(
        left_side, right_side, (((0,), (0,)), ((), ())), preferred_element_type=jnp.float32
    )


def contract_cols(left_side, right_side):
    return lax.dot_general(
        left_side, right_side, (((1,), (1,)), ((), ())), preferred_element_type=jnp.float32
    )


def bits_of(count):
    return count.bit_length() - 1


class Halving:
    def __init__(self, source, landings, send, recv, top_first):
        self.count = lax.axis_size("dp")
        self.d, self.t = lax.axis_index("dp"), lax.axis_index("tensor")
        self.source, self.landings = source, landings
        self.send, self.recv, self.top_first = send, recv, top_first
        self.stages = bits_of(self.count)
        self.at = 0
        self.staging = None

    def begin(self, stage=0):
        self.at = stage
        self.start(stage)

    def step(self, out=None):
        if self.at == self.stages:
            return
        self.finish(self.at, out if self.at == self.stages - 1 else None)
        self.at += 1
        if self.at < self.stages:
            self.start(self.at)

    def plan(self, stage):
        here = self.source if stage == 0 else self.landings[stage - 1]
        half = self.count >> (stage + 1)
        top = self.top_first and stage > 0
        bit = self.stages - stage if top else stage
        own = lax.rem(self.d // (1 << bit), 2)
        partner = self.d + (1 - 2 * own) * (1 << bit)
        base = self.count - 2 * half

        def place(i, value):
            return value * half + i if top else 2 * i + value

        def copy(i):
            return pltpu.make_async_remote_copy(
                here.at[place(i, 1 - own)], self.landings[stage].at[i],
                self.send.at[base + i], self.recv.at[base + i],
                device_id=(partner, self.t), device_id_type=MESH_ID,
            )

        return here, half, own, place, copy

    def start(self, stage):
        here, half, own, place, copy = self.plan(stage)

        def body(i, carry):
            copy(i).start()
            return carry

        lax.fori_loop(0, half, body, 0)

    def finish(self, stage, out=None):
        here, half, own, place, copy = self.plan(stage)
        landing = self.landings[stage]
        rows = landing.shape[1]

        def body(i, carry):
            copy(i).wait()
            kept = here.at[place(i, own)]
            if self.staging is not None and stage == 1:
                load = pltpu.make_async_copy(kept, *self.staging)
                load.start()
                load.wait()
                kept = self.staging[0]
            total = kept[...].astype(jnp.float32) + landing[i].astype(jnp.float32)
            if out is None:
                landing[i] = total.astype(jnp.bfloat16)
            else:
                out[...] = total
            return carry

        lax.fori_loop(0, half, body, 0)


def halving_scratch(count, rows, cols, half):
    landings = []
    while half >= 1:
        landings.append(pltpu.VMEM((half, rows, cols), jnp.bfloat16))
        half //= 2
    return landings + [pltpu.SemaphoreType.DMA((count - 1,))] * 2


class Ring:
    def __init__(self):
        self.count = lax.axis_size("tensor")
        self.d, self.t = lax.axis_index("dp"), lax.axis_index("tensor")

    def at(self, k):
        return lax.rem(self.t + k, self.count)

    def share_copy(self, buffer, sems, k, source):
        return pltpu.make_async_remote_copy(
            buffer.at[source], buffer.at[source], sems.at[0, k], sems.at[1, source],
            device_id=(self.d, self.at(k)), device_id_type=MESH_ID,
        )

    def share_start(self, buffer, sems):
        for k in range(1, self.count):
            self.share_copy(buffer, sems, k, self.t).start()

    def share_finish(self, buffer, sems):
        for k in range(1, self.count):
            self.share_copy(buffer, sems, k, self.t).wait_send()
        for k in range(1, self.count):
            self.share_copy(buffer, sems, k, self.at(k)).wait_recv()

    def give_copy(self, parts, landing, sems, k, slot, part):
        return pltpu.make_async_remote_copy(
            parts.at[part], landing.at[slot], sems.at[0, k], sems.at[1, slot],
            device_id=(self.d, self.at(k)), device_id_type=MESH_ID,
        )

    def give_start(self, parts, landing, sems):
        for k in range(1, self.count):
            self.give_copy(parts, landing, sems, k, self.t, self.at(k)).start()

    def give_finish(self, parts, landing, sems):
        for k in range(1, self.count):
            self.give_copy(parts, landing, sems, k, self.t, self.at(k)).wait_send()
        for k in range(1, self.count):
            self.give_copy(parts, landing, sems, k, self.at(k), self.at(k)).wait_recv()

    def total(self, parts, landing):
        value = parts[self.t].astype(jnp.float32)
        for k in range(1, self.count):
            value = value + landing[self.at(k)].astype(jnp.float32)
        return value


class SmallSum:
    def __init__(self, landed, shared, send, recv, sems):
        self.landed, self.shared = landed, shared
        self.send, self.recv, self.sems = send, recv, sems
        self.ring = Ring()
        self.count = lax.axis_size("dp")

    def copy(self, k, part, slot):
        ring = self.ring
        return pltpu.make_async_remote_copy(
            self.piece(part), self.landed.at[slot], self.send.at[k], self.recv.at[slot],
            device_id=(lax.rem(ring.d + k, self.count), ring.t), device_id_type=MESH_ID,
        )

    def start(self):
        def body(k, carry):
            self.copy(k, lax.rem(self.ring.d + k, self.count), self.ring.d).start()
            return carry

        lax.fori_loop(1, self.count, body, 0)

    def share(self, out):
        out[...] = self.piece(self.ring.d)[...]

        def body(k, carry):
            slot = lax.rem(self.ring.d + k, self.count)
            self.copy(k, slot, self.ring.d).wait_send()
            self.copy(k, slot, slot).wait_recv()
            out[...] += self.landed[slot]
            return carry

        lax.fori_loop(1, self.count, body, 0)
        self.shared[self.ring.t] = out[...]
        self.ring.share_start(self.shared, self.sems)

    def finish(self, out):
        self.ring.share_finish(self.shared, self.sems)
        total = self.shared[0]
        for j in range(1, self.ring.count):
            total = total + self.shared[j]
        out[...] = total


def small_sum_scratch(data, count, rows):
    block = (rows, 2 * LANES)
    return [
        pltpu.VMEM((data,) + block, jnp.float32),
        pltpu.VMEM((count,) + block, jnp.float32),
        pltpu.SemaphoreType.DMA((data,)), pltpu.SemaphoreType.DMA((data,)),
        pltpu.SemaphoreType.DMA((2, count)),
    ]


def norm_parts(values, epsilon):
    centered = values - jnp.mean(values, axis=-1, keepdims=True)
    variance = jnp.mean(centered * centered, axis=-1, keepdims=True)
    scale = lax.rsqrt(variance + epsilon)
    return centered * scale, scale


def norm_pull(grad, xhat, scale, gain):
    scaled = grad * gain
    return scale * (
        scaled
        - jnp.mean(scaled, axis=-1, keepdims=True)
        - xhat * jnp.mean(scaled * xhat, axis=-1, keepdims=True)
    )


def row_sum(values):
    return jnp.sum(values, axis=0, keepdims=True)


def flat_low(buffer):
    count, rows, cols = buffer.shape
    return buffer[...].astype(jnp.float32).reshape(count * rows, cols).astype(jnp.bfloat16)


def fill_rows(blocks, first, value):
    rows = blocks.shape[1]
    for c in range(value.shape[0] // rows):
        blocks[first // rows + c] = value[c * rows : (c + 1) * rows].astype(jnp.bfloat16)


def fill_parts(parts, value):
    count, rows, _ = parts.shape
    for j in range(count):
        parts[j] = value[j * rows : (j + 1) * rows].astype(jnp.bfloat16)


MESH_ID = pl.DeviceIdType.MESH
VMEM_SPEC = pl.BlockSpec(memory_space=pltpu.VMEM)
LANES = 128
SUB = 8
VMEM_BYTES = 62 * 1024 * 1024


def kernel_params(collective_id=None):
    if collective_id is None:
        return pltpu.CompilerParams(vmem_limit_bytes=VMEM_BYTES)
    return pltpu.CompilerParams(
        vmem_limit_bytes=VMEM_BYTES, collective_id=collective_id, has_side_effects=True
    )


def halo_route():
    count = lax.axis_size("tensor")
    d, t = lax.axis_index("dp"), lax.axis_index("tensor")
    odd = lax.rem(d, IMG_SPAN)
    up = (d + (t + 1) // count, lax.rem(t + 1, count))
    down = (d - 1 + (t + count - 1) // count, lax.rem(t + count - 1, count))
    up_here = (t + 1) // count + odd < 2
    down_here = t + odd > 0
    return up, down, up_here, down_here


def seam_here():
    count = lax.axis_size("tensor")
    d, t = lax.axis_index("dp"), lax.axis_index("tensor")
    odd = lax.rem(d, IMG_SPAN)
    at_last = (t + 1) // count
    at_first = 1 - (t + count - 1) // count
    return at_last * (1 - odd) + at_first * odd


def meet(data_peers, across_seam=True):
    count = lax.axis_size("tensor")
    d, t = lax.axis_index("dp"), lax.axis_index("tensor")
    odd = lax.rem(d, IMG_SPAN)
    barrier = pltpu.get_barrier_semaphore()
    for k in range(1, count):
        pl.semaphore_signal(
            barrier, inc=1, device_id=(d, lax.rem(t + k, count)), device_id_type=MESH_ID
        )
    for peer in data_peers:
        pl.semaphore_signal(barrier, inc=1, device_id=(peer, t), device_id_type=MESH_ID)
    if not across_seam:
        pl.semaphore_wait(barrier, count - 1 + len(data_peers))
        return
    seam = seam_here()

    @pl.when(seam > 0)
    def _():
        pl.semaphore_signal(
            barrier, inc=1, device_id=(d + 1 - 2 * odd, count - 1 - t), device_id_type=MESH_ID
        )

    pl.semaphore_wait(barrier, count - 1 + len(data_peers) + seam)


def as_row(ref):
    return ref[...].reshape(1, ref.shape[0])


def halo_copies(route, first_rows, last_rows, low_ref, high_ref, send_sem, recv_sem):
    up, down, up_here, down_here = route
    to_up = pltpu.make_async_remote_copy(
        last_rows, low_ref, send_sem.at[0], recv_sem.at[0], device_id=up, device_id_type=MESH_ID
    )
    to_down = pltpu.make_async_remote_copy(
        first_rows, high_ref, send_sem.at[1], recv_sem.at[1], device_id=down, device_id_type=MESH_ID
    )
    return to_up, to_down


def halo_start(route, copies):
    @pl.when(route[2])
    def _():
        copies[0].start()

    @pl.when(route[3])
    def _():
        copies[1].start()


def halo_finish(route, copies):
    @pl.when(route[2])
    def _():
        copies[0].wait_send()
        copies[1].wait_recv()

    @pl.when(route[3])
    def _():
        copies[1].wait_send()
        copies[0].wait_recv()


def halo_store(route, extended, low_ref, high_ref, rows, cols, rim):
    @pl.when(route[3])
    def _():
        extended[0:rim, SUB : SUB + cols, :] = low_ref[...].astype(jnp.float32)

    @pl.when(route[2])
    def _():
        extended[rim + rows : 2 * rim + rows, SUB : SUB + cols, :] = high_ref[...].astype(
            jnp.float32
        )


def conv_rows(extended, taps_ref, rows, cols, blocks, flipped, emit):
    span = KERNEL * KERNEL - 1
    rim = KERNEL // 2
    tiles = cols // SUB
    inside = lax.broadcasted_iota(jnp.int32, (SUB, LANES), 0)

    def lane_block(block, carry):
        lanes = pl.ds(pl.multiple_of(block * LANES, LANES), LANES)
        for e in range(KERNEL):
            shift = e - rim
            taps = []
            for a in range(KERNEL):
                index = a * KERNEL + e
                taps.append(taps_ref[pl.ds(span - index if flipped else index, 1), lanes])
            first = 1 if shift >= 0 else 0
            last = tiles + 1 if shift <= 0 else tiles + 2
            before = [None] * rows
            for tile in range(first, last):
                cells = [
                    extended[r, SUB * tile : SUB * tile + SUB, lanes]
                    for r in range(rows + KERNEL - 1)
                ]
                for i in range(rows):
                    total = cells[i] * taps[0]
                    for a in range(1, KERNEL):
                        total = total + cells[i + a] * taps[a]
                    if shift == 0:
                        emit(e, i, tile - 1, lanes, total)
                        continue
                    turned = pltpu.roll(total, (SUB - shift) % SUB, 0)
                    if tile > first:
                        split = SUB - shift if shift > 0 else -shift
                        value = jnp.where(inside < split, before[i], turned)
                        emit(e, i, tile - 1 - first, lanes, value)
                    before[i] = turned
        return carry

    lax.fori_loop(blocks[0], blocks[1], lane_block, 0)


def tap_rows(grads, map_refs, tap_grad_ref, rows, cols, blocks):
    rim = KERNEL // 2
    low_ref, own_ref, high_ref = map_refs
    pairs = cols // (2 * SUB)
    inside = lax.broadcasted_iota(jnp.int32, (SUB, LANES), 0)

    def lane_block(block, carry):
        lanes = pl.ds(pl.multiple_of(block * LANES, LANES), LANES)
        for e in range(KERNEL):
            shift = e - rim
            sums = [None] * KERNEL
            for pair in range(pairs):
                here = slice(2 * SUB * pair, 2 * SUB * pair + 2 * SUB)
                cells = (
                    [low_ref[r, here, lanes] for r in range(rim)]
                    + [own_ref[r, here, lanes] for r in range(rows)]
                    + [high_ref[r, here, lanes] for r in range(rim)]
                )
                cells = [cell.astype(jnp.float32) for cell in cells]
                for i in range(rows):
                    first = SUB * (2 * pair + (0 if shift > 0 else 1))
                    count = 2 if shift == 0 else 3
                    given = [
                        grads[rim + i, first + SUB * k : first + SUB * k + SUB, lanes]
                        for k in range(count)
                    ]
                    if shift != 0:
                        turned = [pltpu.roll(tile, shift % SUB, 0) for tile in given]
                        split = shift if shift > 0 else SUB + shift
                        given = [
                            jnp.where(inside < split, turned[k], turned[k + 1]) for k in range(2)
                        ]
                    for a in range(KERNEL):
                        cell = cells[i + a]
                        term = cell[0:SUB] * given[0] + cell[SUB : 2 * SUB] * given[1]
                        sums[a] = term if sums[a] is None else sums[a] + term
            for a in range(KERNEL):
                tap_grad_ref[pl.ds(a * KERNEL + e, 1), lanes] = jnp.sum(
                    sums[a], axis=0, keepdims=True
                )
        return carry

    lax.fori_loop(blocks[0], blocks[1], lane_block, 0)


def conv_forward_kernel(
    own_ref, taps_ref, bias_1d, gain_1d, shift_1d, pool_ref, patches_ref, upstream_ref,
    ln1_gain, ln1_bias,
    normed_ref, conv_ref, low_ref, high_ref, attn_ref, given_ref, mean_ref,
    extended, vectors, given_all, send_sem, recv_sem, given_sems,
):
    rows, cols, channels = own_ref.shape
    rim = KERNEL // 2
    route = halo_route()
    ring = Ring()
    meet(())
    copies = halo_copies(
        route, own_ref.at[pl.ds(0, rim)], own_ref.at[pl.ds(rows - rim, rim)],
        low_ref, high_ref, send_sem, recv_sem,
    )
    halo_start(route, copies)
    given_all[ring.t] = upstream_ref[...]
    xhat, _ = norm_parts(patches_ref[...].astype(jnp.float32), vit_eps)
    attn_ref[...] = (xhat * as_row(ln1_gain) + as_row(ln1_bias)).astype(jnp.bfloat16)
    vectors[0:1, :] = as_row(bias_1d)
    vectors[1:2, :] = as_row(gain_1d)
    vectors[2:3, :] = as_row(shift_1d)
    bias_ref, gain_ref, shift_ref = vectors.at[0:1], vectors.at[1:2], vectors.at[2:3]
    quarter = pool_ref.shape[0]
    for pair in range(rows // 2):
        mean_ref[pair * quarter : (pair + 1) * quarter, :] = jnp.dot(
            pool_ref[...],
            own_ref[2 * pair : 2 * pair + 2].reshape(2 * cols, channels),
            preferred_element_type=jnp.float32,
        )
    for edge in (0, SUB + cols):
        extended[:, edge : edge + SUB, :] = jnp.zeros(
            (rows + 2 * rim, SUB, channels), jnp.float32
        )
    extended[rim : rim + rows, SUB : SUB + cols, :] = own_ref[...].astype(jnp.float32)
    halo_finish(route, copies)
    ring.share_start(given_all, given_sems)

    @pl.when(jnp.logical_not(route[3]))
    def _():
        low_ref[...] = jnp.zeros_like(low_ref)
        extended[0:rim, SUB : SUB + cols, :] = jnp.zeros((rim, cols, channels), jnp.float32)

    @pl.when(jnp.logical_not(route[2]))
    def _():
        high_ref[...] = jnp.zeros_like(high_ref)
        extended[rim + rows : 2 * rim + rows, SUB : SUB + cols, :] = jnp.zeros(
            (rim, cols, channels), jnp.float32
        )

    halo_store(route, extended, low_ref, high_ref, rows, cols, rim)

    def emit(e, i, tile, lanes, value):
        here = slice(i * cols + tile * SUB, i * cols + tile * SUB + SUB)
        if e == 0:
            conv_ref[here, lanes] = value + bias_ref[:, lanes]
        else:
            conv_ref[here, lanes] += value

    conv_rows(extended, taps_ref, rows, cols, (0, channels // LANES), False, emit)
    step = 2 * SUB

    def norm_block(block, carry):
        here = pl.ds(pl.multiple_of(block * step, step), step)
        values = conv_ref[here, :]
        centered = values - jnp.mean(values, axis=-1, keepdims=True)
        variance = jnp.mean(centered * centered, axis=-1, keepdims=True)
        scaled = centered * lax.rsqrt(variance + map_eps) * gain_ref[...] + shift_ref[...]
        normed_ref[here, :] = scaled.astype(jnp.bfloat16)
        return carry

    lax.fori_loop(0, rows * cols // step, norm_block, 0)
    ring.share_finish(given_all, given_sems)
    given_ref[...] = flat_low(given_all)


def pool_matrix(map_cols):
    chunk = 2 * map_cols
    cell_patch = (np.arange(chunk) % map_cols) // 2
    return np.arange(chunk // 4)[:, None] == cell_patch[None, :]


def conv_forward(hires, taps, bias, gain, shift, patches, upstream, ln1_gain, ln1_bias):
    rows, cols, channels = hires.shape
    rim = KERNEL // 2
    cells = rows * cols
    count = lax.axis_size("tensor")
    patch_rows, model = patches.shape
    pool = jnp.asarray(np.where(pool_matrix(cols), 0.25, 0.0), jnp.bfloat16)
    flat = jax.ShapeDtypeStruct((count * patch_rows, model), jnp.bfloat16)
    return pl.pallas_call(
        conv_forward_kernel,
        out_shape=(
            jax.ShapeDtypeStruct((cells, channels), jnp.bfloat16),
            jax.ShapeDtypeStruct((cells, channels), jnp.float32),
            jax.ShapeDtypeStruct((rim, cols, channels), jnp.bfloat16),
            jax.ShapeDtypeStruct((rim, cols, channels), jnp.bfloat16),
            jax.ShapeDtypeStruct((patch_rows, model), jnp.bfloat16),
            flat,
            jax.ShapeDtypeStruct((patch_rows, channels), jnp.float32),
        ),
        in_specs=[VMEM_SPEC] * 10,
        out_specs=(VMEM_SPEC,) * 7,
        scratch_shapes=[
            pltpu.VMEM((rows + 2 * rim, cols + 2 * SUB, channels), jnp.float32),
            pltpu.VMEM((SUB, channels), jnp.float32),
            pltpu.VMEM((count, patch_rows, model), jnp.bfloat16),
            pltpu.SemaphoreType.DMA((2,)),
            pltpu.SemaphoreType.DMA((2,)),
            pltpu.SemaphoreType.DMA((2, count)),
        ],
        compiler_params=kernel_params(0),
        name="conv_forward",
    )(hires, taps, bias, gain, shift, pool, patches, upstream, ln1_gain, ln1_bias)


def window_start(m, width, data):
    block, most = m * (width // data) // LANES, width // LANES - 2
    return (block - block // (most + 1) * (block - most)) * LANES


def lane_start(m, width, data):
    return m * (width // data) // LANES * LANES


JOB_ORDERS = (False, True, False, True, True)


WHOLE = 10


def small_kernel(shapes, tall_ring, tall_data, few_ring, few_data, *refs):
    outs = refs[WHOLE:]
    channels, model, units, width = shapes
    d, t = lax.axis_index("dp"), lax.axis_index("tensor")
    data, count = lax.axis_size("dp"), lax.axis_size("tensor")
    taps = KERNEL * KERNEL

    def turned(value, first):
        size = value.shape[1]
        return pltpu.roll(value, lax.rem(size - first, size), 1)

    here = channels // (data * count)
    start = jnp.minimum(d * (channels // data) // LANES, channels // LANES - 2) * LANES
    first = d * (channels // data) - start
    wide = turned(tall_ring[...], first + t * here)
    outs[0][...] = wide[:, 0:LANES].T[0:here, 0:taps]
    for i in range(5):
        outs[1 + i][...] = wide[taps + i, 0:here]
    step = model // data
    first = d * step - d * step // LANES * LANES + t * (step // count)
    narrow = turned(few_ring[0:SUB, 0:LANES], first)
    for i in range(8):
        outs[6 + i][...] = narrow[i, 0 : step // count]
    step = outs[14].shape[0]
    first = d * step - jnp.minimum(d * step // LANES, channels // LANES - 2) * LANES
    last_rows = tall_data.shape[0] - SUB
    outs[14][...] = turned(tall_data[last_rows:, :], first)[taps + 5 - last_rows, 0:step]
    step = units // data
    first = d * step - d * step // LANES * LANES
    outs[15][...] = turned(few_data[0:SUB, LANES : 2 * LANES], first)[0, 0:step]
    step = width // data
    first = d * step - d * step // LANES * LANES
    outs[16][...] = turned(few_data[SUB : 2 * SUB, 0:LANES], first)[0:2, 0:step]
    joined, patches, hires, pw1, pw2, fc1, fc2, qkv, out, adapt = refs[:WHOLE]
    whole = outs[17:]
    for source, target in zip((joined, patches, hires, pw1, fc1, adapt, pw2), whole[:7]):
        target[...] = source[...]
    for source, target in zip((fc2, out), whole[7:9]):
        target[...] = source[...].T
    for part in range(3):
        whole[9][part] = qkv[:, part * width : (part + 1) * width]


def small_outputs(sums, results, channels, model, units, width):
    data, count = lax.axis_size("dp"), lax.axis_size("tensor")
    taps = KERNEL * KERNEL
    shapes = (
        [(channels // (data * count), taps)]
        + [(channels // (data * count),)] * 5
        + [(model // (data * count),)] * 8
        + [(channels // data,), (units // data,), (2, width // data)]
    )
    joined, patches, hires, pw1, pw2, fc1, fc2, qkv, out, adapt = results
    more = [jax.ShapeDtypeStruct(r.shape, r.dtype) for r in results[:4] + (fc1, adapt, pw2)]
    more += [jax.ShapeDtypeStruct(r.shape[::-1], r.dtype) for r in (fc2, out)]
    more.append(jax.ShapeDtypeStruct((3, qkv.shape[0], width), qkv.dtype))
    return pl.pallas_call(
        partial(small_kernel, (channels, model, units, width)),
        out_shape=tuple(jax.ShapeDtypeStruct(shape, jnp.float32) for shape in shapes) + tuple(more),
        in_specs=[VMEM_SPEC] * (len(sums) + WHOLE),
        out_specs=(VMEM_SPEC,) * (len(shapes) + WHOLE),
        compiler_params=kernel_params(),
        name="small_outputs",
    )(*sums, *results)


def with_loads(kernel, inputs, later):
    specs = [VMEM_SPEC] * len(inputs)
    for index in later:
        specs[index] = pl.BlockSpec(memory_space=pl.ANY)
    buffers = [pltpu.VMEM(inputs[index].shape, inputs[index].dtype) for index in later]
    buffers.append(pltpu.SemaphoreType.DMA((len(later),)))

    def run(*refs):
        refs, own = list(refs[: -len(buffers)]), refs[-len(buffers) :]
        copies = {}
        for place, index in enumerate(later):
            copies[index] = pltpu.make_async_copy(refs[index], own[place], own[-1].at[place])
            copies[index].start()
            refs[index] = own[place]
        kernel(lambda index: copies[index].wait(), *refs)

    return specs, buffers, run


def mirror(index, low_half, last):
    return index + (1 - low_half) * (last - 2 * index)


def map_kernel(
    need, own_ref, w1_ref, b1_1d, w2_ref, given_ref, wadapt_ref, adapt_gain, layer_scale,
    pool_ref, spread_ref, conv_ref, gain_1d, attn_own,
    grad_ref, branch_ref, half1_ref, half2_ref, gb1_ref, pooled_grad_ref, attn_ref, sums_ref,
    gw1_ref, gw2_ref, attn_all, half_sems, attn_sems,
    b1_ref, branch_grad_ref, pooled_grads, rows_all, pre_grads, stash, from_below, from_above, pooled, hidden_grads,
    ag_recv, ag_up, ag_down, up_recv, up_send, down_recv, down_send,
):
    count, cells, channels = rows_all.shape
    hidden = w1_ref.shape[1]
    parts = ag_recv.shape[1]
    chunk = cells // parts
    quarter = chunk // 4
    last = count - 1
    d, t = lax.axis_index("dp"), lax.axis_index("tensor")
    low_half = 1 - t // 2
    place = mirror(t, low_half, last)
    above, below = (d, t + 1), (d, t - 1)
    ring = Ring()
    core = d + 1 - 2 * lax.rem(d, 2)
    meet([core], False)
    job1 = Halving(gw1_ref, [half1_ref], half_sems.at[0], half_sems.at[1], False)
    job2 = Halving(gw2_ref, [half2_ref], half_sems.at[2], half_sems.at[3], False)

    def rows_of(p):
        return pl.ds(pl.multiple_of(p * chunk, chunk), chunk)

    def gather_copy(j, p, target, send):
        return pltpu.make_async_remote_copy(
            rows_all.at[j, rows_of(p)], rows_all.at[j, rows_of(p)],
            send.at[j, p], ag_recv.at[j, p], device_id=target, device_id_type=MESH_ID,
        )

    def sum_copy(j, p, going_up):
        landing = from_below if going_up else from_above
        return pltpu.make_async_remote_copy(
            stash.at[j, rows_of(p)], landing.at[j, rows_of(p)],
            (up_send if going_up else down_send).at[j, p],
            (up_recv if going_up else down_recv).at[j, p],
            device_id=above if going_up else below, device_id_type=MESH_ID,
        )

    rows_all[t] = own_ref[...]
    for p in range(parts):
        @pl.when(t < last)
        def _():
            gather_copy(t, p, above, ag_up).start()

        @pl.when(t > 0)
        def _():
            gather_copy(t, p, below, ag_down).start()

    b1_ref[0:1, :] = as_row(b1_1d)
    adapt_grad = (given_ref[...].astype(jnp.float32) * as_row(adapt_gain)).astype(jnp.bfloat16)
    need(5)
    pooled_grad = contract_cols(adapt_grad, wadapt_ref[...])
    pooled_grads[...] = pooled_grad
    branch_grad_ref[...] = (as_row(layer_scale) * (pooled_grad * 0.25)).astype(jnp.bfloat16)
    own_rows = pooled_grad_ref.shape[0]
    pooled_grad_ref[...] = pooled_grads[pl.ds(pl.multiple_of(t * own_rows, SUB), own_rows), :]
    need(3)
    hidden_grads[...] = contract_cols(branch_grad_ref[...], w2_ref[...])
    gb1_ref[...] = jnp.zeros_like(gb1_ref)
    block = 256

    def pass_on(j, p, going_up):
        copy = sum_copy(j, p, going_up)
        copy.wait_recv()
        landing = from_below if going_up else from_above
        stash[j, rows_of(p), :] = (
            stash[j, rows_of(p), :].astype(jnp.float32)
            + landing[j, rows_of(p), :].astype(jnp.float32)
        ).astype(jnp.bfloat16)
        copy.start()

    middle = place == 1

    def forward_up(s, carry):
        j, p = t + 1 + s // parts, lax.rem(s, parts)
        pass_on(j, p, True)
        return carry

    def forward_down(s, carry):
        j, p = t - 1 - s // parts, lax.rem(s, parts)
        pass_on(j, p, False)
        return carry

    def forward(first, last_step, along):
        @pl.when(jnp.logical_and(middle, low_half == 1))
        def _():
            lax.fori_loop(first, last_step, forward_up if along else forward_down, 0)

        @pl.when(jnp.logical_and(middle, low_half == 0))
        def _():
            lax.fori_loop(first, last_step, forward_down if along else forward_up, 0)

    def order(n):
        return mirror(n + place * (1 - 2 * n) * (1 - n // 2), low_half, last)

    def receive(j, p):
        gather_copy(j, p, above, ag_up).wait_recv()

        @pl.when(jnp.logical_and(j < t, t < last))
        def _():
            gather_copy(j, p, above, ag_up).start()

        @pl.when(jnp.logical_and(j > t, t > 0))
        def _():
            gather_copy(j, p, below, ag_down).start()

    def receive_all(j):
        for p in range(parts):
            receive(j, p)

    def send_sums(j, p):
        @pl.when(jnp.logical_and(j > t, t == 0))
        def _():
            sum_copy(j, p, True).start()

        @pl.when(jnp.logical_and(j < t, t == last))
        def _():
            sum_copy(j, p, False).start()

    def compute(j, here, small):
        rows = here.size
        few = rows // 4
        given = rows_all[j, here, :]
        for first in range(0, hidden, block):
            cols = slice(first, first + block)
            pre = (
                jnp.dot(given, w1_ref[:, cols], preferred_element_type=jnp.float32)
                + b1_ref[0:1, cols]
            )
            wide_grad = hidden_grads[small, cols]
            high = wide_grad.astype(jnp.bfloat16)
            rest = (wide_grad - high.astype(jnp.float32)).astype(jnp.bfloat16)
            spread = spread_ref[0:rows, 0:few]
            spread_grad = jnp.dot(
                spread, high, preferred_element_type=jnp.float32
            ) + jnp.dot(spread, rest, preferred_element_type=jnp.float32)
            below_curve = 0.5 + 0.5 * lax.erf(pre * ROOT_HALF)
            slope = below_curve + pre * jnp.exp(-0.5 * pre * pre) * NORMAL_PEAK
            active = (pre * below_curve).astype(jnp.bfloat16)
            pooled[small, cols] = jnp.dot(
                pool_ref[0:few, 0:rows], active, preferred_element_type=jnp.float32
            )
            pre_low = (spread_grad * slope).astype(jnp.bfloat16)
            gb1_ref[:, cols] += jnp.sum(pre_low.astype(jnp.float32), axis=0, keepdims=True)
            pre_grads[j, here, cols] = pre_low
        return contract_cols(pre_grads[j, here, :], w1_ref[...])

    def whole_shard(n, carry):
        j = order(n)

        @pl.when(jnp.logical_and(place == 1, n == 1))
        def _():
            receive_all(order(1))
            receive_all(order(2))

        @pl.when(jnp.logical_and(place == 1, n == last))
        def _():
            receive_all(order(last))
            forward(0, 1, True)

        few = cells // 4
        partial_grad = compute(
            j, pl.ds(0, cells), pl.ds(pl.multiple_of(j * few, SUB), few)
        )

        @pl.when(n == 0)
        def _():
            grad_ref[...] = partial_grad

        @pl.when(n > 0)
        def _():
            stash[j] = partial_grad.astype(jnp.bfloat16)

        return carry

    def one_chunk(q, carry):
        j, p = order(1 + q // parts), lax.rem(q, parts)
        receive(j, p)
        small = pl.ds(pl.multiple_of((j * parts + p) * quarter, SUB), quarter)
        stash[j, rows_of(p), :] = compute(j, rows_of(p), small).astype(jnp.bfloat16)
        send_sums(j, p)
        return carry

    attn_all[t] = attn_own[...]
    need(1)
    lax.fori_loop(0, 1 + last * place, whole_shard, 0)
    lax.fori_loop(0, last * parts * (1 - place), one_chunk, 0)
    ring.share_start(attn_all, attn_sems)

    wide = 384
    rows_flat = rows_all.reshape(count * cells, channels)
    pre_flat = pre_grads.reshape(count * cells, hidden)
    steps = []
    for p in range(1, 2 * parts):
        steps.append((p, True))
        if p > parts:
            steps.append((p - parts - 1, False))
    steps += [(p, False) for p in range(parts - 1, parts)]
    starts = list(range(0, channels, wide))
    for index, (p, along) in enumerate(steps):
        forward(p, p + 1, along)
        if index < len(starts):
            first = starts[index]
            fill_rows(
                gw1_ref, first, contract_rows(rows_flat[:, first : first + wide], pre_flat[...])
            )
    job1.start(0)
    pooled_low = pooled[...].astype(jnp.bfloat16)
    for first in range(0, channels, wide):
        fill_rows(
            gw2_ref, first,
            4.0 * contract_rows(branch_grad_ref[:, first : first + wide], pooled_low),
        )
    job2.start(0)
    branch_ref[...] = jnp.dot(
        pooled_low, w2_ref[...], preferred_element_type=jnp.float32
    ).astype(jnp.bfloat16)

    def finish(p, carry):
        @pl.when(t > 0)
        def _():
            sum_copy(t, p, True).wait_recv()
            grad_ref[rows_of(p), :] += from_below[t, rows_of(p), :].astype(jnp.float32)

        @pl.when(t < last)
        def _():
            sum_copy(t, p, False).wait_recv()
            grad_ref[rows_of(p), :] += from_above[t, rows_of(p), :].astype(jnp.float32)

        return carry

    lax.fori_loop(0, parts, finish, 0)
    need(10)
    sums_ref[...] = jnp.zeros_like(sums_ref)
    gain = as_row(gain_1d)
    step = 2 * SUB

    def grad_block(block, carry):
        here = pl.ds(pl.multiple_of(block * step, step), step)
        dy = grad_ref[here, :]
        xhat, rs = norm_parts(conv_ref[here, :], map_eps)
        grad = norm_pull(dy, xhat, rs, gain)
        grad_ref[here, :] = grad
        sums_ref[0:1, :] += row_sum(dy * xhat)
        sums_ref[1:2, :] += row_sum(dy)
        sums_ref[2:3, :] += row_sum(grad)
        return carry

    lax.fori_loop(0, cells // step, grad_block, 0)
    ring.share_finish(attn_all, attn_sems)
    attn_ref[...] = flat_low(attn_all)
    job1.finish(0)
    job2.finish(0)

    def drain(q, carry):
        j, p = q // parts, lax.rem(q, parts)

        @pl.when(jnp.logical_and(j <= t, t < last))
        def _():
            gather_copy(j, p, above, ag_up).wait_send()

        @pl.when(jnp.logical_and(j >= t, t > 0))
        def _():
            gather_copy(j, p, below, ag_down).wait_send()

        @pl.when(j > t)
        def _():
            sum_copy(j, p, True).wait_send()

        @pl.when(j < t)
        def _():
            sum_copy(j, p, False).wait_send()

        return carry

    lax.fori_loop(0, count * parts, drain, 0)


def map_block(
    normed_low, w_pw1, pw1_bias, w_pw2, grad_all, w_adapt, adapt_gain, layer_scale,
    conv, gain, attn_own, map_cols,
):
    cells, channels = normed_low.shape
    hidden = w_pw1.shape[1]
    count, data = lax.axis_size("tensor"), lax.axis_size("dp")
    chunk = 2 * map_cols
    parts = cells // chunk
    patches, model = grad_all.shape
    match = np.kron(np.eye(parts), pool_matrix(map_cols)) > 0.5
    pool = jnp.asarray(np.where(match, 0.25, 0.0), jnp.bfloat16)
    spread = jnp.asarray(match.T, jnp.bfloat16)
    low_all = pltpu.VMEM((count, cells, channels), jnp.bfloat16)
    sems = pltpu.SemaphoreType.DMA((count, parts))
    weight = pltpu.VMEM((data, channels // data, hidden), jnp.bfloat16)
    half = jax.ShapeDtypeStruct((data // 2, channels // data, hidden), jnp.bfloat16)
    inputs = (
        normed_low, w_pw1, pw1_bias, w_pw2, grad_all, w_adapt, adapt_gain, layer_scale,
        pool, spread, conv, gain, attn_own,
    )
    later = (5, 3, 1, 10)
    specs, buffers, run = with_loads(map_kernel, inputs, later)
    return pl.pallas_call(
        run,
        out_shape=(
            jax.ShapeDtypeStruct((cells, channels), jnp.float32),
            jax.ShapeDtypeStruct((patches, channels), jnp.bfloat16),
            half,
            half,
            jax.ShapeDtypeStruct((1, hidden), jnp.float32),
            jax.ShapeDtypeStruct((patches // count, channels), jnp.float32),
            jax.ShapeDtypeStruct((patches, model), jnp.bfloat16),
            jax.ShapeDtypeStruct((SUB, channels), jnp.float32),
        ),
        in_specs=specs,
        out_specs=(VMEM_SPEC,) * 8,
        scratch_shapes=[
            weight,
            weight,
            pltpu.VMEM((count, patches // count, model), jnp.bfloat16),
            pltpu.SemaphoreType.DMA((4, data - 1)),
            pltpu.SemaphoreType.DMA((2, count)),
            pltpu.VMEM((SUB, hidden), jnp.float32),
            pltpu.VMEM((patches, channels), jnp.bfloat16),
            pltpu.VMEM((patches, channels), jnp.float32),
            low_all,
            pltpu.VMEM((count, cells, hidden), jnp.bfloat16),
            low_all,
            low_all,
            low_all,
            pltpu.VMEM((patches, hidden), jnp.float32),
            pltpu.VMEM((patches, hidden), jnp.float32),
        ]
        + [sems] * 7
        + buffers,
        compiler_params=kernel_params(2),
        name="map_block",
    )(*inputs)


def last_kernel(
    need, patches_ref, attn_ref, given_ref, map_mean_ref, grad_pooled_ref, branch_parts, half1_ref, half2_ref,
    ln1_gain, wqkv_ref, qv_bias, wout_ref, out_bias, ln2_gain, ln2_bias,
    wfc1_ref, fc1_bias, wfc2_ref, fc2_bias, wadapt_ref, adapt_bias, adapt_gain,
    pw2_bias, layer_scale, live_ref, pick_ref, upstream_keep, conv_grad_ref,
    own_map, low_map, high_map, taps_ref, spread_ref, sums_conv, pw1_sums,
    joined_ref, grad_patches_ref, red1_ref, red2_ref, hires_grad_ref, tall_ring, tall_data, few_ring, few_data,
    job_outs,
    keys_all, values_all, kv_own, kv_other, queries, hidden_grad, probs, attended, middle_keep,
    hidden, pre_grad, dkv_other, mlp_flat,
    parts, landing, out_parts, out_land, shared, branch_land, pool_parts, pool_land,
    sums_model, sums_map, sums_heads, sums_ff,
    grads, first_low, last_low, low_in, high_in, tap_grad_ref, tall_sum, few_sum, few_packed,
    halo_send, halo_recv, local_sem,
    proj_sems, mlp_sems, in_sems, out_sems, share_sems, attn_sems, branch_sems, pool_sems, pair_sems,
    staging, stage_sem, job_sources, job_scratch,
):
    dqkv, dkv_send, proj_flat = pre_grad, kv_own, mlp_flat
    ring = Ring()
    count, d, t = ring.count, ring.d, ring.t
    data = lax.axis_size("dp")
    stages = bits_of(data)
    rows, model = patches_ref.shape
    half_rows, width = queries.shape
    heads = width // HEAD_DIM
    scale = HEAD_DIM**-0.5
    partner = d + 1 - 2 * lax.rem(d, 2)
    map_rows, map_cols, channels = own_map.shape
    rim = KERNEL // 2
    lane_blocks = channels // LANES
    inner = slice(SUB, SUB + map_cols)

    meet([lax.rem(d + k, data) for k in range(1, data)])
    load = pltpu.make_async_copy(
        conv_grad_ref, grads.at[pl.ds(rim, map_rows), pl.ds(SUB, map_cols)], local_sem
    )
    load.start()
    map_jobs = []
    for half, scratch, top in zip((half1_ref, half2_ref), job_scratch[:2], (False, True)):
        landings = [half] + list(scratch[: stages - 1])
        job = Halving(None, landings, scratch[stages - 1], scratch[stages], top)
        job.staging = (staging, stage_sem)
        map_jobs.append(job)
    jobs = [
        Halving(source, scratch[:stages], scratch[stages], scratch[stages + 1], top)
        for source, scratch, top in zip(job_sources, job_scratch[2:], JOB_ORDERS)
    ]
    fc1_job, fc2_job, qkv_job, out_job, adapt_job = jobs
    gfc1, gfc2, gqkv, gout, gadapt = job_sources

    def step_map_jobs():
        for job, out in zip(map_jobs, (red1_ref, red2_ref)):
            job.step(out)

    def step_jobs(*which):
        for index in which:
            jobs[index].step(job_outs[index])

    for edge in (0, SUB + map_cols):
        grads[:, edge : edge + SUB, :] = jnp.zeros(
            (map_rows + 2 * rim, SUB, channels), jnp.float32
        )
    sums_model[...] = jnp.zeros_like(sums_model)
    sums_map[...] = jnp.zeros_like(sums_map)
    sums_heads[...] = jnp.zeros_like(sums_heads)
    sums_ff[...] = jnp.zeros_like(sums_ff)
    load.wait()
    route = halo_route()
    first_low[...] = grads[rim : 2 * rim, inner, :].astype(jnp.bfloat16)
    last_low[...] = grads[map_rows : map_rows + rim, inner, :].astype(jnp.bfloat16)
    halo = halo_copies(route, first_low, last_low, low_in, high_in, halo_send, halo_recv)
    halo_start(route, halo)
    for job in map_jobs:
        job.begin(1)

    attn = attn_ref[...]
    need(9)
    own_keys = jnp.dot(attn, wqkv_ref[1], preferred_element_type=jnp.float32).astype(jnp.bfloat16)
    own_values = (
        jnp.dot(attn, wqkv_ref[2], preferred_element_type=jnp.float32) + qv_bias[1:2, :]
    ).astype(jnp.bfloat16)
    kv_own[:, 0:width] = own_keys
    kv_own[:, width : 2 * width] = own_values

    def pair_copy(source, target, slot):
        return pltpu.make_async_remote_copy(
            source, target, pair_sems.at[0, slot], pair_sems.at[1, slot],
            device_id=(partner, t), device_id_type=MESH_ID,
        )

    pair_copy(kv_own, kv_other, 0).start()
    need(5)
    ring.give_start(branch_parts, branch_land, branch_sems)
    queries[...] = (
        jnp.dot(attn, wqkv_ref[0], preferred_element_type=jnp.float32) + qv_bias[0:1, :]
    ).astype(jnp.bfloat16)
    keys_all[0:half_rows, :] = own_keys
    values_all[0:half_rows, :] = own_values
    pair_copy(kv_own, kv_other, 0).wait()
    keys_all[half_rows : 2 * half_rows, :] = kv_other[:, 0:width]
    values_all[half_rows : 2 * half_rows, :] = kv_other[:, width : 2 * width]
    live = live_ref[...] > 0.5
    for h in range(heads):
        here = slice(h * HEAD_DIM, (h + 1) * HEAD_DIM)
        raw = contract_cols(queries[:, here], keys_all[:, here]) * scale
        scores = jnp.where(live, raw, masked_score)
        grown = jnp.exp(scores - jnp.max(scores, axis=-1, keepdims=True))
        prob = grown * (1.0 / jnp.sum(grown, axis=-1, keepdims=True))
        probs[h] = prob
        attended[:, here] = jnp.dot(
            prob.astype(jnp.bfloat16), values_all[:, here], preferred_element_type=jnp.float32
        ).astype(jnp.bfloat16)
    need(11)
    fill_parts(parts, jnp.dot(attended[...], wout_ref[...], preferred_element_type=jnp.float32))
    ring.give_start(parts, landing, proj_sems)

    need(2)
    need(17)
    need(4)
    need(29)
    need(28)
    need(30)
    hidden_grad[...] = contract_cols(given_ref[...], wfc2_ref[...])
    for pair in range(map_rows // 2):
        half = map_cols // 2
        spread = jnp.dot(
            spread_ref[...],
            grad_pooled_ref[pair * half : (pair + 1) * half, :],
            precision=lax.Precision.HIGHEST,
            preferred_element_type=jnp.float32,
        )
        for i in range(2):
            hires_grad_ref[2 * pair + i] = spread
    map_refs = (low_map, own_map, high_map)
    tap_rows(grads, map_refs, tap_grad_ref, map_rows, map_cols, (0, lane_blocks // 2))
    ring.give_finish(parts, landing, proj_sems)
    inputs = patches_ref[...].astype(jnp.float32)
    middle = inputs + (ring.total(parts, landing) + as_row(out_bias))
    middle_keep[...] = middle
    xhat, _ = norm_parts(middle, vit_eps)
    shared[t] = (xhat * as_row(ln2_gain) + as_row(ln2_bias)).astype(jnp.bfloat16)
    ring.share_start(shared, mlp_sems)

    ring.give_finish(branch_parts, branch_land, branch_sems)
    branch = ring.total(branch_parts, branch_land) + as_row(pw2_bias)
    need(3)
    pooled = (map_mean_ref[...] + as_row(layer_scale) * branch).astype(jnp.bfloat16)
    pooled_grad = grad_pooled_ref[...]
    sums_map[0:1, :] = 4.0 * row_sum(
        (as_row(layer_scale) * (pooled_grad * 0.25)).astype(jnp.bfloat16).astype(jnp.float32)
    )
    sums_map[1:2, :] = row_sum(pooled_grad * branch)
    per_peer = channels // count
    place = lax.broadcasted_iota(jnp.int32, (channels, per_peer), 0)
    for j in range(count):
        choose = jnp.where(place == pick_ref[j : j + 1, :], 1.0, 0.0).astype(jnp.bfloat16)
        pool_parts[j] = jnp.dot(pooled, choose, preferred_element_type=jnp.float32).astype(
            jnp.bfloat16
        )
    ring.give_start(pool_parts, pool_land, pool_sems)
    need(19)
    adapted = (
        jnp.dot(pooled, wadapt_ref[...], preferred_element_type=jnp.float32) + as_row(adapt_bias)
    )
    upstream = upstream_keep[...].astype(jnp.float32)
    sums_model[5:6, :] = row_sum(upstream)
    sums_model[6:7, :] = row_sum(
        (upstream * as_row(adapt_gain)).astype(jnp.bfloat16).astype(jnp.float32)
    )
    sums_model[7:8, :] = row_sum(upstream * adapted)
    adapted_part = as_row(adapt_gain) * adapted
    step_map_jobs()
    tap_rows(grads, map_refs, tap_grad_ref, map_rows, map_cols, (lane_blocks // 2, lane_blocks))
    taps = KERNEL * KERNEL
    tap_grad_ref[taps : taps + 3, :] = sums_conv[0:3, :]
    tap_grad_ref[taps + 3 : taps + 5, :] = sums_map[0:2, :]
    tap_grad_ref[taps + 5 : taps + 6, :] = pw1_sums[...]
    tap_grad_ref[taps + 6 : taps + 7, :] = jnp.zeros((1, channels), jnp.float32)
    tall_sum.piece = lambda m: tap_grad_ref.at[
        :, pl.ds(pl.multiple_of(window_start(m, channels, data), LANES), 2 * LANES)
    ]
    tall_sum.start()

    need(15)
    ring.share_finish(shared, mlp_sems)
    mlp_flat[...] = flat_low(shared)
    units = wfc1_ref.shape[1]
    block = 256
    for first in range(0, units, block):
        cols = slice(first, first + block)
        pre = (
            jnp.dot(mlp_flat[...], wfc1_ref[:, cols], preferred_element_type=jnp.float32)
            + as_row(fc1_bias)[:, cols]
        )
        below_curve = 0.5 + 0.5 * lax.erf(pre * ROOT_HALF)
        slope = below_curve + pre * jnp.exp(-0.5 * pre * pre) * NORMAL_PEAK
        hidden[:, cols] = (pre * below_curve).astype(jnp.bfloat16)
        pre_low = (hidden_grad[:, cols] * slope).astype(jnp.bfloat16)
        pre_grad[:, cols] = pre_low
        sums_ff[0:1, cols] = row_sum(pre_low.astype(jnp.float32))
    fill_parts(parts, contract_cols(pre_grad[:, 0:units], wfc1_ref[...]))
    ring.give_start(parts, landing, in_sems)
    fill_parts(
        out_parts, jnp.dot(hidden[...], wfc2_ref[...], preferred_element_type=jnp.float32)
    )
    ring.give_start(out_parts, out_land, out_sems)

    for first in range(0, model, block):
        cols = slice(first, first + block)
        fill_rows(gfc1, first, contract_rows(mlp_flat[:, cols], pre_grad[:, 0:units]))
    fc1_job.begin()
    for first in range(0, model, block):
        cols = slice(first, first + block)
        fill_rows(gfc2, first, contract_rows(given_ref[:, cols], hidden[...]))
    fc2_job.begin()
    halo_finish(route, halo)

    @pl.when(jnp.logical_not(route[3]))
    def _():
        grads[0:rim, inner, :] = jnp.zeros((rim, map_cols, channels), jnp.float32)

    @pl.when(jnp.logical_not(route[2]))
    def _():
        grads[rim + map_rows : 2 * rim + map_rows, inner, :] = jnp.zeros(
            (rim, map_cols, channels), jnp.float32
        )

    need(31)
    halo_store(route, grads, low_in, high_in, map_rows, map_cols, rim)

    def emit(e, i, tile, lanes, value):
        hires_grad_ref[i, tile * SUB : (tile + 1) * SUB, lanes] += value

    third = lane_blocks // 3
    conv_rows(grads, taps_ref, map_rows, map_cols, (0, third), True, emit)
    ring.give_finish(parts, landing, in_sems)
    mlp_in_grad = ring.total(parts, landing)
    middle = middle_keep[...]
    xhat, rs = norm_parts(middle, vit_eps)
    sums_model[3:4, :] = row_sum(mlp_in_grad * xhat)
    sums_model[4:5, :] = row_sum(mlp_in_grad)
    middle_grad = upstream + norm_pull(mlp_in_grad, xhat, rs, as_row(ln2_gain))
    grad_patches_ref[...] = middle_grad
    proj_low = middle_grad.astype(jnp.bfloat16)
    sums_model[2:3, :] = row_sum(proj_low.astype(jnp.float32))
    shared[t] = proj_low
    ring.share_start(shared, share_sems)

    tall_sum.share(tall_data)
    step_map_jobs()
    step_jobs(0, 1)
    conv_rows(grads, taps_ref, map_rows, map_cols, (third, 2 * third), True, emit)
    ring.give_finish(pool_parts, pool_land, pool_sems)
    pool_land[t] = pool_parts[t]
    adapt_grad = (given_ref[...].astype(jnp.float32) * as_row(adapt_gain)).astype(jnp.bfloat16)
    fill_rows(gadapt, 0, contract_rows(flat_low(pool_land), adapt_grad))
    adapt_job.begin()
    ring.give_finish(out_parts, out_land, out_sems)
    vit_out = middle + (ring.total(out_parts, out_land) + as_row(fc2_bias))
    joined_ref[...] = (vit_out + adapted_part).astype(jnp.bfloat16)

    ring.share_finish(shared, share_sems)
    proj_flat[...] = flat_low(shared)
    attended_grad = contract_cols(proj_flat[...], wout_ref[...]).astype(jnp.bfloat16)
    for h in range(heads):
        here = slice(h * HEAD_DIM, (h + 1) * HEAD_DIM)
        there = slice(width + h * HEAD_DIM, width + (h + 1) * HEAD_DIM)
        head_grad = attended_grad[:, here]
        prob = probs[h]
        value_part = contract_rows(prob.astype(jnp.bfloat16), head_grad)
        prob_grad = contract_cols(head_grad, values_all[:, here])
        dot_rows = jnp.sum(prob * prob_grad, axis=-1, keepdims=True)
        score_grad = (prob * (prob_grad - dot_rows)).astype(jnp.bfloat16)
        dqkv[:, here] = (
            jnp.dot(score_grad, keys_all[:, here], preferred_element_type=jnp.float32) * scale
        ).astype(jnp.bfloat16)
        key_part = contract_rows(score_grad, queries[:, here]) * scale
        dkv_send[:, here] = key_part[half_rows:].astype(jnp.bfloat16)
        dkv_send[:, there] = value_part[half_rows:].astype(jnp.bfloat16)
        hidden_grad[:, here] = key_part[:half_rows]
        hidden_grad[:, there] = value_part[:half_rows]
    pair_copy(dkv_send, dkv_other, 1).start()
    for first in range(0, model, block):
        cols = slice(first, first + block)
        fill_rows(gout, first, contract_rows(proj_flat[:, cols], attended[...]))
    out_job.begin()
    pair_copy(dkv_send, dkv_other, 1).wait()
    kv_grad = (hidden_grad[:, 0 : 2 * width] + dkv_other[...].astype(jnp.float32)).astype(
        jnp.bfloat16
    )
    dqkv[:, width : 3 * width] = kv_grad
    attn_grad = contract_cols(dqkv[:, 0:width], wqkv_ref[0])
    for part in (1, 2):
        attn_grad += contract_cols(dqkv[:, part * width : (part + 1) * width], wqkv_ref[part])
    fill_parts(parts, attn_grad)
    ring.give_start(parts, landing, attn_sems)

    sums_heads[0:1, :] = row_sum(dqkv[:, 0:width].astype(jnp.float32))
    sums_heads[1:2, :] = row_sum(dqkv[:, 2 * width : 3 * width].astype(jnp.float32))
    for first in range(0, model, block):
        cols = slice(first, first + block)
        fill_rows(gqkv, first, contract_rows(attn_ref[:, cols], dqkv[:, 0 : 3 * width]))
    qkv_job.begin()
    step_jobs(0, 1, 4, 3, 2)
    conv_rows(grads, taps_ref, map_rows, map_cols, (2 * third, lane_blocks), True, emit)
    ring.give_finish(parts, landing, attn_sems)
    attn_in_grad = ring.total(parts, landing)
    xhat, rs = norm_parts(inputs, vit_eps)
    sums_model[0:1, :] = row_sum(attn_in_grad * xhat)
    sums_model[1:2, :] = row_sum(attn_in_grad)
    zero = jnp.zeros((SUB, LANES), jnp.float32)
    for m in range(data):
        for lane, (row, source) in enumerate(((0, sums_model), (0, sums_ff), (SUB, sums_heads))):
            first = lane_start(m, source.shape[1], data)
            side = LANES * (lane % 2)
            few_packed[m, row : row + SUB, side : side + LANES] = source[
                :, first : first + LANES
            ]
        few_packed[m, SUB : 2 * SUB, LANES : 2 * LANES] = zero
    few_sum.piece = lambda m: few_packed.at[m]
    few_sum.start()
    grad_patches_ref[...] += norm_pull(attn_in_grad, xhat, rs, as_row(ln1_gain))
    step_map_jobs()
    step_jobs(0, 1, 4, 3, 2)
    few_sum.share(few_data)
    for _ in range(stages):
        step_map_jobs()
        step_jobs(0, 1, 4, 3, 2)
    tall_sum.finish(tall_ring)
    few_sum.finish(few_ring)


def last_block(
    patches, attn_all, grad_all, map_mean, grad_pooled, branch_partial, half1, half2,
    ln1_gain, w_qkv, qv_bias, w_out, out_bias, ln2_gain, ln2_bias,
    w_fc1, fc1_bias, w_fc2, fc2_bias, w_adapt, adapt_bias, adapt_gain, pw2_bias, layer_scale,
    key_live, grad_own, conv_grad, hires, low_rim, high_rim, taps, sums_conv, pw1_sums,
):
    count = lax.axis_size("tensor")
    data = lax.axis_size("dp")
    stages = bits_of(data)
    rows, model = patches.shape
    half_rows = rows * count
    width = w_out.shape[0]
    heads = width // HEAD_DIM
    units = w_fc1.shape[1]
    map_rows, map_cols, channels = hires.shape
    rim = KERNEL // 2
    stage_rows = channels // (data * count)
    place = np.arange(channels // count)
    pick = np.stack(
        [(place // stage_rows * count + j) * stage_rows + place % stage_rows for j in range(count)]
    ).astype(np.int32)
    near = np.arange(map_cols)[:, None] // 2 == np.arange(map_cols // 2)[None, :]
    spread = jnp.asarray(np.where(near, 0.25, 0.0), jnp.float32)
    f32, low = jnp.float32, jnp.bfloat16

    def vmem(*shape, dtype=low):
        return pltpu.VMEM(shape, dtype)

    shard = vmem(count, rows, model)
    rim_low = vmem(rim, map_cols, channels)
    tall = (KERNEL * KERNEL + SUB - 1) // SUB * SUB
    tall_block, few_block = (tall, 2 * LANES), (2 * SUB, 2 * LANES)
    dma = pltpu.SemaphoreType.DMA
    scratch = [
        vmem(2 * half_rows, width), vmem(2 * half_rows, width),
        vmem(half_rows, 2 * width), vmem(half_rows, 2 * width), vmem(half_rows, width),
        vmem(half_rows, units, dtype=f32), vmem(heads, half_rows, 2 * half_rows, dtype=f32),
        vmem(half_rows, width), vmem(rows, model, dtype=f32),
        vmem(half_rows, units), vmem(half_rows, max(units, 3 * width)),
        vmem(half_rows, 2 * width), vmem(half_rows, model),
        shard, shard, shard, shard, shard,
        vmem(count, rows, channels),
        vmem(count, rows, channels // count), vmem(count, rows, channels // count),
        vmem(SUB, model, dtype=f32), vmem(SUB, channels, dtype=f32),
        vmem(SUB, width, dtype=f32), vmem(SUB, units, dtype=f32),
        vmem(map_rows + 2 * rim, map_cols + 2 * SUB, channels, dtype=f32),
        rim_low, rim_low, rim_low, rim_low, vmem(tall, channels, dtype=f32),
        vmem(data, *few_block, dtype=f32),
        dma((2,)), dma((2,)), dma,
    ] + [dma((2, count))] * 9 + [vmem(*half1.shape[1:]), dma]
    fixed = len(scratch)
    sum_place = fixed - 15
    sources = [
        (data, model // data, units), (data, model // data, units),
        (data, model // data, 3 * width), (data, model // data, width),
        (data, channels // (count * data), model),
    ]
    n_jobs = len(sources)
    scratch += [vmem(*shape) for shape in sources]
    map_shape = half1.shape
    sizes = []
    for shape in [(data, map_shape[1], map_shape[2])] * 2 + sources:
        first = data // 4 if len(sizes) < 2 else data // 2
        more = halving_scratch(*shape, first)
        sizes.append(len(more))
        scratch += more
    n_in, n_out, few_outs = 35, 9 + n_jobs, 9
    sum_scratch = small_sum_scratch(data, count, tall) + small_sum_scratch(data, count, 2 * SUB)
    n_sum = len(sum_scratch)
    scratch += sum_scratch

    def kernel(need, *refs):
        ins, outs, rest = refs[:n_in], refs[n_in : n_in + n_out], refs[n_in + n_out :]
        rest, sum_refs = rest[:-n_sum], rest[-n_sum:]
        own, more = list(rest[:fixed]), list(rest[fixed + n_jobs :])
        own[sum_place:sum_place] = [
            SmallSum(*sum_refs[: n_sum // 2]), SmallSum(*sum_refs[n_sum // 2 :])
        ]
        job_scratch = []
        for size in sizes:
            job_scratch.append(more[:size])
            more = more[size:]
        last_kernel(
            need, *ins, *outs[:few_outs], outs[few_outs:], *own, rest[fixed : fixed + n_jobs], job_scratch
        )

    def out(*shape, dtype=f32):
        return jax.ShapeDtypeStruct(shape, dtype)

    inputs = (
        patches, attn_all, grad_all, map_mean, grad_pooled,
        branch_partial.reshape(count, rows, channels), half1, half2,
        ln1_gain, w_qkv, qv_bias, w_out, out_bias, ln2_gain, ln2_bias,
        w_fc1, fc1_bias, w_fc2, fc2_bias, w_adapt, adapt_bias, adapt_gain,
        pw2_bias, layer_scale, key_live, jnp.asarray(pick), grad_own,
        conv_grad.reshape(map_rows, map_cols, channels),
        hires, low_rim, high_rim, taps, spread, sums_conv, pw1_sums,
    )
    later = (9, 5, 11, 2, 17, 4, 29, 28, 30, 3, 19, 15, 31)
    specs, buffers, run = with_loads(kernel, inputs, later)
    for index in (6, 7, 27):
        specs[index] = pl.BlockSpec(memory_space=pl.ANY)
    return pl.pallas_call(
        run,
        out_shape=(
            out(rows, model, dtype=low), out(rows, model),
            out(*map_shape[1:]), out(*map_shape[1:]),
            out(map_rows, map_cols, channels),
            out(*tall_block), out(*tall_block), out(*few_block), out(*few_block),
        )
        + tuple(out(*shape[1:]) for shape in sources),
        in_specs=specs,
        out_specs=(VMEM_SPEC,) * n_out,
        scratch_shapes=scratch + buffers,
        compiler_params=kernel_params(3),
        name="last_block",
    )(*inputs)


def local(
    patches,
    hires,
    valid_rows,
    ln1_gain,
    ln1_bias,
    w_qkv,
    qv_bias,
    w_out,
    out_bias,
    ln2_gain,
    ln2_bias,
    w_fc1,
    fc1_bias,
    w_fc2,
    fc2_bias,
    dw_weight,
    dw_bias,
    lnc_gain,
    lnc_bias,
    w_pw1,
    pw1_bias,
    w_pw2,
    pw2_bias,
    layer_scale,
    w_adapt,
    adapt_bias,
    adapt_gain,
    grad_out,
):
    data_index = lax.axis_index("dp")
    image_index = data_index // IMG_SPAN
    map_cols, channels = hires.shape[1:]
    patch_rows, model = patches.shape
    half_rows = patch_rows * lax.axis_size("tensor")
    normed_low, conv_flat, low_rim, high_rim, attn_own, grad_all, map_mean = conv_forward(
        hires, dw_weight, dw_bias, lnc_gain, lnc_bias, patches, grad_out, ln1_gain, ln1_bias
    )
    conv_grad, branch_partial, half1, half2, pw1_sums, grad_pooled, attn_all, sums_conv = map_block(
        normed_low, w_pw1, pw1_bias, w_pw2, grad_all, w_adapt, adapt_gain, layer_scale,
        conv_flat, lnc_gain, attn_own, map_cols,
    )
    own_first = data_index % IMG_SPAN * half_rows
    other_first = (1 - data_index % IMG_SPAN) * half_rows
    key_place = jnp.concatenate(
        [own_first + jnp.arange(half_rows), other_first + jnp.arange(half_rows)]
    )
    image_valid = jnp.sum(jnp.where(jnp.arange(valid_rows.shape[0]) == image_index, valid_rows, 0))
    key_live = (key_place // SIDE < image_valid).astype(jnp.float32)[None]
    (
        joined_out, grad_patches, reduced_pw1, reduced_pw2, grad_hires,
        tall_ring, tall_data, few_ring, few_data,
        reduced_fc1, reduced_fc2, reduced_qkv, reduced_out, reduced_adapt,
    ) = last_block(
        patches, attn_all, grad_all, map_mean, grad_pooled, branch_partial, half1, half2,
        ln1_gain, w_qkv, qv_bias, w_out, out_bias, ln2_gain, ln2_bias,
        w_fc1, fc1_bias, w_fc2, fc2_bias, w_adapt, adapt_bias, adapt_gain, pw2_bias, layer_scale,
        key_live, grad_out, conv_grad, hires, low_rim, high_rim, dw_weight, sums_conv, pw1_sums,
    )
    width = w_out.shape[0]
    sums = (tall_ring, tall_data, few_ring, few_data)
    results = (
        joined_out, grad_patches, grad_hires, reduced_pw1, reduced_pw2, reduced_fc1, reduced_fc2,
        reduced_qkv, reduced_out, reduced_adapt,
    )
    (
        grad_dw_weight,
        grad_lnc_gain, grad_lnc_bias, grad_dw_bias, grad_pw2_bias, grad_layer_scale,
        grad_ln1_gain, grad_ln1_bias, grad_out_bias, grad_ln2_gain, grad_ln2_bias, grad_fc2_bias,
        grad_adapt_bias, grad_adapt_gain,
        grad_pw1_bias, grad_fc1_bias, grad_qv_bias,
        joined_out, grad_patches, grad_hires, reduced_pw1, reduced_fc1, reduced_adapt,
        reduced_pw2, reduced_fc2, reduced_out, reduced_qkv,
    ) = small_outputs(sums, results, channels, model, w_fc1.shape[1], width)
    return (
        joined_out,
        grad_patches,
        grad_hires,
        grad_ln1_gain,
        grad_ln1_bias,
        reduced_qkv,
        grad_qv_bias,
        reduced_out,
        grad_out_bias,
        grad_ln2_gain,
        grad_ln2_bias,
        reduced_fc1,
        grad_fc1_bias,
        reduced_fc2,
        grad_fc2_bias,
        grad_dw_weight.T,
        grad_dw_bias,
        grad_lnc_gain,
        grad_lnc_bias,
        reduced_pw1,
        grad_pw1_bias,
        reduced_pw2.T,
        grad_pw2_bias,
        grad_layer_scale,
        reduced_adapt,
        grad_adapt_bias,
        grad_adapt_gain,
    )


def solution(mesh):
    return jax.shard_map(
        local,
        mesh=mesh,
        in_specs=(
            P(("dp", "tensor"), None),
            P(("dp", "tensor"), None, None),
            P(),
            P(),
            P(),
            P(None, None, "tensor"),
            P(None, "tensor"),
            P("tensor", None),
            P(),
            P(),
            P(),
            P(None, "tensor"),
            P("tensor"),
            P("tensor", None),
            P(),
            P(),
            P(),
            P(),
            P(),
            P(None, "tensor"),
            P("tensor"),
            P("tensor", None),
            P(),
            P(),
            P(),
            P(),
            P(),
            P(("dp", "tensor"), None),
        ),
        out_specs=(
            P(("dp", "tensor"), None),
            P(("dp", "tensor"), None),
            P(("dp", "tensor"), None, None),
            P(("dp", "tensor")),
            P(("dp", "tensor")),
            P(None, "dp", "tensor"),
            P(None, ("tensor", "dp")),
            P("tensor", "dp"),
            P(("dp", "tensor")),
            P(("dp", "tensor")),
            P(("dp", "tensor")),
            P("dp", "tensor"),
            P(("tensor", "dp")),
            P("tensor", "dp"),
            P(("dp", "tensor")),
            P(None, ("dp", "tensor")),
            P(("dp", "tensor")),
            P(("dp", "tensor")),
            P(("dp", "tensor")),
            P("dp", "tensor"),
            P(("tensor", "dp")),
            P("tensor", "dp"),
            P(("dp", "tensor")),
            P(("dp", "tensor")),
            P(("dp", "tensor"), None),
            P(("dp", "tensor")),
            P(("dp", "tensor")),
        ),
        check_vma=False,
    )
```

```python
from functools import partial

import jax
import jax.numpy as jnp
import numpy as np
from jax import lax
from jax.experimental import pallas as pl
from jax.experimental.pallas import tpu as pltpu
from jax.sharding import PartitionSpec as P

HEAD_DIM = 64
SIDE = 24
KERNEL = 7
IMG_SPAN = 2


vit_eps = 1e-05
map_eps = 1e-06
masked_score = -1e30
ROOT_HALF = 0.7071067811865476
NORMAL_PEAK = 0.3989422804014327


def contract_rows(left_side, right_side):
    return lax.dot_general(
        left_side, right_side, (((0,), (0,)), ((), ())), preferred_element_type=jnp.float32
    )


def contract_cols(left_side, right_side):
    return lax.dot_general(
        left_side, right_side, (((1,), (1,)), ((), ())), preferred_element_type=jnp.float32
    )


def bits_of(count):
    return count.bit_length() - 1


class Halving:
    def __init__(self, source, landings, send, recv, top_first):
        self.count = lax.axis_size("dp")
        self.d, self.t = lax.axis_index("dp"), lax.axis_index("tensor")
        self.source, self.landings = source, landings
        self.send, self.recv, self.top_first = send, recv, top_first
        self.stages = bits_of(self.count)
        self.at = 0
        self.staging = None

    def begin(self, stage=0):
        self.at = stage
        self.start(stage)

    def step(self, out=None):
        if self.at == self.stages:
            return
        self.finish(self.at, out if self.at == self.stages - 1 else None)
        self.at += 1
        if self.at < self.stages:
            self.start(self.at)

    def plan(self, stage):
        here = self.source if stage == 0 else self.landings[stage - 1]
        half = self.count >> (stage + 1)
        top = self.top_first and stage > 0
        bit = self.stages - stage if top else stage
        own = lax.rem(self.d // (1 << bit), 2)
        partner = self.d + (1 - 2 * own) * (1 << bit)
        base = self.count - 2 * half

        def place(i, value):
            return value * half + i if top else 2 * i + value

        def copy(i):
            return pltpu.make_async_remote_copy(
                here.at[place(i, 1 - own)], self.landings[stage].at[i],
                self.send.at[base + i], self.recv.at[base + i],
                device_id=(partner, self.t), device_id_type=MESH_ID,
            )

        return here, half, own, place, copy

    def start(self, stage):
        here, half, own, place, copy = self.plan(stage)

        def body(i, carry):
            copy(i).start()
            return carry

        lax.fori_loop(0, half, body, 0)

    def finish(self, stage, out=None):
        here, half, own, place, copy = self.plan(stage)
        landing = self.landings[stage]
        rows = landing.shape[1]

        def body(i, carry):
            copy(i).wait()
            kept = here.at[place(i, own)]
            if self.staging is not None and stage == 1:
                load = pltpu.make_async_copy(kept, *self.staging)
                load.start()
                load.wait()
                kept = self.staging[0]
            total = kept[...].astype(jnp.float32) + landing[i].astype(jnp.float32)
            if out is None:
                landing[i] = total.astype(jnp.bfloat16)
            else:
                out[...] = total
            return carry

        lax.fori_loop(0, half, body, 0)


def halving_scratch(count, rows, cols, half):
    landings = []
    while half >= 1:
        landings.append(pltpu.VMEM((half, rows, cols), jnp.bfloat16))
        half //= 2
    return landings + [pltpu.SemaphoreType.DMA((count - 1,))] * 2


class Ring:
    def __init__(self):
        self.count = lax.axis_size("tensor")
        self.d, self.t = lax.axis_index("dp"), lax.axis_index("tensor")

    def at(self, k):
        return lax.rem(self.t + k, self.count)

    def share_copy(self, buffer, sems, k, source):
        return pltpu.make_async_remote_copy(
            buffer.at[source], buffer.at[source], sems.at[0, k], sems.at[1, source],
            device_id=(self.d, self.at(k)), device_id_type=MESH_ID,
        )

    def share_start(self, buffer, sems):
        for k in range(1, self.count):
            self.share_copy(buffer, sems, k, self.t).start()

    def share_finish(self, buffer, sems):
        for k in range(1, self.count):
            self.share_copy(buffer, sems, k, self.t).wait_send()
        for k in range(1, self.count):
            self.share_copy(buffer, sems, k, self.at(k)).wait_recv()

    def give_copy(self, parts, landing, sems, k, slot, part):
        return pltpu.make_async_remote_copy(
            parts.at[part], landing.at[slot], sems.at[0, k], sems.at[1, slot],
            device_id=(self.d, self.at(k)), device_id_type=MESH_ID,
        )

    def give_start(self, parts, landing, sems):
        for k in range(1, self.count):
            self.give_copy(parts, landing, sems, k, self.t, self.at(k)).start()

    def give_finish(self, parts, landing, sems):
        for k in range(1, self.count):
            self.give_copy(parts, landing, sems, k, self.t, self.at(k)).wait_send()
        for k in range(1, self.count):
            self.give_copy(parts, landing, sems, k, self.at(k), self.at(k)).wait_recv()


    def halves(self):
        half = self.t // 2
        buddy = self.t + 1 - 2 * lax.rem(self.t, 2)
        at_middle = lax.rem(self.t + half, 2) == 1
        return buddy, 2 - 2 * half, 2 - half, at_middle

    def pass_copy(self, source, target, send, recv, device):
        return pltpu.make_async_remote_copy(
            source, target, send, recv, device_id=(self.d, device), device_id_type=MESH_ID
        )

    def spread_copy(self, buffer, sems, j, slot, device):
        return self.pass_copy(buffer.at[j], buffer.at[j], sems.at[0, slot], sems.at[1, j], device)

    def spread_start(self, buffer, sems):
        buddy, _, middle, _ = self.halves()
        self.spread_copy(buffer, sems, self.t, 0, middle).start()
        self.spread_copy(buffer, sems, self.t, 1, buddy).start()

    def spread_relay(self, buffer, sems):
        buddy, far, middle, at_middle = self.halves()

        @pl.when(at_middle)
        def _():
            for i, j in enumerate((middle, 2 * far + 1 - middle)):
                copy = self.spread_copy(buffer, sems, j, 2 + i, buddy)
                copy.wait_recv()
                copy.start()

    def spread_finish(self, buffer, sems):
        buddy, far, middle, at_middle = self.halves()
        self.spread_copy(buffer, sems, self.t, 0, middle).wait_send()
        self.spread_copy(buffer, sems, self.t, 1, buddy).wait_send()
        self.spread_copy(buffer, sems, buddy, 1, buddy).wait_recv()

        @pl.when(at_middle)
        def _():
            for i in range(2):
                self.spread_copy(buffer, sems, far + i, 2 + i, buddy).wait_send()

        @pl.when(jnp.logical_not(at_middle))
        def _():
            for i in range(2):
                self.spread_copy(buffer, sems, far + i, 2 + i, buddy).wait_recv()

    def sum_copies(self, parts, landing, sems):
        buddy, far, _, _ = self.halves()
        to_buddy = self.pass_copy(
            parts.at[buddy], landing.at[0], sems.at[0, 0], sems.at[1, 0], buddy
        )
        inward = [
            self.pass_copy(
                parts.at[far + i], landing.at[2 + i], sems.at[0, 1 + i], sems.at[1, 2 + i], buddy
            )
            for i in range(2)
        ]
        across = [
            self.pass_copy(
                parts.at[far + i], landing.at[1], sems.at[0, 1 + i], sems.at[1, 1], far + i
            )
            for i in range(2)
        ]
        return to_buddy, inward, across

    def sum_start(self, parts, landing, sems):
        to_buddy, inward, _ = self.sum_copies(parts, landing, sems)

        @pl.when(jnp.logical_not(self.halves()[3]))
        def _():
            for copy in inward:
                copy.start()

        to_buddy.start()

    def sum_relay(self, parts, landing, sems):
        _, far, _, at_middle = self.halves()
        _, inward, across = self.sum_copies(parts, landing, sems)

        @pl.when(at_middle)
        def _():
            for i in range(2):
                inward[i].wait_recv()
                parts[far + i] = (
                    parts[far + i].astype(jnp.float32) + landing[2 + i].astype(jnp.float32)
                ).astype(jnp.bfloat16)
                across[i].start()

    def sum_finish(self, parts, landing, sems):
        to_buddy, inward, across = self.sum_copies(parts, landing, sems)
        to_buddy.wait()
        at_middle = self.halves()[3]

        @pl.when(at_middle)
        def _():
            for copy in across:
                copy.wait_send()

        @pl.when(jnp.logical_not(at_middle))
        def _():
            for copy in inward:
                copy.wait_send()

        across[0].wait_recv()
        return (
            parts[self.t].astype(jnp.float32)
            + landing[0].astype(jnp.float32)
            + landing[1].astype(jnp.float32)
        )

    def total(self, parts, landing):
        value = parts[self.t].astype(jnp.float32)
        for k in range(1, self.count):
            value = value + landing[self.at(k)].astype(jnp.float32)
        return value


class SmallSum:
    def __init__(self, landed, shared, send, recv, sems):
        self.landed, self.shared = landed, shared
        self.send, self.recv, self.sems = send, recv, sems
        self.ring = Ring()
        self.count = lax.axis_size("dp")

    def copy(self, k, part, slot):
        ring = self.ring
        return pltpu.make_async_remote_copy(
            self.piece(part), self.landed.at[slot], self.send.at[k], self.recv.at[slot],
            device_id=(lax.rem(ring.d + k, self.count), ring.t), device_id_type=MESH_ID,
        )

    def start(self):
        def body(k, carry):
            self.copy(k, lax.rem(self.ring.d + k, self.count), self.ring.d).start()
            return carry

        lax.fori_loop(1, self.count, body, 0)

    def share(self, out):
        out[...] = self.piece(self.ring.d)[...]

        def body(k, carry):
            slot = lax.rem(self.ring.d + k, self.count)
            self.copy(k, slot, self.ring.d).wait_send()
            self.copy(k, slot, slot).wait_recv()
            out[...] += self.landed[slot]
            return carry

        lax.fori_loop(1, self.count, body, 0)
        self.shared[self.ring.t] = out[...]
        self.ring.share_start(self.shared, self.sems)

    def finish(self, out):
        self.ring.share_finish(self.shared, self.sems)
        total = self.shared[0]
        for j in range(1, self.ring.count):
            total = total + self.shared[j]
        out[...] = total


def small_sum_scratch(data, count, rows):
    block = (rows, 2 * LANES)
    return [
        pltpu.VMEM((data,) + block, jnp.float32),
        pltpu.VMEM((count,) + block, jnp.float32),
        pltpu.SemaphoreType.DMA((data,)), pltpu.SemaphoreType.DMA((data,)),
        pltpu.SemaphoreType.DMA((2, count)),
    ]


def norm_parts(values, epsilon):
    centered = values - jnp.mean(values, axis=-1, keepdims=True)
    variance = jnp.mean(centered * centered, axis=-1, keepdims=True)
    scale = lax.rsqrt(variance + epsilon)
    return centered * scale, scale


def norm_pull(grad, xhat, scale, gain):
    scaled = grad * gain
    return scale * (
        scaled
        - jnp.mean(scaled, axis=-1, keepdims=True)
        - xhat * jnp.mean(scaled * xhat, axis=-1, keepdims=True)
    )


def row_sum(values):
    return jnp.sum(values, axis=0, keepdims=True)


def flat_low(buffer):
    count, rows, cols = buffer.shape
    return buffer[...].astype(jnp.float32).reshape(count * rows, cols).astype(jnp.bfloat16)


def fill_rows(blocks, first, value):
    rows = blocks.shape[1]
    for c in range(value.shape[0] // rows):
        blocks[first // rows + c] = value[c * rows : (c + 1) * rows].astype(jnp.bfloat16)


def fill_parts(parts, value):
    count, rows, _ = parts.shape
    for j in range(count):
        parts[j] = value[j * rows : (j + 1) * rows].astype(jnp.bfloat16)


MESH_ID = pl.DeviceIdType.MESH
VMEM_SPEC = pl.BlockSpec(memory_space=pltpu.VMEM)
LANES = 128
SUB = 8
VMEM_BYTES = 125 * 512 * 1024


def kernel_params(collective_id=None):
    if collective_id is None:
        return pltpu.CompilerParams(vmem_limit_bytes=VMEM_BYTES)
    return pltpu.CompilerParams(
        vmem_limit_bytes=VMEM_BYTES, collective_id=collective_id, has_side_effects=True
    )


def halo_route():
    count = lax.axis_size("tensor")
    d, t = lax.axis_index("dp"), lax.axis_index("tensor")
    odd = lax.rem(d, IMG_SPAN)
    up = (d + (t + 1) // count, lax.rem(t + 1, count))
    down = (d - 1 + (t + count - 1) // count, lax.rem(t + count - 1, count))
    up_here = (t + 1) // count + odd < 2
    down_here = t + odd > 0
    return up, down, up_here, down_here


def seam_here():
    count = lax.axis_size("tensor")
    d, t = lax.axis_index("dp"), lax.axis_index("tensor")
    odd = lax.rem(d, IMG_SPAN)
    at_last = (t + 1) // count
    at_first = 1 - (t + count - 1) // count
    return at_last * (1 - odd) + at_first * odd


def meet(data_peers, across_seam=True):
    count = lax.axis_size("tensor")
    d, t = lax.axis_index("dp"), lax.axis_index("tensor")
    odd = lax.rem(d, IMG_SPAN)
    barrier = pltpu.get_barrier_semaphore()
    for k in range(1, count):
        pl.semaphore_signal(
            barrier, inc=1, device_id=(d, lax.rem(t + k, count)), device_id_type=MESH_ID
        )
    for peer in data_peers:
        pl.semaphore_signal(barrier, inc=1, device_id=(peer, t), device_id_type=MESH_ID)
    if not across_seam:
        pl.semaphore_wait(barrier, count - 1 + len(data_peers))
        return
    seam = seam_here()

    @pl.when(seam > 0)
    def _():
        pl.semaphore_signal(
            barrier, inc=1, device_id=(d + 1 - 2 * odd, count - 1 - t), device_id_type=MESH_ID
        )

    pl.semaphore_wait(barrier, count - 1 + len(data_peers) + seam)


def as_row(ref):
    return ref[...].reshape(1, ref.shape[0])


def halo_copies(route, first_rows, last_rows, low_ref, high_ref, send_sem, recv_sem):
    up, down, up_here, down_here = route
    to_up = pltpu.make_async_remote_copy(
        last_rows, low_ref, send_sem.at[0], recv_sem.at[0], device_id=up, device_id_type=MESH_ID
    )
    to_down = pltpu.make_async_remote_copy(
        first_rows, high_ref, send_sem.at[1], recv_sem.at[1], device_id=down, device_id_type=MESH_ID
    )
    return to_up, to_down


def halo_start(route, copies):
    @pl.when(route[2])
    def _():
        copies[0].start()

    @pl.when(route[3])
    def _():
        copies[1].start()


def halo_finish(route, copies):
    @pl.when(route[2])
    def _():
        copies[0].wait_send()
        copies[1].wait_recv()

    @pl.when(route[3])
    def _():
        copies[1].wait_send()
        copies[0].wait_recv()


def halo_store(route, extended, low_ref, high_ref, rows, cols, rim):
    @pl.when(route[3])
    def _():
        extended[0:rim, SUB : SUB + cols, :] = low_ref[...].astype(jnp.float32)

    @pl.when(route[2])
    def _():
        extended[rim + rows : 2 * rim + rows, SUB : SUB + cols, :] = high_ref[...].astype(
            jnp.float32
        )


def conv_rows(extended, taps_ref, rows, cols, blocks, flipped, emit):
    span = KERNEL * KERNEL - 1
    rim = KERNEL // 2
    tiles = cols // SUB
    inside = lax.broadcasted_iota(jnp.int32, (SUB, LANES), 0)

    def lane_block(block, carry):
        lanes = pl.ds(pl.multiple_of(block * LANES, LANES), LANES)
        for e in range(KERNEL):
            shift = e - rim
            taps = []
            for a in range(KERNEL):
                index = a * KERNEL + e
                taps.append(taps_ref[pl.ds(span - index if flipped else index, 1), lanes])
            first = 1 if shift >= 0 else 0
            last = tiles + 1 if shift <= 0 else tiles + 2
            before = [None] * rows
            for tile in range(first, last):
                cells = [
                    extended[r, SUB * tile : SUB * tile + SUB, lanes]
                    for r in range(rows + KERNEL - 1)
                ]
                for i in range(rows):
                    total = cells[i] * taps[0]
                    for a in range(1, KERNEL):
                        total = total + cells[i + a] * taps[a]
                    if shift == 0:
                        emit(e, i, tile - 1, lanes, total)
                        continue
                    turned = pltpu.roll(total, (SUB - shift) % SUB, 0)
                    if tile > first:
                        split = SUB - shift if shift > 0 else -shift
                        value = jnp.where(inside < split, before[i], turned)
                        emit(e, i, tile - 1 - first, lanes, value)
                    before[i] = turned
        return carry

    lax.fori_loop(blocks[0], blocks[1], lane_block, 0)


def tap_rows(grads, map_refs, tap_grad_ref, rows, cols, blocks):
    rim = KERNEL // 2
    low_ref, own_ref, high_ref = map_refs
    pairs = cols // (2 * SUB)
    inside = lax.broadcasted_iota(jnp.int32, (SUB, LANES), 0)

    def lane_block(block, carry):
        lanes = pl.ds(pl.multiple_of(block * LANES, LANES), LANES)
        for e in range(KERNEL):
            shift = e - rim
            sums = [None] * KERNEL
            for pair in range(pairs):
                here = slice(2 * SUB * pair, 2 * SUB * pair + 2 * SUB)
                cells = (
                    [low_ref[r, here, lanes] for r in range(rim)]
                    + [own_ref[r, here, lanes] for r in range(rows)]
                    + [high_ref[r, here, lanes] for r in range(rim)]
                )
                cells = [cell.astype(jnp.float32) for cell in cells]
                for i in range(rows):
                    first = SUB * (2 * pair + (0 if shift > 0 else 1))
                    count = 2 if shift == 0 else 3
                    given = [
                        grads[rim + i, first + SUB * k : first + SUB * k + SUB, lanes]
                        for k in range(count)
                    ]
                    if shift != 0:
                        turned = [pltpu.roll(tile, shift % SUB, 0) for tile in given]
                        split = shift if shift > 0 else SUB + shift
                        given = [
                            jnp.where(inside < split, turned[k], turned[k + 1]) for k in range(2)
                        ]
                    for a in range(KERNEL):
                        cell = cells[i + a]
                        term = cell[0:SUB] * given[0] + cell[SUB : 2 * SUB] * given[1]
                        sums[a] = term if sums[a] is None else sums[a] + term
            for a in range(KERNEL):
                tap_grad_ref[pl.ds(a * KERNEL + e, 1), lanes] = jnp.sum(
                    sums[a], axis=0, keepdims=True
                )
        return carry

    lax.fori_loop(blocks[0], blocks[1], lane_block, 0)


def conv_forward_kernel(
    own_ref, taps_ref, bias_1d, gain_1d, shift_1d, pool_ref, upstream_ref,
    normed_ref, conv_ref, low_ref, high_ref, given_ref, mean_ref,
    extended, vectors, given_all, send_sem, recv_sem, given_sems,
):
    rows, cols, channels = own_ref.shape
    rim = KERNEL // 2
    route = halo_route()
    ring = Ring()
    meet(())
    copies = halo_copies(
        route, own_ref.at[pl.ds(0, rim)], own_ref.at[pl.ds(rows - rim, rim)],
        low_ref, high_ref, send_sem, recv_sem,
    )
    halo_start(route, copies)
    given_all[ring.t] = upstream_ref[...]
    vectors[0:1, :] = as_row(bias_1d)
    vectors[1:2, :] = as_row(gain_1d)
    vectors[2:3, :] = as_row(shift_1d)
    bias_ref, gain_ref, shift_ref = vectors.at[0:1], vectors.at[1:2], vectors.at[2:3]
    quarter = pool_ref.shape[0]
    for pair in range(rows // 2):
        mean_ref[pair * quarter : (pair + 1) * quarter, :] = jnp.dot(
            pool_ref[...],
            own_ref[2 * pair : 2 * pair + 2].reshape(2 * cols, channels),
            preferred_element_type=jnp.float32,
        )
    for edge in (0, SUB + cols):
        extended[:, edge : edge + SUB, :] = jnp.zeros(
            (rows + 2 * rim, SUB, channels), jnp.float32
        )
    extended[rim : rim + rows, SUB : SUB + cols, :] = own_ref[...].astype(jnp.float32)
    halo_finish(route, copies)
    ring.share_start(given_all, given_sems)

    @pl.when(jnp.logical_not(route[3]))
    def _():
        low_ref[...] = jnp.zeros_like(low_ref)
        extended[0:rim, SUB : SUB + cols, :] = jnp.zeros((rim, cols, channels), jnp.float32)

    @pl.when(jnp.logical_not(route[2]))
    def _():
        high_ref[...] = jnp.zeros_like(high_ref)
        extended[rim + rows : 2 * rim + rows, SUB : SUB + cols, :] = jnp.zeros(
            (rim, cols, channels), jnp.float32
        )

    halo_store(route, extended, low_ref, high_ref, rows, cols, rim)

    def emit(e, i, tile, lanes, value):
        here = slice(i * cols + tile * SUB, i * cols + tile * SUB + SUB)
        if e == 0:
            conv_ref[here, lanes] = value + bias_ref[:, lanes]
        else:
            conv_ref[here, lanes] += value

    half_blocks = channels // LANES // 2
    conv_rows(extended, taps_ref, rows, cols, (0, half_blocks), False, emit)
    conv_rows(extended, taps_ref, rows, cols, (half_blocks, channels // LANES), False, emit)
    step = 2 * SUB

    def norm_block(block, carry):
        here = pl.ds(pl.multiple_of(block * step, step), step)
        values = conv_ref[here, :]
        centered = values - jnp.mean(values, axis=-1, keepdims=True)
        variance = jnp.mean(centered * centered, axis=-1, keepdims=True)
        scaled = centered * lax.rsqrt(variance + map_eps) * gain_ref[...] + shift_ref[...]
        normed_ref[here, :] = scaled.astype(jnp.bfloat16)
        return carry

    lax.fori_loop(0, rows * cols // step, norm_block, 0)
    ring.share_finish(given_all, given_sems)
    given_ref[...] = flat_low(given_all)


def pool_matrix(map_cols):
    chunk = 2 * map_cols
    cell_patch = (np.arange(chunk) % map_cols) // 2
    return np.arange(chunk // 4)[:, None] == cell_patch[None, :]


def conv_forward(hires, taps, bias, gain, shift, upstream):
    rows, cols, channels = hires.shape
    rim = KERNEL // 2
    cells = rows * cols
    count = lax.axis_size("tensor")
    patch_rows, model = upstream.shape
    pool = jnp.asarray(np.where(pool_matrix(cols), 0.25, 0.0), jnp.bfloat16)
    flat = jax.ShapeDtypeStruct((count * patch_rows, model), jnp.bfloat16)
    return pl.pallas_call(
        conv_forward_kernel,
        out_shape=(
            jax.ShapeDtypeStruct((cells, channels), jnp.bfloat16),
            jax.ShapeDtypeStruct((cells, channels), jnp.float32),
            jax.ShapeDtypeStruct((rim, cols, channels), jnp.bfloat16),
            jax.ShapeDtypeStruct((rim, cols, channels), jnp.bfloat16),
            flat,
            jax.ShapeDtypeStruct((patch_rows, channels), jnp.float32),
        ),
        in_specs=[VMEM_SPEC] * 7,
        out_specs=(VMEM_SPEC,) * 6,
        scratch_shapes=[
            pltpu.VMEM((rows + 2 * rim, cols + 2 * SUB, channels), jnp.float32),
            pltpu.VMEM((SUB, channels), jnp.float32),
            pltpu.VMEM((count, patch_rows, model), jnp.bfloat16),
            pltpu.SemaphoreType.DMA((2,)),
            pltpu.SemaphoreType.DMA((2,)),
            pltpu.SemaphoreType.DMA((2, count)),
        ],
        compiler_params=kernel_params(0),
        name="conv_forward",
    )(hires, taps, bias, gain, shift, pool, upstream)


def window_start(m, width, data):
    block, most = m * (width // data) // LANES, width // LANES - 2
    return (block - block // (most + 1) * (block - most)) * LANES


def lane_start(m, width, data):
    return m * (width // data) // LANES * LANES


JOB_ORDERS = (False, True, False, True, True)


WHOLE = 10


def small_kernel(shapes, tall_ring, tall_data, few_ring, few_data, *refs):
    outs = refs[WHOLE:]
    channels, model, units, width = shapes
    d, t = lax.axis_index("dp"), lax.axis_index("tensor")
    data, count = lax.axis_size("dp"), lax.axis_size("tensor")
    taps = KERNEL * KERNEL

    def turned(value, first):
        size = value.shape[1]
        return pltpu.roll(value, lax.rem(size - first, size), 1)

    here = channels // (data * count)
    start = jnp.minimum(d * (channels // data) // LANES, channels // LANES - 2) * LANES
    first = d * (channels // data) - start
    wide = turned(tall_ring[...], first + t * here)
    outs[0][...] = wide[:, 0:LANES].T[0:here, 0:taps]
    for i in range(5):
        outs[1 + i][...] = wide[taps + i, 0:here]
    step = model // data
    first = d * step - d * step // LANES * LANES + t * (step // count)
    narrow = turned(few_ring[0:SUB, 0:LANES], first)
    for i in range(8):
        outs[6 + i][...] = narrow[i, 0 : step // count]
    step = outs[14].shape[0]
    first = d * step - jnp.minimum(d * step // LANES, channels // LANES - 2) * LANES
    last_rows = tall_data.shape[0] - SUB
    outs[14][...] = turned(tall_data[last_rows:, :], first)[taps + 5 - last_rows, 0:step]
    step = units // data
    first = d * step - d * step // LANES * LANES
    outs[15][...] = turned(few_data[0:SUB, LANES : 2 * LANES], first)[0, 0:step]
    step = width // data
    first = d * step - d * step // LANES * LANES
    outs[16][...] = turned(few_data[SUB : 2 * SUB, 0:LANES], first)[0:2, 0:step]
    joined, patches, hires, pw1, pw2, fc1, fc2, qkv, out, adapt = refs[:WHOLE]
    whole = outs[17:]
    for source, target in zip((joined, patches, hires, pw1, fc1, adapt, pw2), whole[:7]):
        target[...] = source[...]
    for source, target in zip((fc2, out), whole[7:9]):
        target[...] = source[...].T
    for part in range(3):
        whole[9][part] = qkv[:, part * width : (part + 1) * width]


def small_outputs(sums, results, channels, model, units, width):
    data, count = lax.axis_size("dp"), lax.axis_size("tensor")
    taps = KERNEL * KERNEL
    shapes = (
        [(channels // (data * count), taps)]
        + [(channels // (data * count),)] * 5
        + [(model // (data * count),)] * 8
        + [(channels // data,), (units // data,), (2, width // data)]
    )
    joined, patches, hires, pw1, pw2, fc1, fc2, qkv, out, adapt = results
    more = [jax.ShapeDtypeStruct(r.shape, r.dtype) for r in results[:4] + (fc1, adapt, pw2)]
    more += [jax.ShapeDtypeStruct(r.shape[::-1], r.dtype) for r in (fc2, out)]
    more.append(jax.ShapeDtypeStruct((3, qkv.shape[0], width), qkv.dtype))
    return pl.pallas_call(
        partial(small_kernel, (channels, model, units, width)),
        out_shape=tuple(jax.ShapeDtypeStruct(shape, jnp.float32) for shape in shapes) + tuple(more),
        in_specs=[VMEM_SPEC] * (len(sums) + WHOLE),
        out_specs=(VMEM_SPEC,) * (len(shapes) + WHOLE),
        compiler_params=kernel_params(),
        name="small_outputs",
    )(*sums, *results)


def with_loads(kernel, inputs, later):
    specs = [VMEM_SPEC] * len(inputs)
    for index in later:
        specs[index] = pl.BlockSpec(memory_space=pl.ANY)
    buffers = [pltpu.VMEM(inputs[index].shape, inputs[index].dtype) for index in later]
    buffers.append(pltpu.SemaphoreType.DMA((len(later),)))

    def run(*refs):
        refs, own = list(refs[: -len(buffers)]), refs[-len(buffers) :]
        copies = {}
        for place, index in enumerate(later):
            copies[index] = pltpu.make_async_copy(refs[index], own[place], own[-1].at[place])
            copies[index].start()
            refs[index] = own[place]
        kernel(lambda index: copies[index].wait(), *refs)

    return specs, buffers, run


def mirror(index, low_half, last):
    return index + (1 - low_half) * (last - 2 * index)


def map_kernel(
    need, own_ref, w1_ref, b1_1d, w2_ref, given_ref, wadapt_ref, adapt_gain, layer_scale,
    pool_ref, spread_ref, conv_ref, gain_1d, attn_own,
    grad_ref, branch_ref, half1_ref, half2_ref, gb1_ref, pooled_grad_ref, attn_ref, sums_ref,
    gw1_ref, gw2_ref, patches_all, half_sems, attn_sems,
    b1_ref, branch_grad_ref, pooled_grads, rows_all, pre_grads, stash, from_below, from_above, pooled, hidden_grads,
    ag_recv, ag_up, ag_down, up_recv, up_send, down_recv, down_send,
):
    count, cells, channels = rows_all.shape
    hidden = w1_ref.shape[1]
    parts = ag_recv.shape[1]
    chunk = cells // parts
    quarter = chunk // 4
    last = count - 1
    d, t = lax.axis_index("dp"), lax.axis_index("tensor")
    low_half = 1 - t // 2
    place = mirror(t, low_half, last)
    above, below = (d, t + 1), (d, t - 1)
    ring = Ring()
    core = d + 1 - 2 * lax.rem(d, 2)
    meet([core], False)
    job1 = Halving(gw1_ref, [half1_ref], half_sems.at[0], half_sems.at[1], False)
    job2 = Halving(gw2_ref, [half2_ref], half_sems.at[2], half_sems.at[3], False)

    def rows_of(p):
        return pl.ds(pl.multiple_of(p * chunk, chunk), chunk)

    def gather_copy(j, p, target, send):
        return pltpu.make_async_remote_copy(
            rows_all.at[j, rows_of(p)], rows_all.at[j, rows_of(p)],
            send.at[j, p], ag_recv.at[j, p], device_id=target, device_id_type=MESH_ID,
        )

    def sum_copy(j, p, going_up):
        landing = from_below if going_up else from_above
        return pltpu.make_async_remote_copy(
            stash.at[j, rows_of(p)], landing.at[j, rows_of(p)],
            (up_send if going_up else down_send).at[j, p],
            (up_recv if going_up else down_recv).at[j, p],
            device_id=above if going_up else below, device_id_type=MESH_ID,
        )

    rows_all[t] = own_ref[...]
    for p in range(parts):
        @pl.when(t < last)
        def _():
            gather_copy(t, p, above, ag_up).start()

        @pl.when(t > 0)
        def _():
            gather_copy(t, p, below, ag_down).start()

    b1_ref[0:1, :] = as_row(b1_1d)
    adapt_grad = (given_ref[...].astype(jnp.float32) * as_row(adapt_gain)).astype(jnp.bfloat16)
    need(5)
    pooled_grad = contract_cols(adapt_grad, wadapt_ref[...])
    pooled_grads[...] = pooled_grad
    branch_grad_ref[...] = (as_row(layer_scale) * (pooled_grad * 0.25)).astype(jnp.bfloat16)
    own_rows = pooled_grad_ref.shape[0]
    pooled_grad_ref[...] = pooled_grads[pl.ds(pl.multiple_of(t * own_rows, SUB), own_rows), :]
    need(3)
    hidden_grads[...] = contract_cols(branch_grad_ref[...], w2_ref[...])
    gb1_ref[...] = jnp.zeros_like(gb1_ref)
    block = 256

    def pass_on(j, p, going_up):
        copy = sum_copy(j, p, going_up)
        copy.wait_recv()
        landing = from_below if going_up else from_above
        stash[j, rows_of(p), :] = (
            stash[j, rows_of(p), :].astype(jnp.float32)
            + landing[j, rows_of(p), :].astype(jnp.float32)
        ).astype(jnp.bfloat16)
        copy.start()

    middle = place == 1

    def forward_up(s, carry):
        j, p = t + 1 + s // parts, lax.rem(s, parts)
        pass_on(j, p, True)
        return carry

    def forward_down(s, carry):
        j, p = t - 1 - s // parts, lax.rem(s, parts)
        pass_on(j, p, False)
        return carry

    def forward(first, last_step, along):
        @pl.when(jnp.logical_and(middle, low_half == 1))
        def _():
            lax.fori_loop(first, last_step, forward_up if along else forward_down, 0)

        @pl.when(jnp.logical_and(middle, low_half == 0))
        def _():
            lax.fori_loop(first, last_step, forward_down if along else forward_up, 0)

    def order(n):
        return mirror(n + place * (1 - 2 * n) * (1 - n // 2), low_half, last)

    def receive(j, p):
        gather_copy(j, p, above, ag_up).wait_recv()

        @pl.when(jnp.logical_and(j < t, t < last))
        def _():
            gather_copy(j, p, above, ag_up).start()

        @pl.when(jnp.logical_and(j > t, t > 0))
        def _():
            gather_copy(j, p, below, ag_down).start()

    def receive_all(j):
        for p in range(parts):
            receive(j, p)

    def send_sums(j, p):
        @pl.when(jnp.logical_and(j > t, t == 0))
        def _():
            sum_copy(j, p, True).start()

        @pl.when(jnp.logical_and(j < t, t == last))
        def _():
            sum_copy(j, p, False).start()

    def compute(j, here, small):
        rows = here.size
        few = rows // 4
        given = rows_all[j, here, :]
        for first in range(0, hidden, block):
            cols = slice(first, first + block)
            pre = (
                jnp.dot(given, w1_ref[:, cols], preferred_element_type=jnp.float32)
                + b1_ref[0:1, cols]
            )
            wide_grad = hidden_grads[small, cols]
            high = wide_grad.astype(jnp.bfloat16)
            rest = (wide_grad - high.astype(jnp.float32)).astype(jnp.bfloat16)
            spread = spread_ref[0:rows, 0:few]
            spread_grad = jnp.dot(
                spread, high, preferred_element_type=jnp.float32
            ) + jnp.dot(spread, rest, preferred_element_type=jnp.float32)
            below_curve = 0.5 + 0.5 * lax.erf(pre * ROOT_HALF)
            slope = below_curve + pre * jnp.exp(-0.5 * pre * pre) * NORMAL_PEAK
            active = (pre * below_curve).astype(jnp.bfloat16)
            pooled[small, cols] = jnp.dot(
                pool_ref[0:few, 0:rows], active, preferred_element_type=jnp.float32
            )
            pre_low = (spread_grad * slope).astype(jnp.bfloat16)
            gb1_ref[:, cols] += jnp.sum(pre_low.astype(jnp.float32), axis=0, keepdims=True)
            pre_grads[j, here, cols] = pre_low
        return contract_cols(pre_grads[j, here, :], w1_ref[...])

    def whole_shard(n, carry):
        j = order(n)

        @pl.when(jnp.logical_and(place == 1, n == 1))
        def _():
            receive_all(order(1))
            receive_all(order(2))

        @pl.when(jnp.logical_and(place == 1, n == last))
        def _():
            receive_all(order(last))
            forward(0, 1, True)

        few = cells // 4
        partial_grad = compute(
            j, pl.ds(0, cells), pl.ds(pl.multiple_of(j * few, SUB), few)
        )

        @pl.when(n == 0)
        def _():
            grad_ref[...] = partial_grad

        @pl.when(n > 0)
        def _():
            stash[j] = partial_grad.astype(jnp.bfloat16)

        return carry

    def one_chunk(q, carry):
        j, p = order(1 + q // parts), lax.rem(q, parts)
        receive(j, p)
        small = pl.ds(pl.multiple_of((j * parts + p) * quarter, SUB), quarter)
        stash[j, rows_of(p), :] = compute(j, rows_of(p), small).astype(jnp.bfloat16)
        send_sums(j, p)
        return carry

    patches_all[t] = attn_own[...]
    need(1)
    lax.fori_loop(0, 1 + last * place, whole_shard, 0)
    lax.fori_loop(0, last * parts * (1 - place), one_chunk, 0)
    ring.spread_start(patches_all, attn_sems)

    wide = 384
    rows_flat = rows_all.reshape(count * cells, channels)
    pre_flat = pre_grads.reshape(count * cells, hidden)
    steps = []
    for p in range(1, 2 * parts):
        steps.append((p, True))
        if p > parts:
            steps.append((p - parts - 1, False))
    steps += [(p, False) for p in range(parts - 1, parts)]
    starts = list(range(0, channels, wide))
    for index, (p, along) in enumerate(steps):
        forward(p, p + 1, along)
        if index < len(starts):
            first = starts[index]
            fill_rows(
                gw1_ref, first, contract_rows(rows_flat[:, first : first + wide], pre_flat[...])
            )
    job1.start(0)
    ring.spread_relay(patches_all, attn_sems)
    pooled_low = pooled[...].astype(jnp.bfloat16)
    for first in range(0, channels, wide):
        fill_rows(
            gw2_ref, first,
            4.0 * contract_rows(branch_grad_ref[:, first : first + wide], pooled_low),
        )
    job2.start(0)
    branch_ref[...] = jnp.dot(
        pooled_low, w2_ref[...], preferred_element_type=jnp.float32
    ).astype(jnp.bfloat16)

    def finish(p, carry):
        @pl.when(t > 0)
        def _():
            sum_copy(t, p, True).wait_recv()
            grad_ref[rows_of(p), :] += from_below[t, rows_of(p), :].astype(jnp.float32)

        @pl.when(t < last)
        def _():
            sum_copy(t, p, False).wait_recv()
            grad_ref[rows_of(p), :] += from_above[t, rows_of(p), :].astype(jnp.float32)

        return carry

    lax.fori_loop(0, parts, finish, 0)
    need(10)
    sums_ref[...] = jnp.zeros_like(sums_ref)
    gain = as_row(gain_1d)
    step = 2 * SUB

    def grad_block(block, carry):
        here = pl.ds(pl.multiple_of(block * step, step), step)
        dy = grad_ref[here, :]
        xhat, rs = norm_parts(conv_ref[here, :], map_eps)
        grad = norm_pull(dy, xhat, rs, gain)
        grad_ref[here, :] = grad
        sums_ref[0:1, :] += row_sum(dy * xhat)
        sums_ref[1:2, :] += row_sum(dy)
        sums_ref[2:3, :] += row_sum(grad)
        return carry

    lax.fori_loop(0, cells // step, grad_block, 0)
    ring.spread_finish(patches_all, attn_sems)
    attn_ref[...] = flat_low(patches_all)
    job1.finish(0)
    job2.finish(0)

    def drain(q, carry):
        j, p = q // parts, lax.rem(q, parts)

        @pl.when(jnp.logical_and(j <= t, t < last))
        def _():
            gather_copy(j, p, above, ag_up).wait_send()

        @pl.when(jnp.logical_and(j >= t, t > 0))
        def _():
            gather_copy(j, p, below, ag_down).wait_send()

        @pl.when(j > t)
        def _():
            sum_copy(j, p, True).wait_send()

        @pl.when(j < t)
        def _():
            sum_copy(j, p, False).wait_send()

        return carry

    lax.fori_loop(0, count * parts, drain, 0)


def map_block(
    normed_low, w_pw1, pw1_bias, w_pw2, grad_all, w_adapt, adapt_gain, layer_scale,
    conv, gain, attn_own, map_cols,
):
    cells, channels = normed_low.shape
    hidden = w_pw1.shape[1]
    count, data = lax.axis_size("tensor"), lax.axis_size("dp")
    chunk = 2 * map_cols
    parts = cells // chunk
    patches, model = grad_all.shape
    match = np.kron(np.eye(parts), pool_matrix(map_cols)) > 0.5
    pool = jnp.asarray(np.where(match, 0.25, 0.0), jnp.bfloat16)
    spread = jnp.asarray(match.T, jnp.bfloat16)
    low_all = pltpu.VMEM((count, cells, channels), jnp.bfloat16)
    sems = pltpu.SemaphoreType.DMA((count, parts))
    weight = pltpu.VMEM((data, channels // data, hidden), jnp.bfloat16)
    half = jax.ShapeDtypeStruct((data // 2, channels // data, hidden), jnp.bfloat16)
    inputs = (
        normed_low, w_pw1, pw1_bias, w_pw2, grad_all, w_adapt, adapt_gain, layer_scale,
        pool, spread, conv, gain, attn_own,
    )
    later = (5, 3, 1, 10)
    specs, buffers, run = with_loads(map_kernel, inputs, later)
    return pl.pallas_call(
        run,
        out_shape=(
            jax.ShapeDtypeStruct((cells, channels), jnp.float32),
            jax.ShapeDtypeStruct((patches, channels), jnp.bfloat16),
            half,
            half,
            jax.ShapeDtypeStruct((1, hidden), jnp.float32),
            jax.ShapeDtypeStruct((patches // count, channels), jnp.float32),
            jax.ShapeDtypeStruct((patches, model), jnp.bfloat16),
            jax.ShapeDtypeStruct((SUB, channels), jnp.float32),
        ),
        in_specs=specs,
        out_specs=(VMEM_SPEC,) * 8,
        scratch_shapes=[
            weight,
            weight,
            pltpu.VMEM((count, patches // count, model), jnp.bfloat16),
            pltpu.SemaphoreType.DMA((4, data - 1)),
            pltpu.SemaphoreType.DMA((2, count)),
            pltpu.VMEM((SUB, hidden), jnp.float32),
            pltpu.VMEM((patches, channels), jnp.bfloat16),
            pltpu.VMEM((patches, channels), jnp.float32),
            low_all,
            pltpu.VMEM((count, cells, hidden), jnp.bfloat16),
            low_all,
            low_all,
            low_all,
            pltpu.VMEM((patches, hidden), jnp.float32),
            pltpu.VMEM((patches, hidden), jnp.float32),
        ]
        + [sems] * 7
        + buffers,
        compiler_params=kernel_params(2),
        name="map_block",
    )(*inputs)


def last_kernel(
    need, patches_ref, attn_ref, given_ref, map_mean_ref, grad_pooled_ref, branch_parts, half1_ref, half2_ref,
    ln1_gain, wqkv_ref, qv_bias, wout_ref, out_bias, ln2_gain, ln2_bias,
    wfc1_ref, fc1_bias, wfc2_ref, fc2_bias, wadapt_ref, adapt_bias, adapt_gain,
    pw2_bias, layer_scale, live_ref, pick_ref, upstream_keep, conv_grad_ref,
    own_map, low_map, high_map, taps_ref, spread_ref, sums_conv, pw1_sums, ln1_bias, patches_all,
    joined_ref, grad_patches_ref, red1_ref, red2_ref, hires_grad_ref, tall_ring, tall_data, few_ring, few_data,
    job_outs,
    keys_all, values_all, kv_own, kv_other, queries, hidden_grad, probs, attended, middle_keep,
    hidden, pre_grad, dkv_other, mlp_flat, bias_row,
    parts, landing, out_parts, out_land, shared, branch_land, pool_parts, pool_land,
    sums_model, sums_map, sums_heads, sums_ff,
    grads, first_low, last_low, low_in, high_in, tap_grad_ref, tall_sum, few_sum, few_packed,
    halo_send, halo_recv, local_sem,
    proj_sems, mlp_sems, in_sems, out_sems, share_sems, attn_sems, branch_sems, pool_sems, pair_sems,
    staging, stage_sem, job_sources, job_scratch,
):
    dqkv, dkv_send, proj_flat = pre_grad, kv_own, mlp_flat
    ring = Ring()
    count, d, t = ring.count, ring.d, ring.t
    data = lax.axis_size("dp")
    stages = bits_of(data)
    rows, model = patches_ref.shape
    half_rows, width = queries.shape
    heads = width // HEAD_DIM
    scale = HEAD_DIM**-0.5
    partner = d + 1 - 2 * lax.rem(d, 2)
    map_rows, map_cols, channels = own_map.shape
    rim = KERNEL // 2
    lane_blocks = channels // LANES
    inner = slice(SUB, SUB + map_cols)

    meet([lax.rem(d + k, data) for k in range(1, data)])
    load = pltpu.make_async_copy(
        conv_grad_ref, grads.at[pl.ds(rim, map_rows), pl.ds(SUB, map_cols)], local_sem
    )
    load.start()
    map_jobs = []
    for half, scratch, top in zip((half1_ref, half2_ref), job_scratch[:2], (False, True)):
        landings = [half] + list(scratch[: stages - 1])
        job = Halving(None, landings, scratch[stages - 1], scratch[stages], top)
        job.staging = (staging, stage_sem)
        map_jobs.append(job)
    jobs = [
        Halving(source, scratch[:stages], scratch[stages], scratch[stages + 1], top)
        for source, scratch, top in zip(job_sources, job_scratch[2:], JOB_ORDERS)
    ]
    fc1_job, fc2_job, qkv_job, out_job, adapt_job = jobs
    gfc1, gfc2, gqkv, gout, gadapt = job_sources

    def step_map_jobs():
        for job, out in zip(map_jobs, (red1_ref, red2_ref)):
            job.step(out)

    def step_jobs(*which):
        for index in which:
            jobs[index].step(job_outs[index])

    for edge in (0, SUB + map_cols):
        grads[:, edge : edge + SUB, :] = jnp.zeros(
            (map_rows + 2 * rim, SUB, channels), jnp.float32
        )
    sums_model[...] = jnp.zeros_like(sums_model)
    sums_map[...] = jnp.zeros_like(sums_map)
    sums_heads[...] = jnp.zeros_like(sums_heads)
    sums_ff[...] = jnp.zeros_like(sums_ff)
    load.wait()
    route = halo_route()
    first_low[...] = grads[rim : 2 * rim, inner, :].astype(jnp.bfloat16)
    last_low[...] = grads[map_rows : map_rows + rim, inner, :].astype(jnp.bfloat16)
    halo = halo_copies(route, first_low, last_low, low_in, high_in, halo_send, halo_recv)
    halo_start(route, halo)
    for job in map_jobs:
        job.begin(1)

    need(1)
    band = 6 * 2 * SUB
    for first in range(0, half_rows, band):
        here = slice(first, first + band)
        xhat, _ = norm_parts(attn_ref[here, :].astype(jnp.float32), vit_eps)
        attn_ref[here, :] = (xhat * as_row(ln1_gain) + as_row(ln1_bias)).astype(jnp.bfloat16)
    attn = attn_ref[...]
    need(9)
    own_keys = jnp.dot(attn, wqkv_ref[1], preferred_element_type=jnp.float32).astype(jnp.bfloat16)
    own_values = (
        jnp.dot(attn, wqkv_ref[2], preferred_element_type=jnp.float32) + qv_bias[1:2, :]
    ).astype(jnp.bfloat16)
    kv_own[:, 0:width] = own_keys
    kv_own[:, width : 2 * width] = own_values

    def pair_copy(source, target, slot):
        return pltpu.make_async_remote_copy(
            source, target, pair_sems.at[0, slot], pair_sems.at[1, slot],
            device_id=(partner, t), device_id_type=MESH_ID,
        )

    pair_copy(kv_own, kv_other, 0).start()
    need(5)
    ring.sum_start(branch_parts, branch_land, branch_sems)
    queries[...] = (
        jnp.dot(attn, wqkv_ref[0], preferred_element_type=jnp.float32) + qv_bias[0:1, :]
    ).astype(jnp.bfloat16)
    keys_all[0:half_rows, :] = own_keys
    values_all[0:half_rows, :] = own_values
    pair_copy(kv_own, kv_other, 0).wait()
    keys_all[half_rows : 2 * half_rows, :] = kv_other[:, 0:width]
    values_all[half_rows : 2 * half_rows, :] = kv_other[:, width : 2 * width]
    live = live_ref[...] > 0.5
    for h in range(heads):
        here = slice(h * HEAD_DIM, (h + 1) * HEAD_DIM)
        raw = contract_cols(queries[:, here], keys_all[:, here]) * scale
        scores = jnp.where(live, raw, masked_score)
        grown = jnp.exp(scores - jnp.max(scores, axis=-1, keepdims=True))
        prob = grown * (1.0 / jnp.sum(grown, axis=-1, keepdims=True))
        probs[h] = prob
        attended[:, here] = jnp.dot(
            prob.astype(jnp.bfloat16), values_all[:, here], preferred_element_type=jnp.float32
        ).astype(jnp.bfloat16)
    need(11)
    fill_parts(parts, jnp.dot(attended[...], wout_ref[...], preferred_element_type=jnp.float32))
    ring.give_start(parts, landing, proj_sems)

    need(2)
    need(17)
    need(4)
    need(29)
    need(28)
    need(30)
    hidden_grad[...] = contract_cols(given_ref[...], wfc2_ref[...])
    for pair in range(map_rows // 2):
        half = map_cols // 2
        spread = jnp.dot(
            spread_ref[...],
            grad_pooled_ref[pair * half : (pair + 1) * half, :],
            precision=lax.Precision.HIGHEST,
            preferred_element_type=jnp.float32,
        )
        for i in range(2):
            hires_grad_ref[2 * pair + i] = spread
    map_refs = (low_map, own_map, high_map)
    tap_rows(grads, map_refs, tap_grad_ref, map_rows, map_cols, (0, lane_blocks // 2))
    ring.sum_relay(branch_parts, branch_land, branch_sems)
    ring.give_finish(parts, landing, proj_sems)
    inputs = patches_ref[...].astype(jnp.float32)
    middle = inputs + (ring.total(parts, landing) + as_row(out_bias))
    middle_keep[...] = middle
    xhat, _ = norm_parts(middle, vit_eps)
    shared[t] = (xhat * as_row(ln2_gain) + as_row(ln2_bias)).astype(jnp.bfloat16)
    ring.spread_start(shared, mlp_sems)

    branch = ring.sum_finish(branch_parts, branch_land, branch_sems) + as_row(pw2_bias)
    need(3)
    pooled = (map_mean_ref[...] + as_row(layer_scale) * branch).astype(jnp.bfloat16)
    pooled_grad = grad_pooled_ref[...]
    sums_map[0:1, :] = 4.0 * row_sum(
        (as_row(layer_scale) * (pooled_grad * 0.25)).astype(jnp.bfloat16).astype(jnp.float32)
    )
    sums_map[1:2, :] = row_sum(pooled_grad * branch)
    per_peer = channels // count
    place = lax.broadcasted_iota(jnp.int32, (channels, per_peer), 0)
    for j in range(count):
        choose = jnp.where(place == pick_ref[j : j + 1, :], 1.0, 0.0).astype(jnp.bfloat16)
        pool_parts[j] = jnp.dot(pooled, choose, preferred_element_type=jnp.float32).astype(
            jnp.bfloat16
        )
    ring.give_start(pool_parts, pool_land, pool_sems)
    need(19)
    adapted = (
        jnp.dot(pooled, wadapt_ref[...], preferred_element_type=jnp.float32) + as_row(adapt_bias)
    )
    upstream = upstream_keep[...].astype(jnp.float32)
    sums_model[5:6, :] = row_sum(upstream)
    sums_model[6:7, :] = row_sum(
        (upstream * as_row(adapt_gain)).astype(jnp.bfloat16).astype(jnp.float32)
    )
    sums_model[7:8, :] = row_sum(upstream * adapted)
    adapted_part = as_row(adapt_gain) * adapted
    ring.spread_relay(shared, mlp_sems)
    tap_rows(grads, map_refs, tap_grad_ref, map_rows, map_cols, (lane_blocks // 2, lane_blocks))
    taps = KERNEL * KERNEL
    tap_grad_ref[taps : taps + 3, :] = sums_conv[0:3, :]
    tap_grad_ref[taps + 3 : taps + 5, :] = sums_map[0:2, :]
    tap_grad_ref[taps + 5 : taps + 6, :] = pw1_sums[...]
    tap_grad_ref[taps + 6 : taps + 7, :] = jnp.zeros((1, channels), jnp.float32)
    tall_sum.piece = lambda m: tap_grad_ref.at[
        :, pl.ds(pl.multiple_of(window_start(m, channels, data), LANES), 2 * LANES)
    ]
    tall_sum.start()

    need(15)
    ring.spread_finish(shared, mlp_sems)
    mlp_flat[...] = flat_low(shared)
    units = wfc1_ref.shape[1]
    block = 256
    bias_row[0:1, :] = as_row(fc1_bias)

    def mlp_block(index, carry):
        cols = pl.ds(pl.multiple_of(index * block, block), block)
        pre = (
            jnp.dot(mlp_flat[...], wfc1_ref[:, cols], preferred_element_type=jnp.float32)
            + bias_row[0:1, cols]
        )
        below_curve = 0.5 + 0.5 * lax.erf(pre * ROOT_HALF)
        slope = below_curve + pre * jnp.exp(-0.5 * pre * pre) * NORMAL_PEAK
        hidden[:, cols] = (pre * below_curve).astype(jnp.bfloat16)
        pre_low = (hidden_grad[:, cols] * slope).astype(jnp.bfloat16)
        pre_grad[:, cols] = pre_low
        sums_ff[0:1, cols] = row_sum(pre_low.astype(jnp.float32))
        return carry

    lax.fori_loop(0, units // block, mlp_block, 0)
    fill_parts(parts, contract_cols(pre_grad[:, 0:units], wfc1_ref[...]))
    ring.give_start(parts, landing, in_sems)
    fill_parts(
        out_parts, jnp.dot(hidden[...], wfc2_ref[...], preferred_element_type=jnp.float32)
    )
    ring.sum_start(out_parts, out_land, out_sems)


    def gfc1_block(index, carry):
        first = pl.multiple_of(index * block, block)
        cols = pl.ds(first, block)
        fill_rows(gfc1, first, contract_rows(mlp_flat[:, cols], pre_grad[:, 0:units]))
        return carry

    lax.fori_loop(0, model // block, gfc1_block, 0)
    fc1_job.begin()

    def gfc2_block(index, carry):
        first = pl.multiple_of(index * block, block)
        cols = pl.ds(first, block)
        fill_rows(gfc2, first, contract_rows(given_ref[:, cols], hidden[...]))
        return carry

    lax.fori_loop(0, model // block, gfc2_block, 0)
    fc2_job.begin()
    halo_finish(route, halo)

    @pl.when(jnp.logical_not(route[3]))
    def _():
        grads[0:rim, inner, :] = jnp.zeros((rim, map_cols, channels), jnp.float32)

    @pl.when(jnp.logical_not(route[2]))
    def _():
        grads[rim + map_rows : 2 * rim + map_rows, inner, :] = jnp.zeros(
            (rim, map_cols, channels), jnp.float32
        )

    need(31)
    halo_store(route, grads, low_in, high_in, map_rows, map_cols, rim)

    def emit(e, i, tile, lanes, value):
        hires_grad_ref[i, tile * SUB : (tile + 1) * SUB, lanes] += value

    third = lane_blocks // 3
    conv_rows(grads, taps_ref, map_rows, map_cols, (0, third), True, emit)
    ring.give_finish(parts, landing, in_sems)
    mlp_in_grad = ring.total(parts, landing)
    middle = middle_keep[...]
    xhat, rs = norm_parts(middle, vit_eps)
    sums_model[3:4, :] = row_sum(mlp_in_grad * xhat)
    sums_model[4:5, :] = row_sum(mlp_in_grad)
    middle_grad = upstream + norm_pull(mlp_in_grad, xhat, rs, as_row(ln2_gain))
    grad_patches_ref[...] = middle_grad
    proj_low = middle_grad.astype(jnp.bfloat16)
    sums_model[2:3, :] = row_sum(proj_low.astype(jnp.float32))
    shared[t] = proj_low
    ring.spread_start(shared, share_sems)

    tall_sum.share(tall_data)
    step_map_jobs()
    step_jobs(0, 1)
    ring.spread_relay(shared, share_sems)
    ring.sum_relay(out_parts, out_land, out_sems)
    conv_rows(grads, taps_ref, map_rows, map_cols, (third, 2 * third), True, emit)
    ring.give_finish(pool_parts, pool_land, pool_sems)
    pool_land[t] = pool_parts[t]
    adapt_grad = (given_ref[...].astype(jnp.float32) * as_row(adapt_gain)).astype(jnp.bfloat16)
    fill_rows(gadapt, 0, contract_rows(flat_low(pool_land), adapt_grad))
    adapt_job.begin()
    vit_out = middle + (ring.sum_finish(out_parts, out_land, out_sems) + as_row(fc2_bias))
    joined_ref[...] = (vit_out + adapted_part).astype(jnp.bfloat16)

    ring.spread_finish(shared, share_sems)
    proj_flat[...] = flat_low(shared)
    attended_grad = contract_cols(proj_flat[...], wout_ref[...]).astype(jnp.bfloat16)
    for h in range(heads):
        here = slice(h * HEAD_DIM, (h + 1) * HEAD_DIM)
        there = slice(width + h * HEAD_DIM, width + (h + 1) * HEAD_DIM)
        head_grad = attended_grad[:, here]
        prob = probs[h]
        value_part = contract_rows(prob.astype(jnp.bfloat16), head_grad)
        prob_grad = contract_cols(head_grad, values_all[:, here])
        dot_rows = jnp.sum(prob * prob_grad, axis=-1, keepdims=True)
        score_grad = (prob * (prob_grad - dot_rows)).astype(jnp.bfloat16)
        dqkv[:, here] = (
            jnp.dot(score_grad, keys_all[:, here], preferred_element_type=jnp.float32) * scale
        ).astype(jnp.bfloat16)
        key_part = contract_rows(score_grad, queries[:, here]) * scale
        dkv_send[:, here] = key_part[half_rows:].astype(jnp.bfloat16)
        dkv_send[:, there] = value_part[half_rows:].astype(jnp.bfloat16)
        hidden_grad[:, here] = key_part[:half_rows]
        hidden_grad[:, there] = value_part[:half_rows]
    pair_copy(dkv_send, dkv_other, 1).start()

    def gout_block(index, carry):
        first = pl.multiple_of(index * block, block)
        cols = pl.ds(first, block)
        fill_rows(gout, first, contract_rows(proj_flat[:, cols], attended[...]))
        return carry

    lax.fori_loop(0, model // block, gout_block, 0)
    out_job.begin()
    again = pltpu.make_async_copy(patches_all, proj_flat, local_sem)
    again.start()
    pair_copy(dkv_send, dkv_other, 1).wait()
    kv_grad = (hidden_grad[:, 0 : 2 * width] + dkv_other[...].astype(jnp.float32)).astype(
        jnp.bfloat16
    )
    dqkv[:, width : 3 * width] = kv_grad
    attn_grad = contract_cols(dqkv[:, 0:width], wqkv_ref[0])
    for part in (1, 2):
        attn_grad += contract_cols(dqkv[:, part * width : (part + 1) * width], wqkv_ref[part])
    fill_parts(parts, attn_grad)
    ring.give_start(parts, landing, attn_sems)
    again.wait()
    for first in range(0, half_rows, band):
        rows_grad = attn_grad[first : first + band]
        xhat, _ = norm_parts(proj_flat[first : first + band, :].astype(jnp.float32), vit_eps)
        sums_model[0:1, :] += row_sum(rows_grad * xhat)
        sums_model[1:2, :] += row_sum(rows_grad)

    sums_heads[0:1, :] = row_sum(dqkv[:, 0:width].astype(jnp.float32))
    sums_heads[1:2, :] = row_sum(dqkv[:, 2 * width : 3 * width].astype(jnp.float32))
    zero = jnp.zeros((SUB, LANES), jnp.float32)
    for m in range(data):
        for lane, (row, source) in enumerate(((0, sums_model), (0, sums_ff), (SUB, sums_heads))):
            first = lane_start(m, source.shape[1], data)
            side = LANES * (lane % 2)
            few_packed[m, row : row + SUB, side : side + LANES] = source[
                :, first : first + LANES
            ]
        few_packed[m, SUB : 2 * SUB, LANES : 2 * LANES] = zero
    few_sum.piece = lambda m: few_packed.at[m]
    few_sum.start()

    def gqkv_block(index, carry):
        first = pl.multiple_of(index * block, block)
        cols = pl.ds(first, block)
        fill_rows(gqkv, first, contract_rows(attn_ref[:, cols], dqkv[:, 0 : 3 * width]))
        return carry

    lax.fori_loop(0, model // block, gqkv_block, 0)
    qkv_job.begin()
    step_jobs(0, 1, 4, 3, 2)
    few_sum.share(few_data)
    conv_rows(grads, taps_ref, map_rows, map_cols, (2 * third, lane_blocks), True, emit)
    ring.give_finish(parts, landing, attn_sems)
    attn_in_grad = ring.total(parts, landing)
    xhat, rs = norm_parts(inputs, vit_eps)
    grad_patches_ref[...] += norm_pull(attn_in_grad, xhat, rs, as_row(ln1_gain))
    step_map_jobs()
    step_jobs(0, 1, 4, 3, 2)
    for _ in range(stages):
        step_map_jobs()
        step_jobs(0, 1, 4, 3, 2)
    tall_sum.finish(tall_ring)
    few_sum.finish(few_ring)


def last_block(
    patches, patches_all, grad_all, map_mean, grad_pooled, branch_partial, half1, half2,
    ln1_gain, w_qkv, qv_bias, w_out, out_bias, ln2_gain, ln2_bias,
    w_fc1, fc1_bias, w_fc2, fc2_bias, w_adapt, adapt_bias, adapt_gain, pw2_bias, layer_scale,
    key_live, grad_own, conv_grad, hires, low_rim, high_rim, taps, sums_conv, pw1_sums, ln1_bias,
):
    count = lax.axis_size("tensor")
    data = lax.axis_size("dp")
    stages = bits_of(data)
    rows, model = patches.shape
    half_rows = rows * count
    width = w_out.shape[0]
    heads = width // HEAD_DIM
    units = w_fc1.shape[1]
    map_rows, map_cols, channels = hires.shape
    rim = KERNEL // 2
    stage_rows = channels // (data * count)
    place = np.arange(channels // count)
    pick = np.stack(
        [(place // stage_rows * count + j) * stage_rows + place % stage_rows for j in range(count)]
    ).astype(np.int32)
    near = np.arange(map_cols)[:, None] // 2 == np.arange(map_cols // 2)[None, :]
    spread = jnp.asarray(np.where(near, 0.25, 0.0), jnp.float32)
    f32, low = jnp.float32, jnp.bfloat16

    def vmem(*shape, dtype=low):
        return pltpu.VMEM(shape, dtype)

    shard = vmem(count, rows, model)
    rim_low = vmem(rim, map_cols, channels)
    tall = (KERNEL * KERNEL + SUB - 1) // SUB * SUB
    tall_block, few_block = (tall, 2 * LANES), (2 * SUB, 2 * LANES)
    dma = pltpu.SemaphoreType.DMA
    scratch = [
        vmem(2 * half_rows, width), vmem(2 * half_rows, width),
        vmem(half_rows, 2 * width), vmem(half_rows, 2 * width), vmem(half_rows, width),
        vmem(half_rows, units, dtype=f32), vmem(heads, half_rows, 2 * half_rows, dtype=f32),
        vmem(half_rows, width), vmem(rows, model, dtype=f32),
        vmem(half_rows, units), vmem(half_rows, max(units, 3 * width)),
        vmem(half_rows, 2 * width), vmem(half_rows, model), vmem(SUB, units, dtype=f32),
        shard, shard, shard, shard, shard,
        vmem(count, rows, channels),
        vmem(count, rows, channels // count), vmem(count, rows, channels // count),
        vmem(SUB, model, dtype=f32), vmem(SUB, channels, dtype=f32),
        vmem(SUB, width, dtype=f32), vmem(SUB, units, dtype=f32),
        vmem(map_rows + 2 * rim, map_cols + 2 * SUB, channels, dtype=f32),
        rim_low, rim_low, rim_low, rim_low, vmem(tall, channels, dtype=f32),
        vmem(data, *few_block, dtype=f32),
        dma((2,)), dma((2,)), dma,
    ] + [dma((2, count))] * 9 + [vmem(*half1.shape[1:]), dma]
    fixed = len(scratch)
    sum_place = fixed - 15
    sources = [
        (data, model // data, units), (data, model // data, units),
        (data, model // data, 3 * width), (data, model // data, width),
        (data, channels // (count * data), model),
    ]
    n_jobs = len(sources)
    scratch += [vmem(*shape) for shape in sources]
    map_shape = half1.shape
    sizes = []
    for shape in [(data, map_shape[1], map_shape[2])] * 2 + sources:
        first = data // 4 if len(sizes) < 2 else data // 2
        more = halving_scratch(*shape, first)
        sizes.append(len(more))
        scratch += more
    n_in, n_out, few_outs = 37, 9 + n_jobs, 9
    sum_scratch = small_sum_scratch(data, count, tall) + small_sum_scratch(data, count, 2 * SUB)
    n_sum = len(sum_scratch)
    scratch += sum_scratch

    def kernel(need, *refs):
        ins, outs, rest = refs[:n_in], refs[n_in : n_in + n_out], refs[n_in + n_out :]
        rest, sum_refs = rest[:-n_sum], rest[-n_sum:]
        own, more = list(rest[:fixed]), list(rest[fixed + n_jobs :])
        own[sum_place:sum_place] = [
            SmallSum(*sum_refs[: n_sum // 2]), SmallSum(*sum_refs[n_sum // 2 :])
        ]
        job_scratch = []
        for size in sizes:
            job_scratch.append(more[:size])
            more = more[size:]
        last_kernel(
            need, *ins, *outs[:few_outs], outs[few_outs:], *own, rest[fixed : fixed + n_jobs], job_scratch
        )

    def out(*shape, dtype=f32):
        return jax.ShapeDtypeStruct(shape, dtype)

    inputs = (
        patches, patches_all, grad_all, map_mean, grad_pooled,
        branch_partial.reshape(count, rows, channels), half1, half2,
        ln1_gain, w_qkv, qv_bias, w_out, out_bias, ln2_gain, ln2_bias,
        w_fc1, fc1_bias, w_fc2, fc2_bias, w_adapt, adapt_bias, adapt_gain,
        pw2_bias, layer_scale, key_live, jnp.asarray(pick), grad_own,
        conv_grad.reshape(map_rows, map_cols, channels),
        hires, low_rim, high_rim, taps, spread, sums_conv, pw1_sums, ln1_bias, patches_all,
    )
    later = (1, 9, 5, 11, 2, 17, 4, 29, 28, 30, 3, 19, 15, 31)
    specs, buffers, run = with_loads(kernel, inputs, later)
    for index in (6, 7, 27, 36):
        specs[index] = pl.BlockSpec(memory_space=pl.ANY)
    return pl.pallas_call(
        run,
        out_shape=(
            out(rows, model, dtype=low), out(rows, model),
            out(*map_shape[1:]), out(*map_shape[1:]),
            out(map_rows, map_cols, channels),
            out(*tall_block), out(*tall_block), out(*few_block), out(*few_block),
        )
        + tuple(out(*shape[1:]) for shape in sources),
        in_specs=specs,
        out_specs=(VMEM_SPEC,) * n_out,
        scratch_shapes=scratch + buffers,
        compiler_params=kernel_params(3),
        name="last_block",
    )(*inputs)


def local(
    patches,
    hires,
    valid_rows,
    ln1_gain,
    ln1_bias,
    w_qkv,
    qv_bias,
    w_out,
    out_bias,
    ln2_gain,
    ln2_bias,
    w_fc1,
    fc1_bias,
    w_fc2,
    fc2_bias,
    dw_weight,
    dw_bias,
    lnc_gain,
    lnc_bias,
    w_pw1,
    pw1_bias,
    w_pw2,
    pw2_bias,
    layer_scale,
    w_adapt,
    adapt_bias,
    adapt_gain,
    grad_out,
):
    data_index = lax.axis_index("dp")
    image_index = data_index // IMG_SPAN
    map_cols, channels = hires.shape[1:]
    patch_rows, model = patches.shape
    half_rows = patch_rows * lax.axis_size("tensor")
    normed_low, conv_flat, low_rim, high_rim, grad_all, map_mean = conv_forward(
        hires, dw_weight, dw_bias, lnc_gain, lnc_bias, grad_out
    )
    conv_grad, branch_partial, half1, half2, pw1_sums, grad_pooled, patches_all, sums_conv = map_block(
        normed_low, w_pw1, pw1_bias, w_pw2, grad_all, w_adapt, adapt_gain, layer_scale,
        conv_flat, lnc_gain, patches, map_cols,
    )
    own_first = data_index % IMG_SPAN * half_rows
    other_first = (1 - data_index % IMG_SPAN) * half_rows
    key_place = jnp.concatenate(
        [own_first + jnp.arange(half_rows), other_first + jnp.arange(half_rows)]
    )
    image_valid = jnp.sum(jnp.where(jnp.arange(valid_rows.shape[0]) == image_index, valid_rows, 0))
    key_live = (key_place // SIDE < image_valid).astype(jnp.float32)[None]
    (
        joined_out, grad_patches, reduced_pw1, reduced_pw2, grad_hires,
        tall_ring, tall_data, few_ring, few_data,
        reduced_fc1, reduced_fc2, reduced_qkv, reduced_out, reduced_adapt,
    ) = last_block(
        patches, patches_all, grad_all, map_mean, grad_pooled, branch_partial, half1, half2,
        ln1_gain, w_qkv, qv_bias, w_out, out_bias, ln2_gain, ln2_bias,
        w_fc1, fc1_bias, w_fc2, fc2_bias, w_adapt, adapt_bias, adapt_gain, pw2_bias, layer_scale,
        key_live, grad_out, conv_grad, hires, low_rim, high_rim, dw_weight, sums_conv, pw1_sums,
        ln1_bias,
    )
    width = w_out.shape[0]
    sums = (tall_ring, tall_data, few_ring, few_data)
    results = (
        joined_out, grad_patches, grad_hires, reduced_pw1, reduced_pw2, reduced_fc1, reduced_fc2,
        reduced_qkv, reduced_out, reduced_adapt,
    )
    (
        grad_dw_weight,
        grad_lnc_gain, grad_lnc_bias, grad_dw_bias, grad_pw2_bias, grad_layer_scale,
        grad_ln1_gain, grad_ln1_bias, grad_out_bias, grad_ln2_gain, grad_ln2_bias, grad_fc2_bias,
        grad_adapt_bias, grad_adapt_gain,
        grad_pw1_bias, grad_fc1_bias, grad_qv_bias,
        joined_out, grad_patches, grad_hires, reduced_pw1, reduced_fc1, reduced_adapt,
        reduced_pw2, reduced_fc2, reduced_out, reduced_qkv,
    ) = small_outputs(sums, results, channels, model, w_fc1.shape[1], width)
    return (
        joined_out,
        grad_patches,
        grad_hires,
        grad_ln1_gain,
        grad_ln1_bias,
        reduced_qkv,
        grad_qv_bias,
        reduced_out,
        grad_out_bias,
        grad_ln2_gain,
        grad_ln2_bias,
        reduced_fc1,
        grad_fc1_bias,
        reduced_fc2,
        grad_fc2_bias,
        grad_dw_weight.T,
        grad_dw_bias,
        grad_lnc_gain,
        grad_lnc_bias,
        reduced_pw1,
        grad_pw1_bias,
        reduced_pw2.T,
        grad_pw2_bias,
        grad_layer_scale,
        reduced_adapt,
        grad_adapt_bias,
        grad_adapt_gain,
    )


def solution(mesh):
    return jax.shard_map(
        local,
        mesh=mesh,
        in_specs=(
            P(("dp", "tensor"), None),
            P(("dp", "tensor"), None, None),
            P(),
            P(),
            P(),
            P(None, None, "tensor"),
            P(None, "tensor"),
            P("tensor", None),
            P(),
            P(),
            P(),
            P(None, "tensor"),
            P("tensor"),
            P("tensor", None),
            P(),
            P(),
            P(),
            P(),
            P(),
            P(None, "tensor"),
            P("tensor"),
            P("tensor", None),
            P(),
            P(),
            P(),
            P(),
            P(),
            P(("dp", "tensor"), None),
        ),
        out_specs=(
            P(("dp", "tensor"), None),
            P(("dp", "tensor"), None),
            P(("dp", "tensor"), None, None),
            P(("dp", "tensor")),
            P(("dp", "tensor")),
            P(None, "dp", "tensor"),
            P(None, ("tensor", "dp")),
            P("tensor", "dp"),
            P(("dp", "tensor")),
            P(("dp", "tensor")),
            P(("dp", "tensor")),
            P("dp", "tensor"),
            P(("tensor", "dp")),
            P("tensor", "dp"),
            P(("dp", "tensor")),
            P(None, ("dp", "tensor")),
            P(("dp", "tensor")),
            P(("dp", "tensor")),
            P(("dp", "tensor")),
            P("dp", "tensor"),
            P(("tensor", "dp")),
            P("tensor", "dp"),
            P(("dp", "tensor")),
            P(("dp", "tensor")),
            P(("dp", "tensor"), None),
            P(("dp", "tensor")),
            P(("dp", "tensor")),
        ),
        check_vma=False,
    )
```

```python
from functools import partial

import jax
import jax.numpy as jnp
import numpy as np
from jax import lax
from jax.experimental import pallas as pl
from jax.experimental.pallas import tpu as pltpu
from jax.sharding import PartitionSpec as P

HEAD_DIM = 64
SIDE = 24
KERNEL = 7
IMG_SPAN = 2


vit_eps = 1e-05
map_eps = 1e-06
masked_score = -1e30
ROOT_HALF = 0.7071067811865476
NORMAL_PEAK = 0.3989422804014327


def contract_rows(left_side, right_side):
    return lax.dot_general(
        left_side, right_side, (((0,), (0,)), ((), ())), preferred_element_type=jnp.float32
    )


def contract_cols(left_side, right_side):
    return lax.dot_general(
        left_side, right_side, (((1,), (1,)), ((), ())), preferred_element_type=jnp.float32
    )


def bits_of(count):
    return count.bit_length() - 1


class Halving:
    def __init__(self, source, landings, send, recv, top_first):
        self.count = lax.axis_size("dp")
        self.d, self.t = lax.axis_index("dp"), lax.axis_index("tensor")
        self.source, self.landings = source, landings
        self.send, self.recv, self.top_first = send, recv, top_first
        self.stages = bits_of(self.count)
        self.at = 0
        self.staging = None

    def begin(self, stage=0):
        self.at = stage
        self.start(stage)

    def step(self, out=None):
        if self.at == self.stages:
            return
        self.finish(self.at, out if self.at == self.stages - 1 else None)
        self.at += 1
        if self.at < self.stages:
            self.start(self.at)

    def plan(self, stage):
        here = self.source if stage == 0 else self.landings[stage - 1]
        half = self.count >> (stage + 1)
        top = self.top_first and stage > 0
        bit = self.stages - stage if top else stage
        own = lax.rem(self.d // (1 << bit), 2)
        partner = self.d + (1 - 2 * own) * (1 << bit)
        base = self.count - 2 * half

        def place(i, value):
            return value * half + i if top else 2 * i + value

        def copy(i):
            return pltpu.make_async_remote_copy(
                here.at[place(i, 1 - own)], self.landings[stage].at[i],
                self.send.at[base + i], self.recv.at[base + i],
                device_id=(partner, self.t), device_id_type=MESH_ID,
            )

        return here, half, own, place, copy

    def start(self, stage):
        here, half, own, place, copy = self.plan(stage)

        def body(i, carry):
            copy(i).start()
            return carry

        lax.fori_loop(0, half, body, 0)

    def finish(self, stage, out=None):
        here, half, own, place, copy = self.plan(stage)
        landing = self.landings[stage]
        rows = landing.shape[1]

        def body(i, carry):
            copy(i).wait()
            kept = here.at[place(i, own)]
            if self.staging is not None and stage == 1:
                load = pltpu.make_async_copy(kept, *self.staging)
                load.start()
                load.wait()
                kept = self.staging[0]
            total = kept[...].astype(jnp.float32) + landing[i].astype(jnp.float32)
            if out is None:
                landing[i] = total.astype(jnp.bfloat16)
            else:
                out[...] = total
            return carry

        lax.fori_loop(0, half, body, 0)


def halving_scratch(count, rows, cols, half):
    landings = []
    while half >= 1:
        landings.append(pltpu.VMEM((half, rows, cols), jnp.bfloat16))
        half //= 2
    return landings + [pltpu.SemaphoreType.DMA((count - 1,))] * 2


class Ring:
    def __init__(self):
        self.count = lax.axis_size("tensor")
        self.d, self.t = lax.axis_index("dp"), lax.axis_index("tensor")

    def at(self, k):
        return lax.rem(self.t + k, self.count)

    def share_copy(self, buffer, sems, k, source):
        return pltpu.make_async_remote_copy(
            buffer.at[source], buffer.at[source], sems.at[0, k], sems.at[1, source],
            device_id=(self.d, self.at(k)), device_id_type=MESH_ID,
        )

    def share_start(self, buffer, sems):
        for k in range(1, self.count):
            self.share_copy(buffer, sems, k, self.t).start()

    def share_finish(self, buffer, sems):
        for k in range(1, self.count):
            self.share_copy(buffer, sems, k, self.t).wait_send()
        for k in range(1, self.count):
            self.share_copy(buffer, sems, k, self.at(k)).wait_recv()

    def give_copy(self, parts, landing, sems, k, slot, part):
        return pltpu.make_async_remote_copy(
            parts.at[part], landing.at[slot], sems.at[0, k], sems.at[1, slot],
            device_id=(self.d, self.at(k)), device_id_type=MESH_ID,
        )

    def give_start(self, parts, landing, sems):
        for k in range(1, self.count):
            self.give_copy(parts, landing, sems, k, self.t, self.at(k)).start()

    def give_finish(self, parts, landing, sems):
        for k in range(1, self.count):
            self.give_copy(parts, landing, sems, k, self.t, self.at(k)).wait_send()
        for k in range(1, self.count):
            self.give_copy(parts, landing, sems, k, self.at(k), self.at(k)).wait_recv()


    def halves(self):
        half = self.t // 2
        buddy = self.t + 1 - 2 * lax.rem(self.t, 2)
        at_middle = lax.rem(self.t + half, 2) == 1
        return buddy, 2 - 2 * half, 2 - half, at_middle

    def pass_copy(self, source, target, send, recv, device):
        return pltpu.make_async_remote_copy(
            source, target, send, recv, device_id=(self.d, device), device_id_type=MESH_ID
        )

    def spread_copy(self, buffer, sems, j, slot, device):
        return self.pass_copy(buffer.at[j], buffer.at[j], sems.at[0, slot], sems.at[1, j], device)

    def spread_start(self, buffer, sems):
        buddy, _, middle, _ = self.halves()
        self.spread_copy(buffer, sems, self.t, 0, middle).start()
        self.spread_copy(buffer, sems, self.t, 1, buddy).start()

    def spread_relay(self, buffer, sems):
        buddy, far, middle, at_middle = self.halves()

        @pl.when(at_middle)
        def _():
            for i, j in enumerate((middle, 2 * far + 1 - middle)):
                copy = self.spread_copy(buffer, sems, j, 2 + i, buddy)
                copy.wait_recv()
                copy.start()

    def spread_finish(self, buffer, sems):
        buddy, far, middle, at_middle = self.halves()
        self.spread_copy(buffer, sems, self.t, 0, middle).wait_send()
        self.spread_copy(buffer, sems, self.t, 1, buddy).wait_send()
        self.spread_copy(buffer, sems, buddy, 1, buddy).wait_recv()

        @pl.when(at_middle)
        def _():
            for i in range(2):
                self.spread_copy(buffer, sems, far + i, 2 + i, buddy).wait_send()

        @pl.when(jnp.logical_not(at_middle))
        def _():
            for i in range(2):
                self.spread_copy(buffer, sems, far + i, 2 + i, buddy).wait_recv()

    def sum_copies(self, parts, landing, sems):
        buddy, far, _, _ = self.halves()
        to_buddy = self.pass_copy(
            parts.at[buddy], landing.at[0], sems.at[0, 0], sems.at[1, 0], buddy
        )
        inward = [
            self.pass_copy(
                parts.at[far + i], landing.at[2 + i], sems.at[0, 1 + i], sems.at[1, 2 + i], buddy
            )
            for i in range(2)
        ]
        across = [
            self.pass_copy(
                parts.at[far + i], landing.at[1], sems.at[0, 1 + i], sems.at[1, 1], far + i
            )
            for i in range(2)
        ]
        return to_buddy, inward, across

    def sum_start(self, parts, landing, sems):
        to_buddy, inward, _ = self.sum_copies(parts, landing, sems)

        @pl.when(jnp.logical_not(self.halves()[3]))
        def _():
            for copy in inward:
                copy.start()

        to_buddy.start()

    def sum_relay(self, parts, landing, sems):
        _, far, _, at_middle = self.halves()
        _, inward, across = self.sum_copies(parts, landing, sems)

        @pl.when(at_middle)
        def _():
            for i in range(2):
                inward[i].wait_recv()
                parts[far + i] = (
                    parts[far + i].astype(jnp.float32) + landing[2 + i].astype(jnp.float32)
                ).astype(jnp.bfloat16)
                across[i].start()

    def sum_finish(self, parts, landing, sems):
        to_buddy, inward, across = self.sum_copies(parts, landing, sems)
        to_buddy.wait()
        at_middle = self.halves()[3]

        @pl.when(at_middle)
        def _():
            for copy in across:
                copy.wait_send()

        @pl.when(jnp.logical_not(at_middle))
        def _():
            for copy in inward:
                copy.wait_send()

        across[0].wait_recv()
        return (
            parts[self.t].astype(jnp.float32)
            + landing[0].astype(jnp.float32)
            + landing[1].astype(jnp.float32)
        )

    def total(self, parts, landing):
        value = parts[self.t].astype(jnp.float32)
        for k in range(1, self.count):
            value = value + landing[self.at(k)].astype(jnp.float32)
        return value


class SmallSum:
    def __init__(self, landed, shared, send, recv, sems):
        self.landed, self.shared = landed, shared
        self.send, self.recv, self.sems = send, recv, sems
        self.ring = Ring()
        self.count = lax.axis_size("dp")

    def copy(self, k, part, slot):
        ring = self.ring
        return pltpu.make_async_remote_copy(
            self.piece(part), self.landed.at[slot], self.send.at[k], self.recv.at[slot],
            device_id=(lax.rem(ring.d + k, self.count), ring.t), device_id_type=MESH_ID,
        )

    def start(self):
        def body(k, carry):
            self.copy(k, lax.rem(self.ring.d + k, self.count), self.ring.d).start()
            return carry

        lax.fori_loop(1, self.count, body, 0)

    def share(self, out):
        out[...] = self.piece(self.ring.d)[...]

        def body(k, carry):
            slot = lax.rem(self.ring.d + k, self.count)
            self.copy(k, slot, self.ring.d).wait_send()
            self.copy(k, slot, slot).wait_recv()
            out[...] += self.landed[slot]
            return carry

        lax.fori_loop(1, self.count, body, 0)
        self.shared[self.ring.t] = out[...]
        self.ring.share_start(self.shared, self.sems)

    def finish(self, out):
        self.ring.share_finish(self.shared, self.sems)
        total = self.shared[0]
        for j in range(1, self.ring.count):
            total = total + self.shared[j]
        out[...] = total


def small_sum_scratch(data, count, rows):
    block = (rows, 2 * LANES)
    return [
        pltpu.VMEM((data,) + block, jnp.float32),
        pltpu.VMEM((count,) + block, jnp.float32),
        pltpu.SemaphoreType.DMA((data,)), pltpu.SemaphoreType.DMA((data,)),
        pltpu.SemaphoreType.DMA((2, count)),
    ]


def norm_parts(values, epsilon):
    centered = values - jnp.mean(values, axis=-1, keepdims=True)
    variance = jnp.mean(centered * centered, axis=-1, keepdims=True)
    scale = lax.rsqrt(variance + epsilon)
    return centered * scale, scale


def norm_pull(grad, xhat, scale, gain):
    scaled = grad * gain
    return scale * (
        scaled
        - jnp.mean(scaled, axis=-1, keepdims=True)
        - xhat * jnp.mean(scaled * xhat, axis=-1, keepdims=True)
    )


def row_sum(values):
    return jnp.sum(values, axis=0, keepdims=True)


def flat_low(buffer):
    count, rows, cols = buffer.shape
    return buffer[...].astype(jnp.float32).reshape(count * rows, cols).astype(jnp.bfloat16)


def fill_rows(blocks, first, value):
    rows = blocks.shape[1]
    for c in range(value.shape[0] // rows):
        blocks[first // rows + c] = value[c * rows : (c + 1) * rows].astype(jnp.bfloat16)


def fill_parts(parts, value):
    count, rows, _ = parts.shape
    for j in range(count):
        parts[j] = value[j * rows : (j + 1) * rows].astype(jnp.bfloat16)


MESH_ID = pl.DeviceIdType.MESH
VMEM_SPEC = pl.BlockSpec(memory_space=pltpu.VMEM)
LANES = 128
SUB = 8
VMEM_BYTES = 125 * 512 * 1024


def kernel_params(collective_id=None):
    if collective_id is None:
        return pltpu.CompilerParams(vmem_limit_bytes=VMEM_BYTES)
    return pltpu.CompilerParams(
        vmem_limit_bytes=VMEM_BYTES, collective_id=collective_id, has_side_effects=True
    )


def halo_route():
    count = lax.axis_size("tensor")
    d, t = lax.axis_index("dp"), lax.axis_index("tensor")
    odd = lax.rem(d, IMG_SPAN)
    up = (d + (t + 1) // count, lax.rem(t + 1, count))
    down = (d - 1 + (t + count - 1) // count, lax.rem(t + count - 1, count))
    up_here = (t + 1) // count + odd < 2
    down_here = t + odd > 0
    return up, down, up_here, down_here


def seam_here():
    count = lax.axis_size("tensor")
    d, t = lax.axis_index("dp"), lax.axis_index("tensor")
    odd = lax.rem(d, IMG_SPAN)
    at_last = (t + 1) // count
    at_first = 1 - (t + count - 1) // count
    return at_last * (1 - odd) + at_first * odd


def meet(data_peers, across_seam=True):
    count = lax.axis_size("tensor")
    d, t = lax.axis_index("dp"), lax.axis_index("tensor")
    odd = lax.rem(d, IMG_SPAN)
    barrier = pltpu.get_barrier_semaphore()
    for k in range(1, count):
        pl.semaphore_signal(
            barrier, inc=1, device_id=(d, lax.rem(t + k, count)), device_id_type=MESH_ID
        )
    for peer in data_peers:
        pl.semaphore_signal(barrier, inc=1, device_id=(peer, t), device_id_type=MESH_ID)
    if not across_seam:
        pl.semaphore_wait(barrier, count - 1 + len(data_peers))
        return
    seam = seam_here()

    @pl.when(seam > 0)
    def _():
        pl.semaphore_signal(
            barrier, inc=1, device_id=(d + 1 - 2 * odd, count - 1 - t), device_id_type=MESH_ID
        )

    pl.semaphore_wait(barrier, count - 1 + len(data_peers) + seam)


def as_row(ref):
    return ref[...].reshape(1, ref.shape[0])


def halo_copies(route, first_rows, last_rows, low_ref, high_ref, send_sem, recv_sem):
    up, down, up_here, down_here = route
    to_up = pltpu.make_async_remote_copy(
        last_rows, low_ref, send_sem.at[0], recv_sem.at[0], device_id=up, device_id_type=MESH_ID
    )
    to_down = pltpu.make_async_remote_copy(
        first_rows, high_ref, send_sem.at[1], recv_sem.at[1], device_id=down, device_id_type=MESH_ID
    )
    return to_up, to_down


def halo_start(route, copies):
    @pl.when(route[2])
    def _():
        copies[0].start()

    @pl.when(route[3])
    def _():
        copies[1].start()


def halo_finish(route, copies):
    @pl.when(route[2])
    def _():
        copies[0].wait_send()
        copies[1].wait_recv()

    @pl.when(route[3])
    def _():
        copies[1].wait_send()
        copies[0].wait_recv()


def halo_store(route, extended, low_ref, high_ref, rows, cols, rim):
    @pl.when(route[3])
    def _():
        extended[0:rim, SUB : SUB + cols, :] = low_ref[...].astype(jnp.float32)

    @pl.when(route[2])
    def _():
        extended[rim + rows : 2 * rim + rows, SUB : SUB + cols, :] = high_ref[...].astype(
            jnp.float32
        )


def conv_rows(extended, taps_ref, rows, cols, blocks, flipped, emit):
    span = KERNEL * KERNEL - 1
    rim = KERNEL // 2
    tiles = cols // SUB
    inside = lax.broadcasted_iota(jnp.int32, (SUB, LANES), 0)

    def lane_block(block, carry):
        lanes = pl.ds(pl.multiple_of(block * LANES, LANES), LANES)
        for e in range(KERNEL):
            shift = e - rim
            taps = []
            for a in range(KERNEL):
                index = a * KERNEL + e
                taps.append(taps_ref[pl.ds(span - index if flipped else index, 1), lanes])
            first = 1 if shift >= 0 else 0
            last = tiles + 1 if shift <= 0 else tiles + 2
            before = [None] * rows
            for tile in range(first, last):
                cells = [
                    extended[r, SUB * tile : SUB * tile + SUB, lanes]
                    for r in range(rows + KERNEL - 1)
                ]
                for i in range(rows):
                    total = cells[i] * taps[0]
                    for a in range(1, KERNEL):
                        total = total + cells[i + a] * taps[a]
                    if shift == 0:
                        emit(e, i, tile - 1, lanes, total)
                        continue
                    turned = pltpu.roll(total, (SUB - shift) % SUB, 0)
                    if tile > first:
                        split = SUB - shift if shift > 0 else -shift
                        value = jnp.where(inside < split, before[i], turned)
                        emit(e, i, tile - 1 - first, lanes, value)
                    before[i] = turned
        return carry

    lax.fori_loop(blocks[0], blocks[1], lane_block, 0)


def tap_rows(grads, map_refs, tap_grad_ref, rows, cols, blocks):
    rim = KERNEL // 2
    low_ref, own_ref, high_ref = map_refs
    pairs = cols // (2 * SUB)
    inside = lax.broadcasted_iota(jnp.int32, (SUB, LANES), 0)

    def lane_block(block, carry):
        lanes = pl.ds(pl.multiple_of(block * LANES, LANES), LANES)
        for e in range(KERNEL):
            shift = e - rim
            sums = [None] * KERNEL
            for pair in range(pairs):
                here = slice(2 * SUB * pair, 2 * SUB * pair + 2 * SUB)
                cells = (
                    [low_ref[r, here, lanes] for r in range(rim)]
                    + [own_ref[r, here, lanes] for r in range(rows)]
                    + [high_ref[r, here, lanes] for r in range(rim)]
                )
                cells = [cell.astype(jnp.float32) for cell in cells]
                for i in range(rows):
                    first = SUB * (2 * pair + (0 if shift > 0 else 1))
                    count = 2 if shift == 0 else 3
                    given = [
                        grads[rim + i, first + SUB * k : first + SUB * k + SUB, lanes]
                        for k in range(count)
                    ]
                    if shift != 0:
                        turned = [pltpu.roll(tile, shift % SUB, 0) for tile in given]
                        split = shift if shift > 0 else SUB + shift
                        given = [
                            jnp.where(inside < split, turned[k], turned[k + 1]) for k in range(2)
                        ]
                    for a in range(KERNEL):
                        cell = cells[i + a]
                        term = cell[0:SUB] * given[0] + cell[SUB : 2 * SUB] * given[1]
                        sums[a] = term if sums[a] is None else sums[a] + term
            for a in range(KERNEL):
                tap_grad_ref[pl.ds(a * KERNEL + e, 1), lanes] = jnp.sum(
                    sums[a], axis=0, keepdims=True
                )
        return carry

    lax.fori_loop(blocks[0], blocks[1], lane_block, 0)


def conv_forward_kernel(
    own_ref, taps_ref, bias_1d, gain_1d, shift_1d, pool_ref, upstream_ref,
    normed_ref, conv_ref, low_ref, high_ref, given_ref, mean_ref,
    extended, vectors, given_all, send_sem, recv_sem, given_sems,
):
    rows, cols, channels = own_ref.shape
    rim = KERNEL // 2
    route = halo_route()
    ring = Ring()
    meet(())
    copies = halo_copies(
        route, own_ref.at[pl.ds(0, rim)], own_ref.at[pl.ds(rows - rim, rim)],
        low_ref, high_ref, send_sem, recv_sem,
    )
    halo_start(route, copies)
    given_all[ring.t] = upstream_ref[...]
    vectors[0:1, :] = as_row(bias_1d)
    vectors[1:2, :] = as_row(gain_1d)
    vectors[2:3, :] = as_row(shift_1d)
    bias_ref, gain_ref, shift_ref = vectors.at[0:1], vectors.at[1:2], vectors.at[2:3]
    quarter = pool_ref.shape[0]
    for pair in range(rows // 2):
        mean_ref[pair * quarter : (pair + 1) * quarter, :] = jnp.dot(
            pool_ref[...],
            own_ref[2 * pair : 2 * pair + 2].reshape(2 * cols, channels),
            preferred_element_type=jnp.float32,
        )
    for edge in (0, SUB + cols):
        extended[:, edge : edge + SUB, :] = jnp.zeros(
            (rows + 2 * rim, SUB, channels), jnp.float32
        )
    extended[rim : rim + rows, SUB : SUB + cols, :] = own_ref[...].astype(jnp.float32)
    halo_finish(route, copies)
    ring.share_start(given_all, given_sems)

    @pl.when(jnp.logical_not(route[3]))
    def _():
        low_ref[...] = jnp.zeros_like(low_ref)
        extended[0:rim, SUB : SUB + cols, :] = jnp.zeros((rim, cols, channels), jnp.float32)

    @pl.when(jnp.logical_not(route[2]))
    def _():
        high_ref[...] = jnp.zeros_like(high_ref)
        extended[rim + rows : 2 * rim + rows, SUB : SUB + cols, :] = jnp.zeros(
            (rim, cols, channels), jnp.float32
        )

    halo_store(route, extended, low_ref, high_ref, rows, cols, rim)

    def emit(e, i, tile, lanes, value):
        here = slice(i * cols + tile * SUB, i * cols + tile * SUB + SUB)
        if e == 0:
            conv_ref[here, lanes] = value + bias_ref[:, lanes]
        else:
            conv_ref[here, lanes] += value

    half_blocks = channels // LANES // 2
    conv_rows(extended, taps_ref, rows, cols, (0, half_blocks), False, emit)
    conv_rows(extended, taps_ref, rows, cols, (half_blocks, channels // LANES), False, emit)
    step = 2 * SUB

    def norm_block(block, carry):
        here = pl.ds(pl.multiple_of(block * step, step), step)
        values = conv_ref[here, :]
        centered = values - jnp.mean(values, axis=-1, keepdims=True)
        variance = jnp.mean(centered * centered, axis=-1, keepdims=True)
        scaled = centered * lax.rsqrt(variance + map_eps) * gain_ref[...] + shift_ref[...]
        normed_ref[here, :] = scaled.astype(jnp.bfloat16)
        return carry

    lax.fori_loop(0, rows * cols // step, norm_block, 0)
    ring.share_finish(given_all, given_sems)
    given_ref[...] = flat_low(given_all)


def pool_matrix(map_cols):
    chunk = 2 * map_cols
    cell_patch = (np.arange(chunk) % map_cols) // 2
    return np.arange(chunk // 4)[:, None] == cell_patch[None, :]


def conv_forward(hires, taps, bias, gain, shift, upstream):
    rows, cols, channels = hires.shape
    rim = KERNEL // 2
    cells = rows * cols
    count = lax.axis_size("tensor")
    patch_rows, model = upstream.shape
    pool = jnp.asarray(np.where(pool_matrix(cols), 0.25, 0.0), jnp.bfloat16)
    flat = jax.ShapeDtypeStruct((count * patch_rows, model), jnp.bfloat16)
    return pl.pallas_call(
        conv_forward_kernel,
        out_shape=(
            jax.ShapeDtypeStruct((cells, channels), jnp.bfloat16),
            jax.ShapeDtypeStruct((cells, channels), jnp.float32),
            jax.ShapeDtypeStruct((rim, cols, channels), jnp.bfloat16),
            jax.ShapeDtypeStruct((rim, cols, channels), jnp.bfloat16),
            flat,
            jax.ShapeDtypeStruct((patch_rows, channels), jnp.float32),
        ),
        in_specs=[VMEM_SPEC] * 7,
        out_specs=(VMEM_SPEC,) * 6,
        scratch_shapes=[
            pltpu.VMEM((rows + 2 * rim, cols + 2 * SUB, channels), jnp.float32),
            pltpu.VMEM((SUB, channels), jnp.float32),
            pltpu.VMEM((count, patch_rows, model), jnp.bfloat16),
            pltpu.SemaphoreType.DMA((2,)),
            pltpu.SemaphoreType.DMA((2,)),
            pltpu.SemaphoreType.DMA((2, count)),
        ],
        compiler_params=kernel_params(0),
        name="conv_forward",
    )(hires, taps, bias, gain, shift, pool, upstream)


def window_start(m, width, data):
    block, most = m * (width // data) // LANES, width // LANES - 2
    return (block - block // (most + 1) * (block - most)) * LANES


def lane_start(m, width, data):
    return m * (width // data) // LANES * LANES


JOB_ORDERS = (False, True, False, True, True)


WHOLE = 10


def small_kernel(shapes, tall_ring, tall_data, few_ring, few_data, *refs):
    outs = refs[WHOLE:]
    channels, model, units, width = shapes
    d, t = lax.axis_index("dp"), lax.axis_index("tensor")
    data, count = lax.axis_size("dp"), lax.axis_size("tensor")
    taps = KERNEL * KERNEL

    def turned(value, first):
        size = value.shape[1]
        return pltpu.roll(value, lax.rem(size - first, size), 1)

    here = channels // (data * count)
    start = jnp.minimum(d * (channels // data) // LANES, channels // LANES - 2) * LANES
    first = d * (channels // data) - start
    wide = turned(tall_ring[...], first + t * here)
    outs[0][...] = wide[:, 0:LANES].T[0:here, 0:taps]
    for i in range(5):
        outs[1 + i][...] = wide[taps + i, 0:here]
    step = model // data
    first = d * step - d * step // LANES * LANES + t * (step // count)
    narrow = turned(few_ring[0:SUB, 0:LANES], first)
    for i in range(8):
        outs[6 + i][...] = narrow[i, 0 : step // count]
    step = outs[14].shape[0]
    first = d * step - jnp.minimum(d * step // LANES, channels // LANES - 2) * LANES
    last_rows = tall_data.shape[0] - SUB
    outs[14][...] = turned(tall_data[last_rows:, :], first)[taps + 5 - last_rows, 0:step]
    step = units // data
    first = d * step - d * step // LANES * LANES
    outs[15][...] = turned(few_data[0:SUB, LANES : 2 * LANES], first)[0, 0:step]
    step = width // data
    first = d * step - d * step // LANES * LANES
    outs[16][...] = turned(few_data[SUB : 2 * SUB, 0:LANES], first)[0:2, 0:step]
    joined, patches, hires, pw1, pw2, fc1, fc2, qkv, out, adapt = refs[:WHOLE]
    whole = outs[17:]
    for source, target in zip((joined, patches, hires, pw1, fc1, adapt, pw2), whole[:7]):
        target[...] = source[...]
    for source, target in zip((fc2, out), whole[7:9]):
        target[...] = source[...].T
    for part in range(3):
        whole[9][part] = qkv[:, part * width : (part + 1) * width]


def small_outputs(sums, results, channels, model, units, width):
    data, count = lax.axis_size("dp"), lax.axis_size("tensor")
    taps = KERNEL * KERNEL
    shapes = (
        [(channels // (data * count), taps)]
        + [(channels // (data * count),)] * 5
        + [(model // (data * count),)] * 8
        + [(channels // data,), (units // data,), (2, width // data)]
    )
    joined, patches, hires, pw1, pw2, fc1, fc2, qkv, out, adapt = results
    more = [jax.ShapeDtypeStruct(r.shape, r.dtype) for r in results[:4] + (fc1, adapt, pw2)]
    more += [jax.ShapeDtypeStruct(r.shape[::-1], r.dtype) for r in (fc2, out)]
    more.append(jax.ShapeDtypeStruct((3, qkv.shape[0], width), qkv.dtype))
    return pl.pallas_call(
        partial(small_kernel, (channels, model, units, width)),
        out_shape=tuple(jax.ShapeDtypeStruct(shape, jnp.float32) for shape in shapes) + tuple(more),
        in_specs=[VMEM_SPEC] * (len(sums) + WHOLE),
        out_specs=(VMEM_SPEC,) * (len(shapes) + WHOLE),
        compiler_params=kernel_params(),
        name="small_outputs",
    )(*sums, *results)


def with_loads(kernel, inputs, later):
    specs = [VMEM_SPEC] * len(inputs)
    for index in later:
        specs[index] = pl.BlockSpec(memory_space=pl.ANY)
    buffers = [pltpu.VMEM(inputs[index].shape, inputs[index].dtype) for index in later]
    buffers.append(pltpu.SemaphoreType.DMA((len(later),)))

    def run(*refs):
        refs, own = list(refs[: -len(buffers)]), refs[-len(buffers) :]
        copies = {}
        for place, index in enumerate(later):
            copies[index] = pltpu.make_async_copy(refs[index], own[place], own[-1].at[place])
            copies[index].start()
            refs[index] = own[place]
        kernel(lambda index: copies[index].wait(), *refs)

    return specs, buffers, run


def mirror(index, low_half, last):
    return index + (1 - low_half) * (last - 2 * index)


def map_kernel(
    need, own_ref, w1_ref, b1_1d, w2_ref, given_ref, wadapt_ref, adapt_gain, layer_scale,
    pool_ref, spread_ref, conv_ref, gain_1d, attn_own,
    grad_ref, branch_ref, half1_ref, half2_ref, gb1_ref, pooled_grad_ref, attn_ref, sums_ref,
    gw1_ref, gw2_ref, patches_all, half_sems, attn_sems,
    b1_ref, branch_grad_ref, pooled_grads, rows_all, pre_grads, stash, from_below, from_above, pooled, hidden_grads,
    ag_recv, ag_up, ag_down, up_recv, up_send, down_recv, down_send,
):
    count, cells, channels = rows_all.shape
    hidden = w1_ref.shape[1]
    parts = ag_recv.shape[1]
    chunk = cells // parts
    quarter = chunk // 4
    last = count - 1
    d, t = lax.axis_index("dp"), lax.axis_index("tensor")
    low_half = 1 - t // 2
    place = mirror(t, low_half, last)
    above, below = (d, t + 1), (d, t - 1)
    ring = Ring()
    core = d + 1 - 2 * lax.rem(d, 2)
    meet([core], False)
    job1 = Halving(gw1_ref, [half1_ref], half_sems.at[0], half_sems.at[1], False)
    job2 = Halving(gw2_ref, [half2_ref], half_sems.at[2], half_sems.at[3], False)

    def rows_of(p):
        return pl.ds(pl.multiple_of(p * chunk, chunk), chunk)

    def gather_copy(j, p, target, send):
        return pltpu.make_async_remote_copy(
            rows_all.at[j, rows_of(p)], rows_all.at[j, rows_of(p)],
            send.at[j, p], ag_recv.at[j, p], device_id=target, device_id_type=MESH_ID,
        )

    def sum_copy(j, p, going_up):
        landing = from_below if going_up else from_above
        return pltpu.make_async_remote_copy(
            stash.at[j, rows_of(p)], landing.at[j, rows_of(p)],
            (up_send if going_up else down_send).at[j, p],
            (up_recv if going_up else down_recv).at[j, p],
            device_id=above if going_up else below, device_id_type=MESH_ID,
        )

    rows_all[t] = own_ref[...]
    for p in range(parts):
        @pl.when(t < last)
        def _():
            gather_copy(t, p, above, ag_up).start()

        @pl.when(t > 0)
        def _():
            gather_copy(t, p, below, ag_down).start()

    b1_ref[0:1, :] = as_row(b1_1d)
    adapt_grad = (given_ref[...].astype(jnp.float32) * as_row(adapt_gain)).astype(jnp.bfloat16)
    need(5)
    pooled_grad = contract_cols(adapt_grad, wadapt_ref[...])
    pooled_grads[...] = pooled_grad
    branch_grad_ref[...] = (as_row(layer_scale) * (pooled_grad * 0.25)).astype(jnp.bfloat16)
    own_rows = pooled_grad_ref.shape[0]
    pooled_grad_ref[...] = pooled_grads[pl.ds(pl.multiple_of(t * own_rows, SUB), own_rows), :]
    need(3)
    hidden_grads[...] = contract_cols(branch_grad_ref[...], w2_ref[...])
    gb1_ref[...] = jnp.zeros_like(gb1_ref)
    block = 256

    def pass_on(j, p, going_up):
        copy = sum_copy(j, p, going_up)
        copy.wait_recv()
        landing = from_below if going_up else from_above
        stash[j, rows_of(p), :] = (
            stash[j, rows_of(p), :].astype(jnp.float32)
            + landing[j, rows_of(p), :].astype(jnp.float32)
        ).astype(jnp.bfloat16)
        copy.start()

    middle = place == 1

    def forward_up(s, carry):
        j, p = t + 1 + s // parts, lax.rem(s, parts)
        pass_on(j, p, True)
        return carry

    def forward_down(s, carry):
        j, p = t - 1 - s // parts, lax.rem(s, parts)
        pass_on(j, p, False)
        return carry

    def forward(first, last_step, along):
        @pl.when(jnp.logical_and(middle, low_half == 1))
        def _():
            lax.fori_loop(first, last_step, forward_up if along else forward_down, 0)

        @pl.when(jnp.logical_and(middle, low_half == 0))
        def _():
            lax.fori_loop(first, last_step, forward_down if along else forward_up, 0)

    def order(n):
        return mirror(n + place * (1 - 2 * n) * (1 - n // 2), low_half, last)

    def receive(j, p):
        gather_copy(j, p, above, ag_up).wait_recv()

        @pl.when(jnp.logical_and(j < t, t < last))
        def _():
            gather_copy(j, p, above, ag_up).start()

        @pl.when(jnp.logical_and(j > t, t > 0))
        def _():
            gather_copy(j, p, below, ag_down).start()

    def receive_all(j):
        for p in range(parts):
            receive(j, p)

    def send_sums(j, p):
        @pl.when(jnp.logical_and(j > t, t == 0))
        def _():
            sum_copy(j, p, True).start()

        @pl.when(jnp.logical_and(j < t, t == last))
        def _():
            sum_copy(j, p, False).start()

    def compute(j, here, small):
        rows = here.size
        few = rows // 4
        given = rows_all[j, here, :]
        for first in range(0, hidden, block):
            cols = slice(first, first + block)
            pre = (
                jnp.dot(given, w1_ref[:, cols], preferred_element_type=jnp.float32)
                + b1_ref[0:1, cols]
            )
            wide_grad = hidden_grads[small, cols]
            high = wide_grad.astype(jnp.bfloat16)
            rest = (wide_grad - high.astype(jnp.float32)).astype(jnp.bfloat16)
            spread = spread_ref[0:rows, 0:few]
            spread_grad = jnp.dot(
                spread, high, preferred_element_type=jnp.float32
            ) + jnp.dot(spread, rest, preferred_element_type=jnp.float32)
            below_curve = 0.5 + 0.5 * lax.erf(pre * ROOT_HALF)
            slope = below_curve + pre * jnp.exp(-0.5 * pre * pre) * NORMAL_PEAK
            active = (pre * below_curve).astype(jnp.bfloat16)
            pooled[small, cols] = jnp.dot(
                pool_ref[0:few, 0:rows], active, preferred_element_type=jnp.float32
            )
            pre_low = (spread_grad * slope).astype(jnp.bfloat16)
            gb1_ref[:, cols] += jnp.sum(pre_low.astype(jnp.float32), axis=0, keepdims=True)
            pre_grads[j, here, cols] = pre_low
        return contract_cols(pre_grads[j, here, :], w1_ref[...])

    def whole_shard(n, carry):
        j = order(n)

        @pl.when(jnp.logical_and(place == 1, n == 1))
        def _():
            receive_all(order(1))
            receive_all(order(2))

        @pl.when(jnp.logical_and(place == 1, n == last))
        def _():
            receive_all(order(last))
            forward(0, 1, True)

        few = cells // 4
        partial_grad = compute(
            j, pl.ds(0, cells), pl.ds(pl.multiple_of(j * few, SUB), few)
        )

        @pl.when(n == 0)
        def _():
            grad_ref[...] = partial_grad

        @pl.when(n > 0)
        def _():
            stash[j] = partial_grad.astype(jnp.bfloat16)

        return carry

    def one_chunk(q, carry):
        j, p = order(1 + q // parts), lax.rem(q, parts)
        receive(j, p)
        small = pl.ds(pl.multiple_of((j * parts + p) * quarter, SUB), quarter)
        stash[j, rows_of(p), :] = compute(j, rows_of(p), small).astype(jnp.bfloat16)
        send_sums(j, p)
        return carry

    patches_all[t] = attn_own[...]
    need(1)
    lax.fori_loop(0, 1 + last * place, whole_shard, 0)
    lax.fori_loop(0, last * parts * (1 - place), one_chunk, 0)
    ring.spread_start(patches_all, attn_sems)

    wide = 384
    rows_flat = rows_all.reshape(count * cells, channels)
    pre_flat = pre_grads.reshape(count * cells, hidden)
    steps = []
    for p in range(1, 2 * parts):
        steps.append((p, True))
        if p > parts:
            steps.append((p - parts - 1, False))
    steps += [(p, False) for p in range(parts - 1, parts)]
    starts = list(range(0, channels, wide))
    for index, (p, along) in enumerate(steps):
        forward(p, p + 1, along)
        if index < len(starts):
            first = starts[index]
            fill_rows(
                gw1_ref, first, contract_rows(rows_flat[:, first : first + wide], pre_flat[...])
            )
    job1.start(0)
    ring.spread_relay(patches_all, attn_sems)
    pooled_low = pooled[...].astype(jnp.bfloat16)
    for first in range(0, channels, wide):
        fill_rows(
            gw2_ref, first,
            4.0 * contract_rows(branch_grad_ref[:, first : first + wide], pooled_low),
        )
    job2.start(0)
    branch_ref[...] = jnp.dot(
        pooled_low, w2_ref[...], preferred_element_type=jnp.float32
    ).astype(jnp.bfloat16)

    def finish(p, carry):
        @pl.when(t > 0)
        def _():
            sum_copy(t, p, True).wait_recv()
            grad_ref[rows_of(p), :] += from_below[t, rows_of(p), :].astype(jnp.float32)

        @pl.when(t < last)
        def _():
            sum_copy(t, p, False).wait_recv()
            grad_ref[rows_of(p), :] += from_above[t, rows_of(p), :].astype(jnp.float32)

        return carry

    lax.fori_loop(0, parts, finish, 0)
    need(10)
    sums_ref[...] = jnp.zeros_like(sums_ref)
    gain = as_row(gain_1d)
    step = 2 * SUB

    def grad_block(block, carry):
        here = pl.ds(pl.multiple_of(block * step, step), step)
        dy = grad_ref[here, :]
        xhat, rs = norm_parts(conv_ref[here, :], map_eps)
        grad = norm_pull(dy, xhat, rs, gain)
        grad_ref[here, :] = grad
        sums_ref[0:1, :] += row_sum(dy * xhat)
        sums_ref[1:2, :] += row_sum(dy)
        sums_ref[2:3, :] += row_sum(grad)
        return carry

    lax.fori_loop(0, cells // step, grad_block, 0)
    ring.spread_finish(patches_all, attn_sems)
    attn_ref[...] = flat_low(patches_all)
    job1.finish(0)
    job2.finish(0)

    def drain(q, carry):
        j, p = q // parts, lax.rem(q, parts)

        @pl.when(jnp.logical_and(j <= t, t < last))
        def _():
            gather_copy(j, p, above, ag_up).wait_send()

        @pl.when(jnp.logical_and(j >= t, t > 0))
        def _():
            gather_copy(j, p, below, ag_down).wait_send()

        @pl.when(j > t)
        def _():
            sum_copy(j, p, True).wait_send()

        @pl.when(j < t)
        def _():
            sum_copy(j, p, False).wait_send()

        return carry

    lax.fori_loop(0, count * parts, drain, 0)


def map_block(
    normed_low, w_pw1, pw1_bias, w_pw2, grad_all, w_adapt, adapt_gain, layer_scale,
    conv, gain, attn_own, map_cols,
):
    cells, channels = normed_low.shape
    hidden = w_pw1.shape[1]
    count, data = lax.axis_size("tensor"), lax.axis_size("dp")
    chunk = 2 * map_cols
    parts = cells // chunk
    patches, model = grad_all.shape
    match = np.kron(np.eye(parts), pool_matrix(map_cols)) > 0.5
    pool = jnp.asarray(np.where(match, 0.25, 0.0), jnp.bfloat16)
    spread = jnp.asarray(match.T, jnp.bfloat16)
    low_all = pltpu.VMEM((count, cells, channels), jnp.bfloat16)
    sems = pltpu.SemaphoreType.DMA((count, parts))
    weight = pltpu.VMEM((data, channels // data, hidden), jnp.bfloat16)
    half = jax.ShapeDtypeStruct((data // 2, channels // data, hidden), jnp.bfloat16)
    inputs = (
        normed_low, w_pw1, pw1_bias, w_pw2, grad_all, w_adapt, adapt_gain, layer_scale,
        pool, spread, conv, gain, attn_own,
    )
    later = (5, 3, 1, 10)
    specs, buffers, run = with_loads(map_kernel, inputs, later)
    return pl.pallas_call(
        run,
        out_shape=(
            jax.ShapeDtypeStruct((cells, channels), jnp.float32),
            jax.ShapeDtypeStruct((patches, channels), jnp.bfloat16),
            half,
            half,
            jax.ShapeDtypeStruct((1, hidden), jnp.float32),
            jax.ShapeDtypeStruct((patches // count, channels), jnp.float32),
            jax.ShapeDtypeStruct((patches, model), jnp.bfloat16),
            jax.ShapeDtypeStruct((SUB, channels), jnp.float32),
        ),
        in_specs=specs,
        out_specs=(VMEM_SPEC,) * 8,
        scratch_shapes=[
            weight,
            weight,
            pltpu.VMEM((count, patches // count, model), jnp.bfloat16),
            pltpu.SemaphoreType.DMA((4, data - 1)),
            pltpu.SemaphoreType.DMA((2, count)),
            pltpu.VMEM((SUB, hidden), jnp.float32),
            pltpu.VMEM((patches, channels), jnp.bfloat16),
            pltpu.VMEM((patches, channels), jnp.float32),
            low_all,
            pltpu.VMEM((count, cells, hidden), jnp.bfloat16),
            low_all,
            low_all,
            low_all,
            pltpu.VMEM((patches, hidden), jnp.float32),
            pltpu.VMEM((patches, hidden), jnp.float32),
        ]
        + [sems] * 7
        + buffers,
        compiler_params=kernel_params(2),
        name="map_block",
    )(*inputs)


def last_kernel(
    need, patches_ref, attn_ref, given_ref, map_mean_ref, grad_pooled_ref, branch_parts, half1_ref, half2_ref,
    ln1_gain, wqkv_ref, qv_bias, wout_ref, out_bias, ln2_gain, ln2_bias,
    wfc1_ref, fc1_bias, wfc2_ref, fc2_bias, wadapt_ref, adapt_bias, adapt_gain,
    pw2_bias, layer_scale, valid_ref, pick_ref, upstream_keep, conv_grad_ref,
    own_map, low_map, high_map, taps_ref, spread_ref, sums_conv, pw1_sums, ln1_bias, patches_all,
    joined_ref, grad_patches_ref, red1_ref, red2_ref, hires_grad_ref, tall_ring, tall_data, few_ring, few_data,
    job_outs,
    keys_all, values_all, kv_own, kv_other, queries, hidden_grad, probs, attended, middle_keep,
    hidden, pre_grad, dkv_other, mlp_flat, bias_row,
    parts, landing, out_parts, out_land, shared, branch_land, pool_parts, pool_land,
    sums_model, sums_map, sums_heads, sums_ff,
    grads, first_low, last_low, low_in, high_in, tap_grad_ref, tall_sum, few_sum, few_packed,
    halo_send, halo_recv, local_sem,
    proj_sems, mlp_sems, in_sems, out_sems, share_sems, attn_sems, branch_sems, pool_sems, pair_sems,
    staging, stage_sem, job_sources, job_scratch,
):
    dqkv, dkv_send, proj_flat = pre_grad, kv_own, mlp_flat
    ring = Ring()
    count, d, t = ring.count, ring.d, ring.t
    data = lax.axis_size("dp")
    stages = bits_of(data)
    rows, model = patches_ref.shape
    half_rows, width = queries.shape
    heads = width // HEAD_DIM
    scale = HEAD_DIM**-0.5
    partner = d + 1 - 2 * lax.rem(d, 2)
    map_rows, map_cols, channels = own_map.shape
    rim = KERNEL // 2
    lane_blocks = channels // LANES
    inner = slice(SUB, SUB + map_cols)

    meet([lax.rem(d + k, data) for k in range(1, data)])
    load = pltpu.make_async_copy(
        conv_grad_ref, grads.at[pl.ds(rim, map_rows), pl.ds(SUB, map_cols)], local_sem
    )
    load.start()
    map_jobs = []
    for half, scratch, top in zip((half1_ref, half2_ref), job_scratch[:2], (False, True)):
        landings = [half] + list(scratch[: stages - 1])
        job = Halving(None, landings, scratch[stages - 1], scratch[stages], top)
        job.staging = (staging, stage_sem)
        map_jobs.append(job)
    jobs = [
        Halving(source, scratch[:stages], scratch[stages], scratch[stages + 1], top)
        for source, scratch, top in zip(job_sources, job_scratch[2:], JOB_ORDERS)
    ]
    fc1_job, fc2_job, qkv_job, out_job, adapt_job = jobs
    gfc1, gfc2, gqkv, gout, gadapt = job_sources

    def step_map_jobs():
        for job, out in zip(map_jobs, (red1_ref, red2_ref)):
            job.step(out)

    def step_jobs(*which):
        for index in which:
            jobs[index].step(job_outs[index])

    for edge in (0, SUB + map_cols):
        grads[:, edge : edge + SUB, :] = jnp.zeros(
            (map_rows + 2 * rim, SUB, channels), jnp.float32
        )
    sums_model[...] = jnp.zeros_like(sums_model)
    sums_map[...] = jnp.zeros_like(sums_map)
    sums_heads[...] = jnp.zeros_like(sums_heads)
    sums_ff[...] = jnp.zeros_like(sums_ff)
    load.wait()
    route = halo_route()
    first_low[...] = grads[rim : 2 * rim, inner, :].astype(jnp.bfloat16)
    last_low[...] = grads[map_rows : map_rows + rim, inner, :].astype(jnp.bfloat16)
    halo = halo_copies(route, first_low, last_low, low_in, high_in, halo_send, halo_recv)
    halo_start(route, halo)
    for job in map_jobs:
        job.begin(1)

    need(1)
    band = 6 * 2 * SUB
    for first in range(0, half_rows, band):
        here = slice(first, first + band)
        xhat, _ = norm_parts(attn_ref[here, :].astype(jnp.float32), vit_eps)
        attn_ref[here, :] = (xhat * as_row(ln1_gain) + as_row(ln1_bias)).astype(jnp.bfloat16)
    attn = attn_ref[...]
    need(9)
    own_keys = jnp.dot(attn, wqkv_ref[1], preferred_element_type=jnp.float32).astype(jnp.bfloat16)
    own_values = (
        jnp.dot(attn, wqkv_ref[2], preferred_element_type=jnp.float32) + qv_bias[1:2, :]
    ).astype(jnp.bfloat16)
    kv_own[:, 0:width] = own_keys
    kv_own[:, width : 2 * width] = own_values

    def pair_copy(source, target, slot):
        return pltpu.make_async_remote_copy(
            source, target, pair_sems.at[0, slot], pair_sems.at[1, slot],
            device_id=(partner, t), device_id_type=MESH_ID,
        )

    pair_copy(kv_own, kv_other, 0).start()
    need(5)
    ring.sum_start(branch_parts, branch_land, branch_sems)
    queries[...] = (
        jnp.dot(attn, wqkv_ref[0], preferred_element_type=jnp.float32) + qv_bias[0:1, :]
    ).astype(jnp.bfloat16)
    keys_all[0:half_rows, :] = own_keys
    values_all[0:half_rows, :] = own_values
    pair_copy(kv_own, kv_other, 0).wait()
    keys_all[half_rows : 2 * half_rows, :] = kv_other[:, 0:width]
    values_all[half_rows : 2 * half_rows, :] = kv_other[:, width : 2 * width]
    column = lax.broadcasted_iota(jnp.int32, (1, 2 * half_rows), 1)
    turn = lax.rem(d, IMG_SPAN) * half_rows
    key_place = jnp.where(column < half_rows, column + turn, column - turn)
    live = key_place < valid_ref[d // IMG_SPAN] * SIDE
    for h in range(heads):
        here = slice(h * HEAD_DIM, (h + 1) * HEAD_DIM)
        raw = contract_cols(queries[:, here], keys_all[:, here]) * scale
        scores = jnp.where(live, raw, masked_score)
        grown = jnp.exp(scores - jnp.max(scores, axis=-1, keepdims=True))
        prob = grown * (1.0 / jnp.sum(grown, axis=-1, keepdims=True))
        probs[h] = prob
        attended[:, here] = jnp.dot(
            prob.astype(jnp.bfloat16), values_all[:, here], preferred_element_type=jnp.float32
        ).astype(jnp.bfloat16)
    need(11)
    fill_parts(parts, jnp.dot(attended[...], wout_ref[...], preferred_element_type=jnp.float32))
    ring.give_start(parts, landing, proj_sems)

    need(2)
    need(17)
    need(4)
    need(29)
    need(28)
    need(30)
    hidden_grad[...] = contract_cols(given_ref[...], wfc2_ref[...])
    for pair in range(map_rows // 2):
        half = map_cols // 2
        spread = jnp.dot(
            spread_ref[...],
            grad_pooled_ref[pair * half : (pair + 1) * half, :],
            precision=lax.Precision.HIGHEST,
            preferred_element_type=jnp.float32,
        )
        for i in range(2):
            hires_grad_ref[2 * pair + i] = spread
    map_refs = (low_map, own_map, high_map)
    tap_rows(grads, map_refs, tap_grad_ref, map_rows, map_cols, (0, lane_blocks // 2))
    ring.sum_relay(branch_parts, branch_land, branch_sems)
    ring.give_finish(parts, landing, proj_sems)
    inputs = patches_ref[...].astype(jnp.float32)
    middle = inputs + (ring.total(parts, landing) + as_row(out_bias))
    middle_keep[...] = middle
    xhat, _ = norm_parts(middle, vit_eps)
    shared[t] = (xhat * as_row(ln2_gain) + as_row(ln2_bias)).astype(jnp.bfloat16)
    ring.spread_start(shared, mlp_sems)

    branch = ring.sum_finish(branch_parts, branch_land, branch_sems) + as_row(pw2_bias)
    need(3)
    pooled = (map_mean_ref[...] + as_row(layer_scale) * branch).astype(jnp.bfloat16)
    pooled_grad = grad_pooled_ref[...]
    sums_map[0:1, :] = 4.0 * row_sum(
        (as_row(layer_scale) * (pooled_grad * 0.25)).astype(jnp.bfloat16).astype(jnp.float32)
    )
    sums_map[1:2, :] = row_sum(pooled_grad * branch)
    per_peer = channels // count
    place = lax.broadcasted_iota(jnp.int32, (channels, per_peer), 0)
    for j in range(count):
        choose = jnp.where(place == pick_ref[j : j + 1, :], 1.0, 0.0).astype(jnp.bfloat16)
        pool_parts[j] = jnp.dot(pooled, choose, preferred_element_type=jnp.float32).astype(
            jnp.bfloat16
        )
    ring.give_start(pool_parts, pool_land, pool_sems)
    need(19)
    adapted = (
        jnp.dot(pooled, wadapt_ref[...], preferred_element_type=jnp.float32) + as_row(adapt_bias)
    )
    upstream = upstream_keep[...].astype(jnp.float32)
    sums_model[5:6, :] = row_sum(upstream)
    sums_model[6:7, :] = row_sum(
        (upstream * as_row(adapt_gain)).astype(jnp.bfloat16).astype(jnp.float32)
    )
    sums_model[7:8, :] = row_sum(upstream * adapted)
    adapted_part = as_row(adapt_gain) * adapted
    ring.spread_relay(shared, mlp_sems)
    tap_rows(grads, map_refs, tap_grad_ref, map_rows, map_cols, (lane_blocks // 2, lane_blocks))
    taps = KERNEL * KERNEL
    tap_grad_ref[taps : taps + 3, :] = sums_conv[0:3, :]
    tap_grad_ref[taps + 3 : taps + 5, :] = sums_map[0:2, :]
    tap_grad_ref[taps + 5 : taps + 6, :] = pw1_sums[...]
    tap_grad_ref[taps + 6 : taps + 7, :] = jnp.zeros((1, channels), jnp.float32)
    tall_sum.piece = lambda m: tap_grad_ref.at[
        :, pl.ds(pl.multiple_of(window_start(m, channels, data), LANES), 2 * LANES)
    ]
    tall_sum.start()

    need(15)
    ring.spread_finish(shared, mlp_sems)
    mlp_flat[...] = flat_low(shared)
    units = wfc1_ref.shape[1]
    block = 256
    bias_row[0:1, :] = as_row(fc1_bias)

    def mlp_block(index, carry):
        cols = pl.ds(pl.multiple_of(index * block, block), block)
        pre = (
            jnp.dot(mlp_flat[...], wfc1_ref[:, cols], preferred_element_type=jnp.float32)
            + bias_row[0:1, cols]
        )
        below_curve = 0.5 + 0.5 * lax.erf(pre * ROOT_HALF)
        slope = below_curve + pre * jnp.exp(-0.5 * pre * pre) * NORMAL_PEAK
        hidden[:, cols] = (pre * below_curve).astype(jnp.bfloat16)
        pre_low = (hidden_grad[:, cols] * slope).astype(jnp.bfloat16)
        pre_grad[:, cols] = pre_low
        sums_ff[0:1, cols] = row_sum(pre_low.astype(jnp.float32))
        return carry

    lax.fori_loop(0, units // block, mlp_block, 0)
    fill_parts(parts, contract_cols(pre_grad[:, 0:units], wfc1_ref[...]))
    ring.give_start(parts, landing, in_sems)
    fill_parts(
        out_parts, jnp.dot(hidden[...], wfc2_ref[...], preferred_element_type=jnp.float32)
    )
    ring.sum_start(out_parts, out_land, out_sems)


    def gfc1_block(index, carry):
        first = pl.multiple_of(index * block, block)
        cols = pl.ds(first, block)
        fill_rows(gfc1, first, contract_rows(mlp_flat[:, cols], pre_grad[:, 0:units]))
        return carry

    lax.fori_loop(0, model // block, gfc1_block, 0)
    fc1_job.begin()

    def gfc2_block(index, carry):
        first = pl.multiple_of(index * block, block)
        cols = pl.ds(first, block)
        fill_rows(gfc2, first, contract_rows(given_ref[:, cols], hidden[...]))
        return carry

    lax.fori_loop(0, model // block, gfc2_block, 0)
    fc2_job.begin()
    halo_finish(route, halo)

    @pl.when(jnp.logical_not(route[3]))
    def _():
        grads[0:rim, inner, :] = jnp.zeros((rim, map_cols, channels), jnp.float32)

    @pl.when(jnp.logical_not(route[2]))
    def _():
        grads[rim + map_rows : 2 * rim + map_rows, inner, :] = jnp.zeros(
            (rim, map_cols, channels), jnp.float32
        )

    need(31)
    halo_store(route, grads, low_in, high_in, map_rows, map_cols, rim)

    def emit(e, i, tile, lanes, value):
        hires_grad_ref[i, tile * SUB : (tile + 1) * SUB, lanes] += value

    third = lane_blocks // 3
    conv_rows(grads, taps_ref, map_rows, map_cols, (0, third), True, emit)
    ring.give_finish(parts, landing, in_sems)
    mlp_in_grad = ring.total(parts, landing)
    middle = middle_keep[...]
    xhat, rs = norm_parts(middle, vit_eps)
    sums_model[3:4, :] = row_sum(mlp_in_grad * xhat)
    sums_model[4:5, :] = row_sum(mlp_in_grad)
    middle_grad = upstream + norm_pull(mlp_in_grad, xhat, rs, as_row(ln2_gain))
    grad_patches_ref[...] = middle_grad
    proj_low = middle_grad.astype(jnp.bfloat16)
    sums_model[2:3, :] = row_sum(proj_low.astype(jnp.float32))
    shared[t] = proj_low
    ring.spread_start(shared, share_sems)

    tall_sum.share(tall_data)
    step_map_jobs()
    step_jobs(0, 1)
    ring.spread_relay(shared, share_sems)
    ring.sum_relay(out_parts, out_land, out_sems)
    conv_rows(grads, taps_ref, map_rows, map_cols, (third, 2 * third), True, emit)
    ring.give_finish(pool_parts, pool_land, pool_sems)
    pool_land[t] = pool_parts[t]
    adapt_grad = (given_ref[...].astype(jnp.float32) * as_row(adapt_gain)).astype(jnp.bfloat16)
    fill_rows(gadapt, 0, contract_rows(flat_low(pool_land), adapt_grad))
    adapt_job.begin()
    vit_out = middle + (ring.sum_finish(out_parts, out_land, out_sems) + as_row(fc2_bias))
    joined_ref[...] = (vit_out + adapted_part).astype(jnp.bfloat16)

    ring.spread_finish(shared, share_sems)
    proj_flat[...] = flat_low(shared)
    attended_grad = contract_cols(proj_flat[...], wout_ref[...]).astype(jnp.bfloat16)
    for h in range(heads):
        here = slice(h * HEAD_DIM, (h + 1) * HEAD_DIM)
        there = slice(width + h * HEAD_DIM, width + (h + 1) * HEAD_DIM)
        head_grad = attended_grad[:, here]
        prob = probs[h]
        value_part = contract_rows(prob.astype(jnp.bfloat16), head_grad)
        prob_grad = contract_cols(head_grad, values_all[:, here])
        dot_rows = jnp.sum(prob * prob_grad, axis=-1, keepdims=True)
        score_grad = (prob * (prob_grad - dot_rows)).astype(jnp.bfloat16)
        dqkv[:, here] = (
            jnp.dot(score_grad, keys_all[:, here], preferred_element_type=jnp.float32) * scale
        ).astype(jnp.bfloat16)
        key_part = contract_rows(score_grad, queries[:, here]) * scale
        dkv_send[:, here] = key_part[half_rows:].astype(jnp.bfloat16)
        dkv_send[:, there] = value_part[half_rows:].astype(jnp.bfloat16)
        hidden_grad[:, here] = key_part[:half_rows]
        hidden_grad[:, there] = value_part[:half_rows]
    pair_copy(dkv_send, dkv_other, 1).start()

    def gout_block(index, carry):
        first = pl.multiple_of(index * block, block)
        cols = pl.ds(first, block)
        fill_rows(gout, first, contract_rows(proj_flat[:, cols], attended[...]))
        return carry

    lax.fori_loop(0, model // block, gout_block, 0)
    out_job.begin()
    again = pltpu.make_async_copy(patches_all, proj_flat, local_sem)
    again.start()
    pair_copy(dkv_send, dkv_other, 1).wait()
    kv_grad = (hidden_grad[:, 0 : 2 * width] + dkv_other[...].astype(jnp.float32)).astype(
        jnp.bfloat16
    )
    dqkv[:, width : 3 * width] = kv_grad
    attn_grad = contract_cols(dqkv[:, 0:width], wqkv_ref[0])
    for part in (1, 2):
        attn_grad += contract_cols(dqkv[:, part * width : (part + 1) * width], wqkv_ref[part])
    fill_parts(parts, attn_grad)
    ring.give_start(parts, landing, attn_sems)
    again.wait()
    for first in range(0, half_rows, band):
        rows_grad = attn_grad[first : first + band]
        xhat, _ = norm_parts(proj_flat[first : first + band, :].astype(jnp.float32), vit_eps)
        sums_model[0:1, :] += row_sum(rows_grad * xhat)
        sums_model[1:2, :] += row_sum(rows_grad)

    sums_heads[0:1, :] = row_sum(dqkv[:, 0:width].astype(jnp.float32))
    sums_heads[1:2, :] = row_sum(dqkv[:, 2 * width : 3 * width].astype(jnp.float32))
    zero = jnp.zeros((SUB, LANES), jnp.float32)
    for m in range(data):
        for lane, (row, source) in enumerate(((0, sums_model), (0, sums_ff), (SUB, sums_heads))):
            first = lane_start(m, source.shape[1], data)
            side = LANES * (lane % 2)
            few_packed[m, row : row + SUB, side : side + LANES] = source[
                :, first : first + LANES
            ]
        few_packed[m, SUB : 2 * SUB, LANES : 2 * LANES] = zero
    few_sum.piece = lambda m: few_packed.at[m]
    few_sum.start()

    def gqkv_block(index, carry):
        first = pl.multiple_of(index * block, block)
        cols = pl.ds(first, block)
        fill_rows(gqkv, first, contract_rows(attn_ref[:, cols], dqkv[:, 0 : 3 * width]))
        return carry

    lax.fori_loop(0, model // block, gqkv_block, 0)
    qkv_job.begin()
    step_jobs(0, 1, 4, 3, 2)
    few_sum.share(few_data)
    conv_rows(grads, taps_ref, map_rows, map_cols, (2 * third, lane_blocks), True, emit)
    ring.give_finish(parts, landing, attn_sems)
    attn_in_grad = ring.total(parts, landing)
    xhat, rs = norm_parts(inputs, vit_eps)
    grad_patches_ref[...] += norm_pull(attn_in_grad, xhat, rs, as_row(ln1_gain))
    step_map_jobs()
    step_jobs(0, 1, 4, 3, 2)
    for _ in range(stages):
        step_map_jobs()
        step_jobs(0, 1, 4, 3, 2)
    tall_sum.finish(tall_ring)
    few_sum.finish(few_ring)


def last_block(
    patches, patches_all, grad_all, map_mean, grad_pooled, branch_partial, half1, half2,
    ln1_gain, w_qkv, qv_bias, w_out, out_bias, ln2_gain, ln2_bias,
    w_fc1, fc1_bias, w_fc2, fc2_bias, w_adapt, adapt_bias, adapt_gain, pw2_bias, layer_scale,
    valid_rows, grad_own, conv_grad, hires, low_rim, high_rim, taps, sums_conv, pw1_sums, ln1_bias,
):
    count = lax.axis_size("tensor")
    data = lax.axis_size("dp")
    stages = bits_of(data)
    rows, model = patches.shape
    half_rows = rows * count
    width = w_out.shape[0]
    heads = width // HEAD_DIM
    units = w_fc1.shape[1]
    map_rows, map_cols, channels = hires.shape
    rim = KERNEL // 2
    stage_rows = channels // (data * count)
    place = np.arange(channels // count)
    pick = np.stack(
        [(place // stage_rows * count + j) * stage_rows + place % stage_rows for j in range(count)]
    ).astype(np.int32)
    near = np.arange(map_cols)[:, None] // 2 == np.arange(map_cols // 2)[None, :]
    spread = jnp.asarray(np.where(near, 0.25, 0.0), jnp.float32)
    f32, low = jnp.float32, jnp.bfloat16

    def vmem(*shape, dtype=low):
        return pltpu.VMEM(shape, dtype)

    shard = vmem(count, rows, model)
    rim_low = vmem(rim, map_cols, channels)
    tall = (KERNEL * KERNEL + SUB - 1) // SUB * SUB
    tall_block, few_block = (tall, 2 * LANES), (2 * SUB, 2 * LANES)
    dma = pltpu.SemaphoreType.DMA
    scratch = [
        vmem(2 * half_rows, width), vmem(2 * half_rows, width),
        vmem(half_rows, 2 * width), vmem(half_rows, 2 * width), vmem(half_rows, width),
        vmem(half_rows, units, dtype=f32), vmem(heads, half_rows, 2 * half_rows, dtype=f32),
        vmem(half_rows, width), vmem(rows, model, dtype=f32),
        vmem(half_rows, units), vmem(half_rows, max(units, 3 * width)),
        vmem(half_rows, 2 * width), vmem(half_rows, model), vmem(SUB, units, dtype=f32),
        shard, shard, shard, shard, shard,
        vmem(count, rows, channels),
        vmem(count, rows, channels // count), vmem(count, rows, channels // count),
        vmem(SUB, model, dtype=f32), vmem(SUB, channels, dtype=f32),
        vmem(SUB, width, dtype=f32), vmem(SUB, units, dtype=f32),
        vmem(map_rows + 2 * rim, map_cols + 2 * SUB, channels, dtype=f32),
        rim_low, rim_low, rim_low, rim_low, vmem(tall, channels, dtype=f32),
        vmem(data, *few_block, dtype=f32),
        dma((2,)), dma((2,)), dma,
    ] + [dma((2, count))] * 9 + [vmem(*half1.shape[1:]), dma]
    fixed = len(scratch)
    sum_place = fixed - 15
    sources = [
        (data, model // data, units), (data, model // data, units),
        (data, model // data, 3 * width), (data, model // data, width),
        (data, channels // (count * data), model),
    ]
    n_jobs = len(sources)
    scratch += [vmem(*shape) for shape in sources]
    map_shape = half1.shape
    sizes = []
    for shape in [(data, map_shape[1], map_shape[2])] * 2 + sources:
        first = data // 4 if len(sizes) < 2 else data // 2
        more = halving_scratch(*shape, first)
        sizes.append(len(more))
        scratch += more
    n_in, n_out, few_outs = 37, 9 + n_jobs, 9
    sum_scratch = small_sum_scratch(data, count, tall) + small_sum_scratch(data, count, 2 * SUB)
    n_sum = len(sum_scratch)
    scratch += sum_scratch

    def kernel(need, *refs):
        ins, outs, rest = refs[:n_in], refs[n_in : n_in + n_out], refs[n_in + n_out :]
        rest, sum_refs = rest[:-n_sum], rest[-n_sum:]
        own, more = list(rest[:fixed]), list(rest[fixed + n_jobs :])
        own[sum_place:sum_place] = [
            SmallSum(*sum_refs[: n_sum // 2]), SmallSum(*sum_refs[n_sum // 2 :])
        ]
        job_scratch = []
        for size in sizes:
            job_scratch.append(more[:size])
            more = more[size:]
        last_kernel(
            need, *ins, *outs[:few_outs], outs[few_outs:], *own, rest[fixed : fixed + n_jobs], job_scratch
        )

    def out(*shape, dtype=f32):
        return jax.ShapeDtypeStruct(shape, dtype)

    inputs = (
        patches, patches_all, grad_all, map_mean, grad_pooled,
        branch_partial.reshape(count, rows, channels), half1, half2,
        ln1_gain, w_qkv, qv_bias, w_out, out_bias, ln2_gain, ln2_bias,
        w_fc1, fc1_bias, w_fc2, fc2_bias, w_adapt, adapt_bias, adapt_gain,
        pw2_bias, layer_scale, valid_rows, jnp.asarray(pick), grad_own,
        conv_grad.reshape(map_rows, map_cols, channels),
        hires, low_rim, high_rim, taps, spread, sums_conv, pw1_sums, ln1_bias, patches_all,
    )
    later = (1, 9, 5, 11, 2, 17, 4, 29, 28, 30, 3, 19, 15, 31)
    specs, buffers, run = with_loads(kernel, inputs, later)
    for index in (6, 7, 27, 36):
        specs[index] = pl.BlockSpec(memory_space=pl.ANY)
    specs[24] = pl.BlockSpec(memory_space=pltpu.SMEM)
    return pl.pallas_call(
        run,
        out_shape=(
            out(rows, model, dtype=low), out(rows, model),
            out(*map_shape[1:]), out(*map_shape[1:]),
            out(map_rows, map_cols, channels),
            out(*tall_block), out(*tall_block), out(*few_block), out(*few_block),
        )
        + tuple(out(*shape[1:]) for shape in sources),
        in_specs=specs,
        out_specs=(VMEM_SPEC,) * n_out,
        scratch_shapes=scratch + buffers,
        compiler_params=kernel_params(3),
        name="last_block",
    )(*inputs)


def local(
    patches,
    hires,
    valid_rows,
    ln1_gain,
    ln1_bias,
    w_qkv,
    qv_bias,
    w_out,
    out_bias,
    ln2_gain,
    ln2_bias,
    w_fc1,
    fc1_bias,
    w_fc2,
    fc2_bias,
    dw_weight,
    dw_bias,
    lnc_gain,
    lnc_bias,
    w_pw1,
    pw1_bias,
    w_pw2,
    pw2_bias,
    layer_scale,
    w_adapt,
    adapt_bias,
    adapt_gain,
    grad_out,
):
    map_cols, channels = hires.shape[1:]
    patch_rows, model = patches.shape
    normed_low, conv_flat, low_rim, high_rim, grad_all, map_mean = conv_forward(
        hires, dw_weight, dw_bias, lnc_gain, lnc_bias, grad_out
    )
    conv_grad, branch_partial, half1, half2, pw1_sums, grad_pooled, patches_all, sums_conv = map_block(
        normed_low, w_pw1, pw1_bias, w_pw2, grad_all, w_adapt, adapt_gain, layer_scale,
        conv_flat, lnc_gain, patches, map_cols,
    )
    (
        joined_out, grad_patches, reduced_pw1, reduced_pw2, grad_hires,
        tall_ring, tall_data, few_ring, few_data,
        reduced_fc1, reduced_fc2, reduced_qkv, reduced_out, reduced_adapt,
    ) = last_block(
        patches, patches_all, grad_all, map_mean, grad_pooled, branch_partial, half1, half2,
        ln1_gain, w_qkv, qv_bias, w_out, out_bias, ln2_gain, ln2_bias,
        w_fc1, fc1_bias, w_fc2, fc2_bias, w_adapt, adapt_bias, adapt_gain, pw2_bias, layer_scale,
        valid_rows, grad_out, conv_grad, hires, low_rim, high_rim, dw_weight, sums_conv, pw1_sums,
        ln1_bias,
    )
    width = w_out.shape[0]
    sums = (tall_ring, tall_data, few_ring, few_data)
    results = (
        joined_out, grad_patches, grad_hires, reduced_pw1, reduced_pw2, reduced_fc1, reduced_fc2,
        reduced_qkv, reduced_out, reduced_adapt,
    )
    (
        grad_dw_weight,
        grad_lnc_gain, grad_lnc_bias, grad_dw_bias, grad_pw2_bias, grad_layer_scale,
        grad_ln1_gain, grad_ln1_bias, grad_out_bias, grad_ln2_gain, grad_ln2_bias, grad_fc2_bias,
        grad_adapt_bias, grad_adapt_gain,
        grad_pw1_bias, grad_fc1_bias, grad_qv_bias,
        joined_out, grad_patches, grad_hires, reduced_pw1, reduced_fc1, reduced_adapt,
        reduced_pw2, reduced_fc2, reduced_out, reduced_qkv,
    ) = small_outputs(sums, results, channels, model, w_fc1.shape[1], width)
    return (
        joined_out,
        grad_patches,
        grad_hires,
        grad_ln1_gain,
        grad_ln1_bias,
        reduced_qkv,
        grad_qv_bias,
        reduced_out,
        grad_out_bias,
        grad_ln2_gain,
        grad_ln2_bias,
        reduced_fc1,
        grad_fc1_bias,
        reduced_fc2,
        grad_fc2_bias,
        grad_dw_weight.T,
        grad_dw_bias,
        grad_lnc_gain,
        grad_lnc_bias,
        reduced_pw1,
        grad_pw1_bias,
        reduced_pw2.T,
        grad_pw2_bias,
        grad_layer_scale,
        reduced_adapt,
        grad_adapt_bias,
        grad_adapt_gain,
    )


def solution(mesh):
    return jax.shard_map(
        local,
        mesh=mesh,
        in_specs=(
            P(("dp", "tensor"), None),
            P(("dp", "tensor"), None, None),
            P(),
            P(),
            P(),
            P(None, None, "tensor"),
            P(None, "tensor"),
            P("tensor", None),
            P(),
            P(),
            P(),
            P(None, "tensor"),
            P("tensor"),
            P("tensor", None),
            P(),
            P(),
            P(),
            P(),
            P(),
            P(None, "tensor"),
            P("tensor"),
            P("tensor", None),
            P(),
            P(),
            P(),
            P(),
            P(),
            P(("dp", "tensor"), None),
        ),
        out_specs=(
            P(("dp", "tensor"), None),
            P(("dp", "tensor"), None),
            P(("dp", "tensor"), None, None),
            P(("dp", "tensor")),
            P(("dp", "tensor")),
            P(None, "dp", "tensor"),
            P(None, ("tensor", "dp")),
            P("tensor", "dp"),
            P(("dp", "tensor")),
            P(("dp", "tensor")),
            P(("dp", "tensor")),
            P("dp", "tensor"),
            P(("tensor", "dp")),
            P("tensor", "dp"),
            P(("dp", "tensor")),
            P(None, ("dp", "tensor")),
            P(("dp", "tensor")),
            P(("dp", "tensor")),
            P(("dp", "tensor")),
            P("dp", "tensor"),
            P(("tensor", "dp")),
            P("tensor", "dp"),
            P(("dp", "tensor")),
            P(("dp", "tensor")),
            P(("dp", "tensor"), None),
            P(("dp", "tensor")),
            P(("dp", "tensor")),
        ),
        check_vma=False,
    )
```
